32 devices in a mesh: grp: 2 (over x), seq: 16 (over z, y, core).
Axes of the slice: x: 2, y: 2, z: 4, core: 2. Of those that a mesh axis runs over, the one named last changes fastest.
Arguments:
- queries: bfloat16 [6144, 4096], P(('grp', 'seq')), parts along dimension 0, may hold values from -6 to 6
- keys: bfloat16 [6144, 4096], P(('grp', 'seq')), parts along dimension 0, may hold values from -6 to 6
- values: bfloat16 [6144, 4096], P(('grp', 'seq')), parts along dimension 0, may hold values from -6 to 6
- latent_in: float32 [6144, 64], P(('grp', 'seq')), parts along dimension 0, may hold values from -6 to 6
- mod_table: float32 [16, 2, 4096], replicated, may hold values from -3 to 3
- step_size: float32 [16], replicated, may hold values from 0.25 to 1
- timestep: int32 [64], P('grp'), parts along dimension 0, may hold values from 0 to 15
- head_weight: float32 [4096, 64], replicated, may hold values from -0.09375 to 0.09375
- conv_in_weight: bfloat16 [27, 16, 384], replicated, may hold values from -0.3125 to 0.3125
- conv_in_bias: float32 [384], replicated, may hold values from -3 to 3
- norm_gain: float32 [384], replicated, may hold values from 0.1 to 1.9
- conv_weight: bfloat16 [27, 384, 384], replicated, may hold values from -0.0625 to 0.0625
- conv_bias: float32 [384], replicated, may hold values from -3 to 3
- patch_weight: bfloat16 [1536, 1024], replicated, may hold values from -0.15625 to 0.15625
- patch_gain: float32 [1024], replicated, may hold values from 0.1 to 1.9
- post_gain: float32 [1024], replicated, may hold values from 0.1 to 1.9
- proj_weight: float32 [1024, 768], replicated, may hold values from -0.1875 to 0.1875
- text_table: bfloat16 [24704, 768], P(None, 'seq'), may hold values from -6 to 6
- prompt_ids: int32 [154], P('grp'), parts along dimension 0, may hold values from 0 to 24703
- frame_order: int32 [64], P('grp'), parts along dimension 0, may hold values from 0 to 31, each once
Outputs:
- latent_next: float32 [6144, 64], P(('grp', 'seq')), parts along dimension 0
- decoded: bfloat16 [64, 16, 24, 384], P(('grp', 'seq')), parts along dimension 0
- image_embed: float32 [64, 768], P(('grp', 'seq')), parts along dimension 0
- scores: float32 [64], P(('grp', 'seq')), parts along dimension 0
The draws below stay inside these ranges and needn't reach their ends.
There are 2 independent parts, one for each index of `grp`. The reference program is written for one: setup_inputs(seed, part) draws one part's arguments, and reference() takes and returns one part's arrays. A program takes and returns all parts, laid end to end along the dimension named above; an argument that names none is the same for every part. Nothing has to cross between parts.
All inputs are finite; a program needn't handle non-finite values.
Results may differ from the reference program's by a relative error of at most 0.009.
Values may be sent and summed in bfloat16 or wider, within the bound.
No kernel may reach another device: no remote copies, remote signals or barrier semaphores. Data moves between devices by JAX's collectives and lax.ppermute only.
A program may use at most 128 MiB of HBM per device.

```python
import jax
import jax.numpy as jnp
from jax import lax

GRID_H = 8
GRID_W = 12
HEADS = 32
HD = 128
LAT_C = 16
CH = 384
VIT_W = 1024
TEXT_W = 768
VOCAB = 24704
PROMPT = 77
STEPS = 16
FRAMES = 32
TOKENS = 3072


def backdrop(key):
    canvas = jnp.clip(jax.random.normal(key, (TOKENS, HEADS * HD), jnp.float32), -6.0, 6.0)
    return canvas


def draw_queries(key, part):
    canvas = backdrop(jax.random.fold_in(key, 11))
    return canvas.astype(jnp.bfloat16)


def draw_keys(key, part):
    canvas = backdrop(jax.random.fold_in(key, 12))
    return canvas.astype(jnp.bfloat16)


def touch_ends(drawn, own_key, least, largest):
    longest = drawn.shape.index(max(drawn.shape))
    spots = []
    for shift in (0, 1):
        where = [jax.random.randint(jax.random.fold_in(own_key, axis), (), 0, length) for axis, length in enumerate(drawn.shape)]
        where[longest] = (where[longest] + shift) % drawn.shape[longest]
        spots.append(tuple(where))
    return drawn.at[spots[0]].set(least).at[spots[1]].set(largest)


def block_levels(key, shape, cuts, smallest, high):
    loudness = 1.0
    for axis_at, shards_of in cuts:
        draws = jax.random.uniform(jax.random.fold_in(jax.random.fold_in(key, 6), axis_at), (shards_of,), jnp.float32, smallest / len(cuts), high / len(cuts))
        loudness = loudness * jnp.repeat(jnp.exp(draws), shape[axis_at] // shards_of).reshape((-1,) + (1,) * (len(shape) - 1 - axis_at))
    return loudness


def scatter_about(own_key, dims, deviation, limit, shards=(), held_as=jnp.bfloat16):
    gain = block_levels(own_key, dims, shards, -0.22, 0.18) if shards else 1.0
    drawn = jax.random.normal(own_key, dims, jnp.float32) * deviation * gain
    return jnp.minimum(jnp.maximum(drawn, -limit), limit).astype(held_as)


def setup_inputs(seed: int = 0, part: int = 0) -> dict:
    key_list = jax.random.split(jax.random.key(seed), 21)
    own_keys = jax.random.split(jax.random.fold_in(key_list[20], part), 21)
    queries = draw_queries(jax.random.fold_in(jax.random.fold_in(key_list[20], part), 71), part)
    keys = draw_keys(jax.random.fold_in(jax.random.fold_in(key_list[20], part), 71), part)
    values = scatter_about(own_keys[2], (TOKENS, HEADS * HD), 1.0, 6.0, ((0, 16),))
    latent_in = scatter_about(own_keys[3], (TOKENS, 4 * LAT_C), 1.0, 6.0, ((0, 16),), jnp.float32)
    mod_table = scatter_about(key_list[4], (STEPS, 2, HEADS * HD), 0.5, 3.0, (), jnp.float32)
    step_size = jnp.clip(jax.random.uniform(key_list[5], (STEPS,), jnp.float32, 0.25, 1.0), 0.25, 1.0)
    timestep = touch_ends(jax.random.randint(own_keys[6], (FRAMES,), 0, STEPS), jax.random.fold_in(own_keys[6], 1), 0, STEPS - 1).astype(jnp.int32)
    head_weight = scatter_about(key_list[7], (HEADS * HD, 4 * LAT_C), (HEADS * HD) ** -0.5, 0.09375, (), jnp.float32)
    conv_in_weight = scatter_about(key_list[8], (27, LAT_C, CH), (27 * LAT_C) ** -0.5, 0.3125)
    conv_in_bias = scatter_about(key_list[9], (CH,), 0.5, 3.0, (), jnp.float32)
    norm_gain = jnp.clip(1.0 + 0.18 * jax.random.normal(key_list[10], (CH,), jnp.float32), 0.1, 1.9)
    conv_weight = scatter_about(key_list[11], (27, CH, CH), (27 * CH) ** -0.5, 0.0625)
    conv_bias = scatter_about(key_list[12], (CH,), 0.5, 3.0, (), jnp.float32)
    patch_weight = scatter_about(key_list[13], (4 * CH, VIT_W), (4 * CH) ** -0.5, 0.15625)
    patch_gain = jnp.clip(1.0 + 0.18 * jax.random.normal(key_list[14], (VIT_W,), jnp.float32), 0.1, 1.9)
    post_gain = jnp.clip(1.0 + 0.18 * jax.random.normal(key_list[15], (VIT_W,), jnp.float32), 0.1, 1.9)
    proj_weight = scatter_about(key_list[16], (VIT_W, TEXT_W), VIT_W ** -0.5, 0.1875, (), jnp.float32)
    text_table = scatter_about(key_list[17], (VOCAB, TEXT_W), 1.0, 6.0, ((1, 16),))
    prompt_ids = touch_ends(jax.random.randint(own_keys[18], (PROMPT,), 0, VOCAB), jax.random.fold_in(own_keys[18], 1), 0, VOCAB - 1).astype(jnp.int32)
    frame_order = jax.random.permutation(own_keys[19], FRAMES).astype(jnp.int32)
    return dict(queries=queries, keys=keys, values=values, latent_in=latent_in, mod_table=mod_table, step_size=step_size, timestep=timestep, head_weight=head_weight, conv_in_weight=conv_in_weight, conv_in_bias=conv_in_bias, norm_gain=norm_gain, conv_weight=conv_weight, conv_bias=conv_bias, patch_weight=patch_weight, patch_gain=patch_gain, post_gain=post_gain, proj_weight=proj_weight, text_table=text_table, prompt_ids=prompt_ids, frame_order=frame_order)


highest = lax.Precision.HIGHEST

def lookup(mod_table, step_size, timestep):
    onehot = (jnp.arange(mod_table.shape[0], dtype=jnp.int32)[None, :] == timestep[:, None]).astype(jnp.float32)
    modulation = jnp.dot(onehot, mod_table.reshape(mod_table.shape[0], -1), precision=highest)
    return (modulation[:, :HEADS * HD], modulation[:, HEADS * HD:], lax.optimization_barrier(jnp.sum(onehot * step_size[None, :], axis=1)))

def attend(queries, keys, values):
    length = queries.shape[0]
    block_rows = 512 if length % 512 == 0 else length

    def split_heads(matrix):
        return matrix.reshape(length, HEADS, HD).transpose(1, 0, 2)

    def one_head(triple):
        head_q, head_k, head_v = triple

        def one_block(rows_q):
            logits = jnp.dot(rows_q, head_k.T, preferred_element_type=jnp.float32) * HD ** (-0.5)
            row_peak = lax.optimization_barrier(jnp.max(logits, axis=-1, keepdims=True))
            exponent = jnp.exp(logits - row_peak)
            weights = (exponent / lax.optimization_barrier(jnp.sum(exponent, axis=-1, keepdims=True))).astype(jnp.bfloat16)
            return jnp.dot(weights, head_v, preferred_element_type=jnp.float32).astype(jnp.bfloat16)
        return lax.map(one_block, head_q.reshape(length // block_rows, block_rows, HD)).reshape(length, HD)
    heads_out = lax.map(one_head, (split_heads(queries), split_heads(keys), split_heads(values)))
    return heads_out.transpose(1, 0, 2).reshape(length, HEADS * HD)

def predict(attended, mod_shift, mod_scale, head_weight):
    frames_n = mod_shift.shape[0]
    attended_f = attended.astype(jnp.float32)
    meansq = lax.optimization_barrier(jnp.mean(attended_f * attended_f, axis=-1, keepdims=True))
    normed = (attended_f * lax.rsqrt(meansq + 1e-06)).reshape(frames_n, -1, attended.shape[1])
    normed = normed * (1.0 + mod_scale[:, None, :]) + mod_shift[:, None, :]
    return jnp.dot(normed.reshape(attended.shape[0], -1), head_weight, precision=highest)

def advance(latent_in, step_dt, prediction):
    frames_n = step_dt.shape[0]
    shaped = latent_in.reshape(frames_n, -1, latent_in.shape[1]) + step_dt[:, None, None] * prediction.reshape(frames_n, -1, latent_in.shape[1])
    return shaped.reshape(latent_in.shape)

def to_frames(latent):
    shaped = latent.reshape(-1, GRID_H, GRID_W, 2, 2, LAT_C).transpose(0, 1, 3, 2, 4, 5)
    return shaped.reshape(-1, 2 * GRID_H, 2 * GRID_W, LAT_C)

def causal_conv(padded, weight):
    frames_n = padded.shape[0] - 2
    rows_h = padded.shape[1]
    cols_w = padded.shape[2]
    spaced = jnp.pad(padded, ((0, 0), (1, 1), (1, 1), (0, 0)))
    summed = jnp.zeros((frames_n * rows_h * cols_w, weight.shape[2]), jnp.float32)
    for lag_t in range(3):
        for row_off in range(3):
            for col_off in range(3):
                window = spaced[lag_t:lag_t + frames_n, row_off:row_off + rows_h, col_off:col_off + cols_w]
                window = window.reshape(-1, spaced.shape[3])
                summed = summed + jnp.dot(window, weight[lag_t * 9 + row_off * 3 + col_off], preferred_element_type=jnp.float32)
    return summed.reshape(frames_n, rows_h, cols_w, weight.shape[2])

def activate(first_out, norm_gain):
    first_f = first_out.astype(jnp.float32)
    meansq = lax.optimization_barrier(jnp.mean(first_f * first_f, axis=-1, keepdims=True))
    return jax.nn.silu(first_f * lax.rsqrt(meansq + 1e-06) * norm_gain).astype(jnp.bfloat16)

def to_patches(decoded):
    shaped = decoded.reshape(-1, GRID_H, 2, GRID_W, 2, CH).transpose(0, 1, 3, 2, 4, 5)
    return shaped.reshape(-1, GRID_H * GRID_W, 4 * CH)

def embed(patches, patch_weight):
    flat_rows = patches.reshape(-1, patches.shape[2])
    product = jnp.dot(flat_rows, patch_weight, preferred_element_type=jnp.float32)
    return product.reshape(patches.shape[0], patches.shape[1], -1).astype(jnp.bfloat16)

def layer_norm(matrix, gain_vec):
    centered = matrix - lax.optimization_barrier(jnp.mean(matrix, axis=-1, keepdims=True))
    variance = lax.optimization_barrier(jnp.mean(centered * centered, axis=-1, keepdims=True))
    return centered * lax.rsqrt(variance + 1e-05) * gain_vec

def describe(embedded, patch_gain, post_gain, proj_weight):
    pooled = lax.optimization_barrier(jnp.mean(layer_norm(embedded.astype(jnp.float32), patch_gain), axis=-2))
    return jnp.dot(layer_norm(pooled, post_gain), proj_weight, precision=highest)

def rate(image_vec, text_vector):
    inner = lax.optimization_barrier(jnp.sum(image_vec * text_vector[None, :], axis=-1))
    image_rms = jnp.sqrt(lax.optimization_barrier(jnp.mean(image_vec * image_vec, axis=-1)) + 1e-06)
    text_rms = jnp.sqrt(jnp.mean(text_vector * text_vector) + 1e-06)
    return 100.0 * inner / (TEXT_W * image_rms * text_rms)

def reference(queries, keys, values, latent_in, mod_table, step_size, timestep, head_weight, conv_in_weight, conv_in_bias, norm_gain, conv_weight, conv_bias, patch_weight, patch_gain, post_gain, proj_weight, text_table, prompt_ids, frame_order):
    mod_shift, mod_scale, step_dt = lookup(mod_table, step_size, timestep)
    attended = attend(queries, keys, values)
    latent_next = advance(latent_in, step_dt, predict(attended, mod_shift, mod_scale, head_weight))
    frames = to_frames(latent_next).astype(jnp.bfloat16)
    zeros_lat = jnp.zeros((2,) + frames.shape[1:], jnp.bfloat16)
    first_out = (causal_conv(jnp.concatenate([zeros_lat, frames], axis=0), conv_in_weight) + conv_in_bias).astype(jnp.bfloat16)
    activated = activate(first_out, norm_gain)
    zeros_act = jnp.zeros((2,) + activated.shape[1:], jnp.bfloat16)
    branch = causal_conv(jnp.concatenate([zeros_act, activated], axis=0), conv_weight)
    decoded = (branch + conv_bias + first_out.astype(jnp.float32)).astype(jnp.bfloat16)
    image_vec = describe(embed(to_patches(decoded), patch_weight), patch_gain, post_gain, proj_weight)
    text_vector = lax.optimization_barrier(jnp.mean(jnp.take(text_table, prompt_ids, axis=0).astype(jnp.float32), axis=0))
    image_embed = jnp.take(image_vec, frame_order, axis=0)
    return (latent_next, decoded, image_embed, rate(image_embed, text_vector))
```

```python
import functools

import jax
import jax.numpy as jnp
import numpy as np
from jax import lax
from jax.experimental import pallas as pl
from jax.experimental.pallas import tpu as pltpu
from jax.sharding import PartitionSpec as P

GRID_H = 8
GRID_W = 12
PATCH = GRID_H * GRID_W
HD = 128
LAT = 64
LAT_C = 16
CH = 384
TEXT_W = 768
KEY_CHUNK = 512


highest = lax.Precision.HIGHEST
VM = pl.BlockSpec(memory_space=pltpu.VMEM)
SM = pl.BlockSpec(memory_space=pltpu.SMEM)
ANY = pl.BlockSpec(memory_space=pl.ANY)


def shifted(value, axis, steps):
    count = lax.axis_size(axis)
    initial, last = (max(0, -steps), min(count, count - steps))
    return lax.ppermute(value, axis, [(source, source + steps) for source in range(initial, last)])


def rotate(value, axis, steps):
    count = lax.axis_size(axis)
    return lax.ppermute(value, axis, [(i, (i + 2 * steps) % count) for i in range(count)])


def swap_core(value, axis):
    count = lax.axis_size(axis)
    return lax.ppermute(value, axis, [(i, i ^ 1) for i in range(count)])


def attend_kernel(blocks, sources, heads, frames, t_ref, sc_ref, w_ref, *refs):
    q_refs, refs = refs[:blocks], refs[blocks:]
    kv_refs, refs = refs[:sources], refs[sources:]
    o_refs, refs = refs[:blocks], refs[blocks:]
    k_s, v_s, s_a, s_b, m_a, m_b, sem = refs
    rows = q_refs[0].shape[0]
    keys = sources * rows
    scale = np.float32(HD**-0.5 * np.log2(np.e))
    for h in range(heads):
        for which, dst in ((0, k_s), (1, v_s)):
            for j in range(sources):
                pltpu.make_async_copy(
                    kv_refs[j].at[which, :, pl.ds(h * HD, HD)],
                    dst.at[h, pl.ds(j * rows, rows), :],
                    sem.at[h, which],
                ).start()
    for b in range(blocks):
        o_refs[b][...] = jnp.zeros(o_refs[b].shape, jnp.float32)

    def arrived(h, which):
        whole = (k_s, v_s)[which].at[h]
        pltpu.make_async_copy(whole, whole, sem.at[h, which]).wait()

    def logits(h, b, at, s_ref, peak):
        q = q_refs[b][:, pl.ds(pl.multiple_of(h * HD, HD), HD)]
        s = lax.dot_general(
            q,
            k_s[h, at : at + KEY_CHUNK, :],
            (((1,), (1,)), ((), ())),
            preferred_element_type=jnp.float32,
        )
        s_ref[:, at : at + KEY_CHUNK] = s
        folded = functools.reduce(
            jnp.maximum, [s[:, i : i + 128] for i in range(0, KEY_CHUNK, 128)]
        )
        return folded if peak is None else jnp.maximum(peak, folded)

    def keep_peak(peak, m_ref):
        m_ref[...] = jnp.broadcast_to(jnp.max(peak, axis=-1, keepdims=True) * scale, m_ref.shape)

    slots, peaks = (s_a, s_b), (m_a, m_b)
    chunks = range(0, keys, KEY_CHUNK)
    arrived(0, 0)
    peak = None
    for at in chunks:
        peak = logits(0, 0, at, s_a, peak)
    keep_peak(peak, m_a)

    def one_head(h, carry):
        arrived(h, 1)
        after = jnp.minimum(h + 1, heads - 1)

        @pl.when(h + 1 < heads)
        def _():
            arrived(after, 0)

        for b in range(blocks):
            now, later = slots[b % 2], slots[(b + 1) % 2]
            next_h, next_b = (h, b + 1) if b + 1 < blocks else (after, 0)
            top = peaks[b % 2][:, :1]
            peak, total = None, None
            acc = jnp.zeros((rows, HD), jnp.float32)
            for at in chunks:
                peak = logits(next_h, next_b, at, later, peak)
                e = jnp.exp2(now[:, at : at + KEY_CHUNK] * scale - top)
                folded = functools.reduce(
                    jnp.add, [e[:, i : i + 128] for i in range(0, KEY_CHUNK, 128)]
                )
                total = folded if total is None else total + folded
                acc = acc + jnp.dot(
                    e.astype(jnp.bfloat16),
                    v_s[h, at : at + KEY_CHUNK, :],
                    preferred_element_type=jnp.float32,
                )
            keep_peak(peak, peaks[(b + 1) % 2])
            o = acc / jnp.sum(total, axis=-1, keepdims=True)
            o = o.astype(jnp.bfloat16).astype(jnp.float32)
            square = jnp.sum(o * o, axis=-1, keepdims=True)
            per = rows // frames
            scaled = jnp.concatenate(
                [
                    o[f * per : (f + 1) * per] * (1.0 + sc_ref[t_ref[b * frames + f], h])
                    for f in range(frames)
                ],
                axis=0,
            )
            part = jnp.dot(
                scaled, w_ref[h], precision=highest, preferred_element_type=jnp.float32
            )
            lane = lax.broadcasted_iota(jnp.int32, part.shape, 1)
            o_refs[b][...] = o_refs[b][...] + part + jnp.where(lane >= LAT, square, 0.0)
        return carry

    lax.fori_loop(0, heads, one_head, 0)


def attend(qs, kvs, steps, scale, weight):
    blocks, sources = len(qs), len(kvs)
    rows, cols = qs[0].shape
    heads, keys = cols // HD, sources * rows
    frames = rows // PATCH
    flops = 4 * blocks * rows * keys * cols
    return pl.pallas_call(
        functools.partial(attend_kernel, blocks, sources, heads, frames),
        out_shape=[jax.ShapeDtypeStruct((rows, 128), jnp.float32)] * blocks,
        in_specs=[SM, VM, VM] + [VM] * blocks + [ANY] * sources,
        out_specs=[VM] * blocks,
        scratch_shapes=[
            pltpu.VMEM((heads, keys, HD), jnp.bfloat16),
            pltpu.VMEM((heads, keys, HD), jnp.bfloat16),
            pltpu.VMEM((rows, keys), jnp.float32),
            pltpu.VMEM((rows, keys), jnp.float32),
            pltpu.VMEM((rows, 128), jnp.float32),
            pltpu.VMEM((rows, 128), jnp.float32),
            pltpu.SemaphoreType.DMA((heads, 2)),
        ],
        cost_estimate=pl.CostEstimate(
            flops=flops, bytes_accessed=4 * keys * cols, transcendentals=blocks * rows * keys * heads
        ),
        name="attend",
    )(steps, scale, weight, *qs, *kvs)


WINDOW = ((-1, 1), (0, 0), (0, 1), (1, 0))


def move_matrix(di, dj):
    m = np.zeros((PATCH, PATCH), np.float32)
    for i in range(GRID_H):
        for j in range(GRID_W):
            if 0 <= i + di < GRID_H and 0 <= j + dj < GRID_W:
                m[i * GRID_W + j, (i + di) * GRID_W + j + dj] = 1.0
    return m


OFFSETS = [(di, dj) for di in (-1, 0, 1) for dj in (-1, 0, 1)]


def gather_constants():
    move = np.concatenate([move_matrix(di, dj) for di, dj in OFFSETS], axis=1)
    place = np.zeros((LAT, len(OFFSETS), 16 * LAT_C), np.float32)
    for u, (di, a) in enumerate(WINDOW):
        for w, (dj, b) in enumerate(WINDOW):
            for c in range(LAT_C):
                place[(2 * a + b) * LAT_C + c, OFFSETS.index((di, dj)), (4 * u + w) * LAT_C + c] = 1.0
    return (
        jnp.asarray(move, jnp.bfloat16),
        jnp.asarray(place.reshape(LAT, -1), jnp.bfloat16),
    )


def plane_moves():
    planes = []
    for a in (0, 1):
        for b in (0, 1):
            da, db = (1, -1)[a], (1, -1)[b]
            planes.append(
                np.concatenate([move_matrix(da, 0), move_matrix(0, db), move_matrix(da, db)], axis=0)
            )
    return jnp.asarray(np.stack(planes), jnp.bfloat16)


def pixel_order():
    m = np.zeros((4 * PATCH, 4 * PATCH), np.float32)
    for i in range(GRID_H):
        for j in range(GRID_W):
            for a in (0, 1):
                for b in (0, 1):
                    row = (2 * i + a) * 2 * GRID_W + 2 * j + b
                    m[row, (2 * a + b) * PATCH + i * GRID_W + j] = 1.0
    return jnp.asarray(m, jnp.bfloat16)


def latent_kernel(parts, width, frames, dt_ref, *refs):
    part_refs, refs = refs[:parts], refs[parts:]
    lat_ref, base_ref, move_ref, place_ref, next_ref, win_ref = refs
    total = part_refs[0][...]
    for r in part_refs[1:]:
        total = total + r[...]
    inverse = lax.rsqrt(total[:, LAT:] * np.float32(1.0 / width) + 1e-06)
    scaled = total[:, :LAT] * inverse
    for f in range(frames):
        at = slice(f * PATCH, (f + 1) * PATCH)
        value = lat_ref[at] + dt_ref[f] * (scaled[at] + base_ref[f : f + 1])
        next_ref[at] = value
        spread = jnp.dot(
            value.astype(jnp.bfloat16), place_ref[...], preferred_element_type=jnp.float32
        ).astype(jnp.bfloat16)
        cols = 16 * LAT_C
        stacked = jnp.concatenate(
            [spread[:, o * cols : (o + 1) * cols] for o in range(len(OFFSETS))], axis=0
        )
        win_ref[at] = jnp.dot(
            move_ref[...], stacked, preferred_element_type=jnp.float32
        ).astype(jnp.bfloat16)


def step_latent(parts, latent_in, base, step_dt, width):
    rows = latent_in.shape[0]
    move, place = gather_constants()
    return pl.pallas_call(
        functools.partial(latent_kernel, len(parts), width, rows // PATCH),
        out_shape=[
            jax.ShapeDtypeStruct((rows, LAT), jnp.float32),
            jax.ShapeDtypeStruct((rows, 16 * LAT_C), jnp.bfloat16),
        ],
        in_specs=[SM] + [VM] * (len(parts) + 4),
        out_specs=[VM, VM],
        name="latent",
    )(step_dt, *parts, latent_in, base, move, place)


def decode_kernel(
    frames,
    lead_ref,
    far_ref,
    near_ref,
    own_ref,
    w1_ref,
    b1_ref,
    gain_ref,
    b2_ref,
    pg_ref,
    moves_ref,
    order_ref,
    w2_hbm,
    pw_hbm,
    out_ref,
    pool_ref,
    w2_s,
    pw_s,
    win_s,
    x_s,
    sem,
):
    taps = 9 * CH
    w2_copy = pltpu.make_async_copy(w2_hbm, w2_s, sem.at[0])
    pw_copy = pltpu.make_async_copy(pw_hbm, pw_s, sem.at[1])
    w2_copy.start()
    pw_copy.start()
    rows = frames * PATCH
    for n, r in enumerate((far_ref, near_ref, own_ref)):
        win_s[n * rows : (n + 1) * rows] = r[...]
    wide = frames + 2
    skip = 3 * frames - wide - 2
    cols = 16 * LAT_C
    firsts = []
    for q in range(4):
        acc = jnp.zeros((wide * PATCH, CH), jnp.float32)
        for t in range(3):
            acc = acc + jnp.dot(
                win_s[(skip + t) * PATCH : (skip + t + wide) * PATCH],
                w1_ref[t * cols : (t + 1) * cols, q * CH : (q + 1) * CH],
                preferred_element_type=jnp.float32,
            )
        first = (acc + b1_ref[...]).astype(jnp.bfloat16).astype(jnp.float32)
        firsts.append(first[2 * PATCH :])
        mean = jnp.mean(first * first, axis=-1, keepdims=True)
        v = first * lax.rsqrt(mean + 1e-06) * gain_ref[...]
        act = v / (1.0 + jnp.exp(-v))
        row = lax.broadcasted_iota(jnp.int32, (wide * PATCH, 1), 0)
        act = jnp.where((row >= 2 * PATCH) | (lead_ref[0] == 0), act, 0.0).astype(jnp.bfloat16)
        a, b = q // 2, q % 2
        for f in range(wide):
            plane = act[f * PATCH : (f + 1) * PATCH]
            moved = jnp.dot(
                moves_ref[q], plane, preferred_element_type=jnp.float32
            ).astype(jnp.bfloat16)
            pieces = {
                (0, 0): plane,
                (1, 0): moved[:PATCH],
                (0, 1): moved[PATCH : 2 * PATCH],
                (1, 1): moved[2 * PATCH :],
            }
            for (ma, mb), piece in pieces.items():
                u = WINDOW.index(((1, -1)[a] if ma else 0, a))
                w = WINDOW.index(((1, -1)[b] if mb else 0, b))
                for oa in (0, 1):
                    for ob in (0, 1):
                        dy, dz = u - oa, w - ob
                        if 0 <= dy < 3 and 0 <= dz < 3:
                            at = (f * 4 + 2 * oa + ob) * PATCH
                            tap = (3 * dy + dz) * CH
                            x_s[at : at + PATCH, tap : tap + CH] = piece
    w2_copy.wait()
    block = 4 * PATCH
    out = jnp.zeros((frames * block, CH), jnp.float32)
    for t in range(3):
        out = out + jnp.dot(
            x_s[t * block : (t + frames) * block],
            w2_s[t * taps : (t + 1) * taps],
            preferred_element_type=jnp.float32,
        )
    first = jnp.concatenate(
        [firsts[q][f * PATCH : (f + 1) * PATCH] for f in range(frames) for q in range(4)], axis=0
    )
    dec = (out + b2_ref[...] + first).astype(jnp.bfloat16)
    for f in range(frames):
        out_ref[f * block : (f + 1) * block] = jnp.dot(
            order_ref[...], dec[f * block : (f + 1) * block], preferred_element_type=jnp.float32
        ).astype(jnp.bfloat16)
    pw_copy.wait()
    emb = jnp.zeros((rows, pw_s.shape[1]), jnp.float32)
    for q in range(4):
        lhs = jnp.concatenate(
            [dec[(f * 4 + q) * PATCH : (f * 4 + q + 1) * PATCH] for f in range(frames)], axis=0
        )
        emb = emb + jnp.dot(
            lhs, pw_s[q * CH : (q + 1) * CH], preferred_element_type=jnp.float32
        )
    emb = emb.astype(jnp.bfloat16).astype(jnp.float32)
    centered = emb - jnp.mean(emb, axis=-1, keepdims=True)
    variance = jnp.mean(centered * centered, axis=-1, keepdims=True)
    normed = centered * lax.rsqrt(variance + 1e-05) * pg_ref[...]
    for f in range(frames):
        pool_ref[f : f + 1] = jnp.mean(
            normed[f * PATCH : (f + 1) * PATCH], axis=0, keepdims=True
        )


def window_weight(weight):
    taps = weight.reshape(3, 3, 3, LAT_C, CH)
    grown = [
        jnp.pad(taps, ((0, 0), (a, 1 - a), (b, 1 - b), (0, 0), (0, 0))).reshape(-1, CH)
        for a in (0, 1)
        for b in (0, 1)
    ]
    return jnp.concatenate(grown, axis=1)


def decode(lead, far, near, own, w1, b1, gain, w2, b2, pw, patch_gain):
    rows = own.shape[0]
    frames = rows // PATCH
    wide = frames + 2
    width = pw.shape[1]
    return pl.pallas_call(
        functools.partial(decode_kernel, frames),
        out_shape=[
            jax.ShapeDtypeStruct((frames * 4 * PATCH, CH), jnp.bfloat16),
            jax.ShapeDtypeStruct((frames, width), jnp.float32),
        ],
        in_specs=[SM] + [VM] * 10 + [ANY, ANY],
        out_specs=[VM, VM],
        scratch_shapes=[
            pltpu.VMEM(w2.shape, jnp.bfloat16),
            pltpu.VMEM(pw.shape, jnp.bfloat16),
            pltpu.VMEM((3 * rows, 16 * LAT_C), jnp.bfloat16),
            pltpu.VMEM((wide * 4 * PATCH, 9 * CH), jnp.bfloat16),
            pltpu.SemaphoreType.DMA((2,)),
        ],
        name="decode",
    )(lead, far, near, own, w1, b1, gain, b2, patch_gain, plane_moves(), pixel_order(), w2, pw)


def layer_norm(matrix, gain_vec):
    centered = matrix - jnp.mean(matrix, axis=-1, keepdims=True)
    variance = jnp.mean(centered * centered, axis=-1, keepdims=True)
    return centered * lax.rsqrt(variance + 1e-05) * gain_vec


def rate(image_vec, text_vector):
    inner = jnp.sum(image_vec * text_vector[None, :], axis=-1)
    image_rms = jnp.sqrt(jnp.mean(image_vec * image_vec, axis=-1) + 1e-06)
    text_rms = jnp.sqrt(jnp.mean(text_vector * text_vector) + 1e-06)
    return 100.0 * inner / (TEXT_W * image_rms * text_rms)


def local(
    queries,
    keys,
    values,
    latent_in,
    mod_table,
    step_size,
    timestep,
    head_weight,
    conv_in_weight,
    conv_in_bias,
    norm_gain,
    conv_weight,
    conv_bias,
    patch_weight,
    patch_gain,
    post_gain,
    proj_weight,
    text_table,
    prompt_ids,
    frame_order,
):
    rows, width = queries.shape
    devices = lax.axis_size("seq")
    chips = devices // 2
    cols = width // chips
    heads = cols // HD
    frames = rows // PATCH
    me = lax.axis_index("seq")
    chip, core = me // 2, me % 2

    def columns(matrix, turn):
        return lax.dynamic_slice_in_dim(matrix, ((chip + turn) % chips) * cols, cols, 1)

    received = []
    for turn in range(chips):
        block = jnp.stack([columns(keys, turn), columns(values, turn)])
        received.append(rotate(block, "seq", turn) if turn else block)
    kvs = []
    for block in received:
        kvs += [block, swap_core(block, "seq")]
    qs = []
    for turn in range(chips):
        block = columns(queries, turn)
        qs.append(rotate(block, "seq", turn) if turn else block)

    scale = lax.dynamic_slice_in_dim(mod_table[:, 1, :], chip * cols, cols, 1)
    scale = scale.reshape(-1, heads, 1, HD)
    weight = lax.dynamic_slice_in_dim(head_weight, chip * cols, cols, 0).reshape(heads, HD, LAT)
    weight = jnp.pad(weight, ((0, 0), (0, 0), (0, 128 - LAT)))
    steps_of = timestep.reshape(devices, frames)
    own_steps = lax.dynamic_slice_in_dim(timestep, me * frames, frames, 0)
    base = jnp.dot(jnp.take(mod_table[:, 0, :], own_steps, axis=0), head_weight, precision=highest)
    step_dt = jnp.take(step_size, own_steps)

    parts = []
    group = 2
    for first in range(0, chips, group):
        turns = range(first, first + group)
        origin = jnp.stack([2 * ((chip - t) % chips) + core for t in turns])
        steps = jnp.take(steps_of, origin, axis=0).reshape(-1)
        shares = attend([qs[t] for t in turns], kvs, steps, scale, weight)
        for t, share in zip(turns, shares):
            parts.append(rotate(share, "seq", chips - t) if t else share)

    latent_next, window = step_latent(parts, latent_in, base, step_dt, width)
    near = shifted(window, "seq", 1)
    far = shifted(window, "seq", 2)
    decoded, pooled = decode(
        (me == 0).astype(jnp.int32).reshape(1),
        far,
        near,
        window,
        window_weight(conv_in_weight),
        conv_in_bias.reshape(1, -1),
        norm_gain.reshape(1, -1),
        conv_weight.reshape(-1, CH),
        conv_bias.reshape(1, -1),
        patch_weight,
        patch_gain.reshape(1, -1),
    )
    decoded = decoded.reshape(frames, 2 * GRID_H, 2 * GRID_W, CH)
    image_src = jnp.dot(layer_norm(pooled, post_gain), proj_weight, precision=highest)

    own_text = jnp.mean(jnp.take(text_table, prompt_ids, axis=0).astype(jnp.float32), axis=0)
    text_row = lax.dynamic_update_slice_in_dim(
        jnp.zeros((TEXT_W,), jnp.float32), own_text, me * own_text.shape[0], 0
    )
    sent = jnp.concatenate([image_src, text_row[None]], axis=0)
    sent = jnp.broadcast_to(sent[None], (devices,) + sent.shape)
    spread = lax.all_to_all(sent, "seq", split_axis=0, concat_axis=0, tiled=True)
    text_vector = jnp.sum(spread[:, frames, :], axis=0)
    slots = lax.dynamic_slice_in_dim(frame_order, me * frames, frames, 0)
    image_vec = jnp.take(spread[:, :frames, :].reshape(-1, TEXT_W), slots, axis=0)
    return (latent_next, decoded, image_vec, rate(image_vec, text_vector))


def solution(mesh):
    in_specs = (
        P(("grp", "seq"), None),
        P(("grp", "seq"), None),
        P(("grp", "seq"), None),
        P(("grp", "seq"), None),
        P(),
        P(),
        P("grp"),
        P(),
        P(),
        P(),
        P(),
        P(),
        P(),
        P(),
        P(),
        P(),
        P(),
        P(None, "seq"),
        P("grp"),
        P("grp"),
    )
    out_specs = (
        P(("grp", "seq"), None),
        P(("grp", "seq"), None, None, None),
        P(("grp", "seq"), None),
        P(("grp", "seq")),
    )
    return jax.shard_map(local, mesh=mesh, in_specs=in_specs, out_specs=out_specs, check_vma=False)
```

```python
import functools

import jax
import jax.numpy as jnp
import numpy as np
from jax import lax
from jax.experimental import pallas as pl
from jax.experimental.pallas import tpu as pltpu
from jax.sharding import PartitionSpec as P

GRID_H = 8
GRID_W = 12
PATCH = GRID_H * GRID_W
HD = 128
LAT = 64
LAT_C = 16
CH = 384
TEXT_W = 768
KEY_CHUNK = 512


highest = lax.Precision.HIGHEST
VM = pl.BlockSpec(memory_space=pltpu.VMEM)
SM = pl.BlockSpec(memory_space=pltpu.SMEM)
ANY = pl.BlockSpec(memory_space=pl.ANY)


def shifted(value, axis, steps):
    count = lax.axis_size(axis)
    initial, last = (max(0, -steps), min(count, count - steps))
    return lax.ppermute(value, axis, [(source, source + steps) for source in range(initial, last)])


def rotate(value, axis, steps):
    count = lax.axis_size(axis)
    return lax.ppermute(value, axis, [(i, (i + 2 * steps) % count) for i in range(count)])


def swap_core(value, axis):
    count = lax.axis_size(axis)
    return lax.ppermute(value, axis, [(i, i ^ 1) for i in range(count)])


def pack_kernel(blocks, at_ref, k_hbm, v_hbm, q_hbm, *refs):
    out_refs, (buf, in_sem, out_sem) = refs[:blocks], refs[blocks:]
    width = buf.shape[3]
    gets = []
    for n in range(blocks):
        at = pl.multiple_of(at_ref[n], HD)
        gets.append(
            [
                pltpu.make_async_copy(src.at[:, pl.ds(at, width)], buf.at[n, i], in_sem.at[n, i])
                for i, src in enumerate((k_hbm, v_hbm, q_hbm))
            ]
        )
        for get in gets[-1]:
            get.start()
    puts = [
        pltpu.make_async_copy(buf.at[n], out_refs[n], out_sem.at[n]) for n in range(blocks)
    ]
    for n in range(blocks):
        for get in gets[n]:
            get.wait()
        puts[n].start()
    for put in puts:
        put.wait()


def pack(keys, values, queries, starts, width):
    rows, blocks = keys.shape[0], starts.shape[0]
    return pl.pallas_call(
        functools.partial(pack_kernel, blocks),
        out_shape=[jax.ShapeDtypeStruct((3, rows, width), jnp.bfloat16)] * blocks,
        in_specs=[SM, ANY, ANY, ANY],
        out_specs=[ANY] * blocks,
        scratch_shapes=[
            pltpu.VMEM((blocks, 3, rows, width), jnp.bfloat16),
            pltpu.SemaphoreType.DMA((blocks, 3)),
            pltpu.SemaphoreType.DMA((blocks,)),
        ],
        name="pack",
    )(starts, keys, values, queries)


def attend_kernel(blocks, heads, frames, resumed, last, t_ref, sc_ref, w_ref, *refs):
    if resumed:
        prev_ref, refs = refs[0], refs[1:]
    near_refs, far_refs, refs = refs[:blocks], refs[blocks : 2 * blocks], refs[2 * blocks :]
    if last:
        out_refs, refs = refs[:blocks], refs[blocks:]
    else:
        sum_ref, refs = refs[0], refs[1:]
    q_s, k_s, v_s, s_a, s_b, m_a, m_b, sem, q_sem = refs[:9]
    if last:
        sum_ref = refs[9]
    sources = near_refs + far_refs
    rows = near_refs[0].shape[1]
    keys = len(sources) * rows
    scale = np.float32(HD**-0.5 * np.log2(np.e))

    def fetch(h, which):
        dst = (k_s, v_s)[which]
        for j, src in enumerate(sources):
            pltpu.make_async_copy(
                src.at[which, :, pl.ds(h * HD, HD)],
                dst.at[h, pl.ds(j * rows, rows), :],
                sem.at[h, which],
            ).start()

    fetch(0, 0)
    for b in range(blocks):
        pltpu.make_async_copy(near_refs[b].at[2], q_s.at[b], q_sem).start()
    fetch(0, 1)
    for h in range(1, heads):
        fetch(h, 0)
        fetch(h, 1)
    if resumed:
        sum_ref[...] = prev_ref[...]
    else:
        sum_ref[...] = jnp.zeros(sum_ref.shape, jnp.float32)

    def arrived(h, which):
        whole = (k_s, v_s)[which].at[h]
        pltpu.make_async_copy(whole, whole, sem.at[h, which]).wait()

    def logits(h, b, at, s_ref, peak):
        q = q_s[b, :, pl.ds(pl.multiple_of(h * HD, HD), HD)]
        s = lax.dot_general(
            q,
            k_s[h, at : at + KEY_CHUNK, :],
            (((1,), (1,)), ((), ())),
            preferred_element_type=jnp.float32,
        )
        s_ref[:, at : at + KEY_CHUNK] = s
        folded = functools.reduce(
            jnp.maximum, [s[:, i : i + 128] for i in range(0, KEY_CHUNK, 128)]
        )
        return folded if peak is None else jnp.maximum(peak, folded)

    def keep_peak(peak, m_ref):
        m_ref[...] = jnp.broadcast_to(jnp.max(peak, axis=-1, keepdims=True) * scale, m_ref.shape)

    def one_unit(h, b, now, top_ref, next_h, next_b, later, later_top_ref):
        top = top_ref[:, :1]
        peak, total = None, None
        acc = jnp.zeros((rows, HD), jnp.float32)
        for at in chunks:
            peak = logits(next_h, next_b, at, later, peak)
            e = jnp.exp2(now[:, at : at + KEY_CHUNK] * scale - top)
            folded = functools.reduce(jnp.add, [e[:, i : i + 128] for i in range(0, KEY_CHUNK, 128)])
            total = folded if total is None else total + folded
            acc = acc + jnp.dot(
                e.astype(jnp.bfloat16),
                v_s[h, at : at + KEY_CHUNK, :],
                preferred_element_type=jnp.float32,
            )
        keep_peak(peak, later_top_ref)
        o = acc / jnp.sum(total, axis=-1, keepdims=True)
        o = o.astype(jnp.bfloat16).astype(jnp.float32)
        square = jnp.sum(o * o, axis=-1, keepdims=True)
        per = rows // frames
        scaled = jnp.concatenate(
            [
                o[f * per : (f + 1) * per] * (1.0 + sc_ref[t_ref[b * frames + f], h])
                for f in range(frames)
            ],
            axis=0,
        )
        part = jnp.dot(scaled, w_ref[h], precision=highest, preferred_element_type=jnp.float32)
        lane = lax.broadcasted_iota(jnp.int32, part.shape, 1)
        sum_ref[b] = sum_ref[b] + part + jnp.where(lane >= LAT, square, 0.0)

    chunks = range(0, keys, KEY_CHUNK)
    pltpu.make_async_copy(q_s, q_s, q_sem).wait()
    arrived(0, 0)
    peak = None
    for at in chunks:
        peak = logits(0, 0, at, s_a, peak)
    keep_peak(peak, m_a)
    pairs = blocks // 2

    def one_pair(n, carry):
        h, p = n // pairs, n % pairs
        after = jnp.minimum(n + 1, heads * pairs - 1)
        after_h, after_p = after // pairs, after % pairs

        @pl.when(p == 0)
        def _():
            arrived(h, 1)

        @pl.when(after_h > h)
        def _():
            arrived(after_h, 0)

        one_unit(h, 2 * p, s_a, m_a, h, 2 * p + 1, s_b, m_b)
        one_unit(h, 2 * p + 1, s_b, m_b, after_h, 2 * after_p, s_a, m_a)
        return carry

    lax.fori_loop(0, heads * pairs, one_pair, 0)
    if last:
        for b in range(blocks):
            share = sum_ref[b]
            high = share.astype(jnp.bfloat16)
            rest = (share - high.astype(jnp.float32)).astype(jnp.bfloat16)
            lane = lax.broadcasted_iota(jnp.int32, share.shape, 1)
            out_refs[b][...] = jnp.where(lane < 3 * LAT // 2, high, rest)


def attend(near, far, steps, scale, weight, previous, last):
    blocks = len(near)
    _, rows, cols = near[0].shape
    heads, keys = cols // HD, 2 * blocks * rows
    frames = rows // PATCH
    resumed = previous is not None
    sums = (blocks, rows, 128)
    if last:
        out_shape = [jax.ShapeDtypeStruct(sums[1:], jnp.bfloat16)] * blocks
        out_specs = [VM] * blocks
    else:
        out_shape, out_specs = jax.ShapeDtypeStruct(sums, jnp.float32), VM
    return pl.pallas_call(
        functools.partial(attend_kernel, blocks, heads, frames, resumed, last),
        out_shape=out_shape,
        in_specs=[SM, VM, VM] + [VM] * resumed + [ANY] * (2 * blocks),
        out_specs=out_specs,
        scratch_shapes=[
            pltpu.VMEM((blocks, rows, cols), jnp.bfloat16),
            pltpu.VMEM((heads, keys, HD), jnp.bfloat16),
            pltpu.VMEM((heads, keys, HD), jnp.bfloat16),
            pltpu.VMEM((rows, keys), jnp.float32),
            pltpu.VMEM((rows, keys), jnp.float32),
            pltpu.VMEM((rows, 128), jnp.float32),
            pltpu.VMEM((rows, 128), jnp.float32),
            pltpu.SemaphoreType.DMA((heads, 2)),
            pltpu.SemaphoreType.DMA,
        ]
        + [pltpu.VMEM(sums, jnp.float32)] * last,
        cost_estimate=pl.CostEstimate(
            flops=4 * blocks * rows * keys * cols,
            bytes_accessed=4 * keys * cols,
            transcendentals=blocks * rows * keys * heads,
        ),
        name="attend",
    )(steps, scale, weight, *([previous] if resumed else []), *near, *far)


WINDOW = ((-1, 1), (0, 0), (0, 1), (1, 0))


def move_matrix(di, dj):
    m = np.zeros((PATCH, PATCH), np.float32)
    for i in range(GRID_H):
        for j in range(GRID_W):
            if 0 <= i + di < GRID_H and 0 <= j + dj < GRID_W:
                m[i * GRID_W + j, (i + di) * GRID_W + j + dj] = 1.0
    return m


OFFSETS = [(di, dj) for di in (-1, 0, 1) for dj in (-1, 0, 1)]


def gather_constants():
    move = np.concatenate([move_matrix(di, dj) for di, dj in OFFSETS], axis=1)
    place = np.zeros((LAT, len(OFFSETS), 16 * LAT_C), np.float32)
    for u, (di, a) in enumerate(WINDOW):
        for w, (dj, b) in enumerate(WINDOW):
            for c in range(LAT_C):
                place[(2 * a + b) * LAT_C + c, OFFSETS.index((di, dj)), (4 * u + w) * LAT_C + c] = 1.0
    return (
        jnp.asarray(move, jnp.bfloat16),
        jnp.asarray(place.reshape(LAT, -1), jnp.bfloat16),
    )


def plane_moves():
    planes = []
    for a in (0, 1):
        for b in (0, 1):
            da, db = (1, -1)[a], (1, -1)[b]
            planes.append(
                np.concatenate([move_matrix(da, 0), move_matrix(0, db), move_matrix(da, db)], axis=0)
            )
    return jnp.asarray(np.stack(planes), jnp.bfloat16)


def pixel_order():
    m = np.zeros((4 * PATCH, 4 * PATCH), np.float32)
    for i in range(GRID_H):
        for j in range(GRID_W):
            for a in (0, 1):
                for b in (0, 1):
                    row = (2 * i + a) * 2 * GRID_W + 2 * j + b
                    m[row, (2 * a + b) * PATCH + i * GRID_W + j] = 1.0
    return jnp.asarray(m, jnp.bfloat16)


def latent_kernel(parts, width, frames, dt_ref, *refs):
    part_refs, refs = refs[:parts], refs[parts:]
    lat_ref, base_ref, move_ref, place_ref, next_ref, win_ref = refs
    total = part_refs[0][...].astype(jnp.float32)
    for r in part_refs[1:]:
        total = total + r[...].astype(jnp.float32)
    half = LAT // 2
    square = total[:, LAT : LAT + half] + total[:, LAT + half :]
    inverse = lax.rsqrt(square * np.float32(1.0 / width) + 1e-06)
    scaled = total[:, :LAT] * jnp.concatenate([inverse, inverse], axis=1)
    for f in range(frames):
        at = slice(f * PATCH, (f + 1) * PATCH)
        value = lat_ref[at] + dt_ref[f] * (scaled[at] + base_ref[f : f + 1])
        next_ref[at] = value
        spread = jnp.dot(
            value.astype(jnp.bfloat16), place_ref[...], preferred_element_type=jnp.float32
        ).astype(jnp.bfloat16)
        cols = 16 * LAT_C
        stacked = jnp.concatenate(
            [spread[:, o * cols : (o + 1) * cols] for o in range(len(OFFSETS))], axis=0
        )
        win_ref[at] = jnp.dot(
            move_ref[...], stacked, preferred_element_type=jnp.float32
        ).astype(jnp.bfloat16)


def step_latent(parts, latent_in, base, step_dt, width):
    rows = latent_in.shape[0]
    move, place = gather_constants()
    return pl.pallas_call(
        functools.partial(latent_kernel, len(parts), width, rows // PATCH),
        out_shape=[
            jax.ShapeDtypeStruct((rows, LAT), jnp.float32),
            jax.ShapeDtypeStruct((rows, 16 * LAT_C), jnp.bfloat16),
        ],
        in_specs=[SM] + [VM] * (len(parts) + 4),
        out_specs=[VM, VM],
        name="latent",
    )(step_dt, *parts, latent_in, base, move, place)


def decode_kernel(
    frames,
    lead_ref,
    far_ref,
    near_ref,
    own_ref,
    w1_ref,
    b1_ref,
    gain_ref,
    b2_ref,
    pg_ref,
    post_ref,
    text_ref,
    moves_ref,
    order_ref,
    w2_hbm,
    pw_hbm,
    proj_hbm,
    out_ref,
    sent_ref,
    w2_s,
    pw_s,
    proj_s,
    win_s,
    x_s,
    sem,
):
    taps = 9 * CH
    w2_copy = pltpu.make_async_copy(w2_hbm, w2_s, sem.at[0])
    pw_copy = pltpu.make_async_copy(pw_hbm, pw_s, sem.at[1])
    w2_copy.start()
    pw_copy.start()
    proj_copy = pltpu.make_async_copy(proj_hbm, proj_s, sem.at[2])
    proj_copy.start()
    rows = frames * PATCH
    for n, r in enumerate((far_ref, near_ref, own_ref)):
        win_s[n * rows : (n + 1) * rows] = r[...]
    wide = frames + 2
    skip = 3 * frames - wide - 2
    cols = 16 * LAT_C
    firsts = []
    for q in range(4):
        acc = jnp.zeros((wide * PATCH, CH), jnp.float32)
        for t in range(3):
            acc = acc + jnp.dot(
                win_s[(skip + t) * PATCH : (skip + t + wide) * PATCH],
                w1_ref[t * cols : (t + 1) * cols, q * CH : (q + 1) * CH],
                preferred_element_type=jnp.float32,
            )
        first = (acc + b1_ref[...]).astype(jnp.bfloat16).astype(jnp.float32)
        firsts.append(first[2 * PATCH :])
        mean = jnp.mean(first * first, axis=-1, keepdims=True)
        v = first * lax.rsqrt(mean + 1e-06) * gain_ref[...]
        act = v / (1.0 + jnp.exp(-v))
        row = lax.broadcasted_iota(jnp.int32, (wide * PATCH, 1), 0)
        act = jnp.where((row >= 2 * PATCH) | (lead_ref[0] == 0), act, 0.0).astype(jnp.bfloat16)
        a, b = q // 2, q % 2
        for f in range(wide):
            plane = act[f * PATCH : (f + 1) * PATCH]
            moved = jnp.dot(
                moves_ref[q], plane, preferred_element_type=jnp.float32
            ).astype(jnp.bfloat16)
            pieces = {
                (0, 0): plane,
                (1, 0): moved[:PATCH],
                (0, 1): moved[PATCH : 2 * PATCH],
                (1, 1): moved[2 * PATCH :],
            }
            for (ma, mb), piece in pieces.items():
                u = WINDOW.index(((1, -1)[a] if ma else 0, a))
                w = WINDOW.index(((1, -1)[b] if mb else 0, b))
                for oa in (0, 1):
                    for ob in (0, 1):
                        dy, dz = u - oa, w - ob
                        if 0 <= dy < 3 and 0 <= dz < 3:
                            at = (f * 4 + 2 * oa + ob) * PATCH
                            tap = (3 * dy + dz) * CH
                            x_s[at : at + PATCH, tap : tap + CH] = piece
    w2_copy.wait()
    block = 4 * PATCH
    out = jnp.zeros((frames * block, CH), jnp.float32)
    for t in range(3):
        out = out + jnp.dot(
            x_s[t * block : (t + frames) * block],
            w2_s[t * taps : (t + 1) * taps],
            preferred_element_type=jnp.float32,
        )
    first = jnp.concatenate(
        [firsts[q][f * PATCH : (f + 1) * PATCH] for f in range(frames) for q in range(4)], axis=0
    )
    dec = (out + b2_ref[...] + first).astype(jnp.bfloat16)
    for f in range(frames):
        out_ref[f * block : (f + 1) * block] = jnp.dot(
            order_ref[...], dec[f * block : (f + 1) * block], preferred_element_type=jnp.float32
        ).astype(jnp.bfloat16)
    pw_copy.wait()
    emb = jnp.zeros((rows, pw_s.shape[1]), jnp.float32)
    for q in range(4):
        lhs = jnp.concatenate(
            [dec[(f * 4 + q) * PATCH : (f * 4 + q + 1) * PATCH] for f in range(frames)], axis=0
        )
        emb = emb + jnp.dot(
            lhs, pw_s[q * CH : (q + 1) * CH], preferred_element_type=jnp.float32
        )
    emb = emb.astype(jnp.bfloat16).astype(jnp.float32)
    centered = emb - jnp.mean(emb, axis=-1, keepdims=True)
    variance = jnp.mean(centered * centered, axis=-1, keepdims=True)
    normed = centered * lax.rsqrt(variance + 1e-05) * pg_ref[...]
    pooled = jnp.concatenate(
        [
            jnp.mean(normed[f * PATCH : (f + 1) * PATCH], axis=0, keepdims=True)
            for f in range(frames)
        ],
        axis=0,
    )
    centered = pooled - jnp.mean(pooled, axis=-1, keepdims=True)
    variance = jnp.mean(centered * centered, axis=-1, keepdims=True)
    vec = centered * lax.rsqrt(variance + 1e-05) * post_ref[...]
    columns = jnp.transpose(
        jnp.concatenate([vec, jnp.zeros((8 - frames, vec.shape[1]), jnp.float32)], axis=0)
    )
    proj_copy.wait()
    for f in range(frames):
        row = jnp.sum(columns[:, f : f + 1] * proj_s[...], axis=0, keepdims=True)
        for n in range(sent_ref.shape[0]):
            sent_ref[n, f : f + 1, :] = row
    for n in range(sent_ref.shape[0]):
        sent_ref[n, frames : frames + 1, :] = text_ref[...]


def window_weight(weight):
    taps = weight.reshape(3, 3, 3, LAT_C, CH)
    grown = [
        jnp.pad(taps, ((0, 0), (a, 1 - a), (b, 1 - b), (0, 0), (0, 0))).reshape(-1, CH)
        for a in (0, 1)
        for b in (0, 1)
    ]
    return jnp.concatenate(grown, axis=1)


def decode(lead, far, near, own, w1, b1, gain, w2, b2, pw, patch_gain, post_gain, proj, text, devices):
    rows = own.shape[0]
    frames = rows // PATCH
    wide = frames + 2
    return pl.pallas_call(
        functools.partial(decode_kernel, frames),
        out_shape=[
            jax.ShapeDtypeStruct((frames * 4 * PATCH, CH), jnp.bfloat16),
            jax.ShapeDtypeStruct((devices, frames + 1, proj.shape[1]), jnp.float32),
        ],
        in_specs=[SM] + [VM] * 12 + [ANY, ANY, ANY],
        out_specs=[VM, VM],
        scratch_shapes=[
            pltpu.VMEM(w2.shape, jnp.bfloat16),
            pltpu.VMEM(pw.shape, jnp.bfloat16),
            pltpu.VMEM(proj.shape, jnp.float32),
            pltpu.VMEM((3 * rows, 16 * LAT_C), jnp.bfloat16),
            pltpu.VMEM((wide * 4 * PATCH, 9 * CH), jnp.bfloat16),
            pltpu.SemaphoreType.DMA((3,)),
        ],
        name="decode",
    )(
        lead,
        far,
        near,
        own,
        w1,
        b1,
        gain,
        b2,
        patch_gain,
        post_gain,
        text,
        plane_moves(),
        pixel_order(),
        w2,
        pw,
        proj,
    )


def rate_kernel(frames, slot_ref, got_ref, vec_ref, score_ref):
    text = jnp.sum(got_ref[:, frames, :], axis=0, keepdims=True)
    text_rms = jnp.sqrt(jnp.mean(text * text) + 1e-06)
    for f in range(frames):
        slot = slot_ref[f]
        block = got_ref[slot // frames]
        row = block[:1]
        for n in range(1, frames):
            row = jnp.where(slot % frames == n, block[n : n + 1], row)
        vec_ref[f : f + 1] = row
        inner = jnp.sum(row * text)
        image_rms = jnp.sqrt(jnp.mean(row * row) + 1e-06)
        score_ref[f] = 100.0 * inner / (TEXT_W * image_rms * text_rms)


def rate(slots, got):
    frames = slots.shape[0]
    return pl.pallas_call(
        functools.partial(rate_kernel, frames),
        out_shape=[
            jax.ShapeDtypeStruct((frames, got.shape[2]), jnp.float32),
            jax.ShapeDtypeStruct((frames,), jnp.float32),
        ],
        in_specs=[SM, VM],
        out_specs=[VM, SM],
        name="rate",
    )(slots, got)


def local(
    queries,
    keys,
    values,
    latent_in,
    mod_table,
    step_size,
    timestep,
    head_weight,
    conv_in_weight,
    conv_in_bias,
    norm_gain,
    conv_weight,
    conv_bias,
    patch_weight,
    patch_gain,
    post_gain,
    proj_weight,
    text_table,
    prompt_ids,
    frame_order,
):
    rows, width = queries.shape
    devices = lax.axis_size("seq")
    chips = devices // 2
    cols = width // chips
    heads = cols // HD
    frames = rows // PATCH
    me = lax.axis_index("seq")
    chip, core = me // 2, me % 2

    scale = lax.dynamic_slice_in_dim(mod_table[:, 1, :], chip * cols, cols, 1)
    scale = scale.reshape(-1, heads, 1, HD)
    weight = lax.dynamic_slice_in_dim(head_weight, chip * cols, cols, 0).reshape(heads, HD, LAT)
    weight = jnp.pad(weight, ((0, 0), (0, 0), (0, 128 - LAT)))
    origin = 2 * ((chip - jnp.arange(chips)) % chips) + core
    steps = jnp.take(timestep.reshape(devices, frames), origin, axis=0).reshape(-1)
    own_steps = lax.dynamic_slice_in_dim(timestep, me * frames, frames, 0)
    base = jnp.dot(jnp.take(mod_table[:, 0, :], own_steps, axis=0), head_weight, precision=highest)
    step_dt = jnp.take(step_size, own_steps)
    own_text = jnp.mean(jnp.take(text_table, prompt_ids, axis=0).astype(jnp.float32), axis=0)
    text_row = lax.dynamic_update_slice_in_dim(
        jnp.zeros((TEXT_W,), jnp.float32), own_text, me * own_text.shape[0], 0
    )
    slots = lax.dynamic_slice_in_dim(frame_order, me * frames, frames, 0)
    prepared = (
        scale,
        weight,
        steps,
        base,
        step_dt,
        text_row.reshape(1, -1),
        slots,
        window_weight(conv_in_weight),
        conv_in_bias.reshape(1, -1),
        norm_gain.reshape(1, -1),
        conv_bias.reshape(1, -1),
        patch_gain.reshape(1, -1),
        post_gain.reshape(1, -1),
        (me == 0).astype(jnp.int32).reshape(1),
        latent_in,
    )
    (
        scale,
        weight,
        steps,
        base,
        step_dt,
        text_row,
        slots,
        w1,
        b1,
        gain,
        b2,
        patch_gain,
        post_gain,
        lead,
        latent_in,
    ) = lax.optimization_barrier(prepared)

    tail = max(1, heads // 4)
    phases = (heads - tail, tail) if heads > tail else (tail,)
    order = sorted(range(1, chips), key=lambda t: abs(2 * t - chips))
    arrived, first, phase_blocks = None, 0, []
    for count in phases:
        starts = ((chip + jnp.arange(chips)) % chips) * cols + first * HD
        blocks = pack(keys, values, queries, starts.astype(jnp.int32), count * HD)
        got = [blocks[0]] * chips
        for turn in order:
            block = blocks[turn]
            if arrived is not None:
                block, _ = lax.optimization_barrier((block, arrived[turn]))
            got[turn] = rotate(block, "seq", turn)
        phase_blocks.append((first, count, got))
        arrived = got
        first += count
    sums = None
    for first, count, got in phase_blocks:
        sums = attend(
            got,
            [swap_core(block, "seq") for block in got],
            steps,
            scale[:, first : first + count],
            weight[first : first + count],
            sums,
            first + count == heads,
        )
    parts = [sums[0]] + [rotate(sums[t], "seq", chips - t) for t in order]

    latent_next, window = step_latent(parts, latent_in, base, step_dt, width)
    near = shifted(window, "seq", 1)
    far = shifted(window, "seq", 2)
    decoded, sent = decode(
        lead,
        far,
        near,
        window,
        w1,
        b1,
        gain,
        conv_weight.reshape(-1, CH),
        b2,
        patch_weight,
        patch_gain,
        post_gain,
        proj_weight,
        text_row,
        devices,
    )
    decoded = decoded.reshape(frames, 2 * GRID_H, 2 * GRID_W, CH)
    spread = lax.all_to_all(sent, "seq", split_axis=0, concat_axis=0, tiled=True)
    image_vec, scores = rate(slots, spread)
    return (latent_next, decoded, image_vec, scores)


def solution(mesh):
    in_specs = (
        P(("grp", "seq"), None),
        P(("grp", "seq"), None),
        P(("grp", "seq"), None),
        P(("grp", "seq"), None),
        P(),
        P(),
        P("grp"),
        P(),
        P(),
        P(),
        P(),
        P(),
        P(),
        P(),
        P(),
        P(),
        P(),
        P(None, "seq"),
        P("grp"),
        P("grp"),
    )
    out_specs = (
        P(("grp", "seq"), None),
        P(("grp", "seq"), None, None, None),
        P(("grp", "seq"), None),
        P(("grp", "seq")),
    )
    return jax.shard_map(local, mesh=mesh, in_specs=in_specs, out_specs=out_specs, check_vma=False)
```

```python
import functools

import jax
import jax.numpy as jnp
import numpy as np
from jax import lax
from jax.experimental import pallas as pl
from jax.experimental.pallas import tpu as pltpu
from jax.sharding import PartitionSpec as P

GRID_H = 8
GRID_W = 12
PATCH = GRID_H * GRID_W
HD = 128
LAT = 64
LAT_C = 16
CH = 384
TEXT_W = 768
KEY_CHUNK = 512


highest = lax.Precision.HIGHEST
VM = pl.BlockSpec(memory_space=pltpu.VMEM)
SM = pl.BlockSpec(memory_space=pltpu.SMEM)
ANY = pl.BlockSpec(memory_space=pl.ANY)


def shifted(value, axis, steps):
    count = lax.axis_size(axis)
    initial, last = (max(0, -steps), min(count, count - steps))
    return lax.ppermute(value, axis, [(source, source + steps) for source in range(initial, last)])


def rotate(value, axis, steps):
    count = lax.axis_size(axis)
    return lax.ppermute(value, axis, [(i, (i + 2 * steps) % count) for i in range(count)])


def swap_core(value, axis):
    count = lax.axis_size(axis)
    return lax.ppermute(value, axis, [(i, i ^ 1) for i in range(count)])


def pack_kernel(blocks, at_ref, k_hbm, v_hbm, q_hbm, *refs):
    out_refs, (buf, in_sem, out_sem) = refs[:blocks], refs[blocks:]
    width = buf.shape[3]
    gets = []
    for n in range(blocks):
        at = pl.multiple_of(at_ref[n], HD)
        gets.append(
            [
                pltpu.make_async_copy(src.at[:, pl.ds(at, width)], buf.at[n, i], in_sem.at[n, i])
                for i, src in enumerate((k_hbm, v_hbm, q_hbm))
            ]
        )
        for get in gets[-1]:
            get.start()
    puts = [
        pltpu.make_async_copy(buf.at[n], out_refs[n], out_sem.at[n]) for n in range(blocks)
    ]
    for n in range(blocks):
        for get in gets[n]:
            get.wait()
        puts[n].start()
    for put in puts:
        put.wait()


def pack(keys, values, queries, starts, width):
    rows, blocks = keys.shape[0], starts.shape[0]
    return pl.pallas_call(
        functools.partial(pack_kernel, blocks),
        out_shape=[jax.ShapeDtypeStruct((3, rows, width), jnp.bfloat16)] * blocks,
        in_specs=[SM, ANY, ANY, ANY],
        out_specs=[ANY] * blocks,
        scratch_shapes=[
            pltpu.VMEM((blocks, 3, rows, width), jnp.bfloat16),
            pltpu.SemaphoreType.DMA((blocks, 3)),
            pltpu.SemaphoreType.DMA((blocks,)),
        ],
        name="pack",
    )(starts, keys, values, queries)


def attend_kernel(blocks, heads, frames, resumed, last, t_ref, sc_ref, w_ref, *refs):
    if resumed:
        prev_ref, refs = refs[0], refs[1:]
    near_refs, far_refs, refs = refs[:blocks], refs[blocks : 2 * blocks], refs[2 * blocks :]
    if last:
        out_refs, refs = refs[:blocks], refs[blocks:]
    else:
        sum_ref, refs = refs[0], refs[1:]
    q_s, k_s, v_s, s_a, s_b, m_a, m_b, sem, q_sem = refs[:9]
    if last:
        sum_ref = refs[9]
    sources = near_refs + far_refs
    rows = near_refs[0].shape[1]
    keys = len(sources) * rows
    scale = np.float32(HD**-0.5 * np.log2(np.e))

    def fetch(h, which):
        dst = (k_s, v_s)[which]
        for j, src in enumerate(sources):
            pltpu.make_async_copy(
                src.at[which, :, pl.ds(h * HD, HD)],
                dst.at[h, pl.ds(j * rows, rows), :],
                sem.at[h, which],
            ).start()

    fetch(0, 0)
    for b in range(blocks):
        pltpu.make_async_copy(near_refs[b].at[2], q_s.at[b], q_sem).start()
    fetch(0, 1)
    for h in range(1, heads):
        fetch(h, 0)
        fetch(h, 1)
    if resumed:
        sum_ref[...] = prev_ref[...]
    else:
        sum_ref[...] = jnp.zeros(sum_ref.shape, jnp.float32)

    def arrived(h, which):
        whole = (k_s, v_s)[which].at[h]
        pltpu.make_async_copy(whole, whole, sem.at[h, which]).wait()

    def logits(h, b, at, s_ref, peak):
        q = q_s[b, :, pl.ds(pl.multiple_of(h * HD, HD), HD)]
        s = lax.dot_general(
            q,
            k_s[h, at : at + KEY_CHUNK, :],
            (((1,), (1,)), ((), ())),
            preferred_element_type=jnp.float32,
        )
        s_ref[:, at : at + KEY_CHUNK] = s
        folded = functools.reduce(
            jnp.maximum, [s[:, i : i + 128] for i in range(0, KEY_CHUNK, 128)]
        )
        return folded if peak is None else jnp.maximum(peak, folded)

    def keep_peak(peak, m_ref):
        m_ref[...] = jnp.broadcast_to(jnp.max(peak, axis=-1, keepdims=True) * scale, m_ref.shape)

    def one_unit(h, b, now, top_ref, next_h, next_b, later, later_top_ref):
        top = top_ref[:, :1]
        peak, total = None, None
        acc = jnp.zeros((rows, HD), jnp.float32)
        for at in chunks:
            peak = logits(next_h, next_b, at, later, peak)
            e = jnp.exp2(now[:, at : at + KEY_CHUNK] * scale - top)
            folded = functools.reduce(jnp.add, [e[:, i : i + 128] for i in range(0, KEY_CHUNK, 128)])
            total = folded if total is None else total + folded
            acc = acc + jnp.dot(
                e.astype(jnp.bfloat16),
                v_s[h, at : at + KEY_CHUNK, :],
                preferred_element_type=jnp.float32,
            )
        keep_peak(peak, later_top_ref)
        o = acc / jnp.sum(total, axis=-1, keepdims=True)
        o = o.astype(jnp.bfloat16).astype(jnp.float32)
        square = jnp.sum(o * o, axis=-1, keepdims=True)
        per = rows // frames
        scaled = jnp.concatenate(
            [
                o[f * per : (f + 1) * per] * (1.0 + sc_ref[t_ref[b * frames + f], h])
                for f in range(frames)
            ],
            axis=0,
        )
        part = jnp.dot(scaled, w_ref[h], precision=highest, preferred_element_type=jnp.float32)
        lane = lax.broadcasted_iota(jnp.int32, part.shape, 1)
        sum_ref[b] = sum_ref[b] + part + jnp.where(lane >= LAT, square, 0.0)

    chunks = range(0, keys, KEY_CHUNK)
    pltpu.make_async_copy(q_s, q_s, q_sem).wait()
    arrived(0, 0)
    peak = None
    for at in chunks:
        peak = logits(0, 0, at, s_a, peak)
    keep_peak(peak, m_a)
    pairs = blocks // 2

    def one_pair(n, carry):
        h, p = n // pairs, n % pairs
        after = jnp.minimum(n + 1, heads * pairs - 1)
        after_h, after_p = after // pairs, after % pairs

        @pl.when(p == 0)
        def _():
            arrived(h, 1)

        @pl.when(after_h > h)
        def _():
            arrived(after_h, 0)

        one_unit(h, 2 * p, s_a, m_a, h, 2 * p + 1, s_b, m_b)
        one_unit(h, 2 * p + 1, s_b, m_b, after_h, 2 * after_p, s_a, m_a)
        return carry

    lax.fori_loop(0, heads * pairs, one_pair, 0)
    if last:
        for b in range(blocks):
            share = sum_ref[b]
            high = share.astype(jnp.bfloat16)
            rest = (share - high.astype(jnp.float32)).astype(jnp.bfloat16)
            lane = lax.broadcasted_iota(jnp.int32, share.shape, 1)
            out_refs[b][...] = jnp.where(lane < 3 * LAT // 2, high, rest)


def attend(near, far, steps, scale, weight, previous, last):
    blocks = len(near)
    _, rows, cols = near[0].shape
    heads, keys = cols // HD, 2 * blocks * rows
    frames = rows // PATCH
    resumed = previous is not None
    sums = (blocks, rows, 128)
    if last:
        out_shape = [jax.ShapeDtypeStruct(sums[1:], jnp.bfloat16)] * blocks
        out_specs = [VM] * blocks
    else:
        out_shape, out_specs = jax.ShapeDtypeStruct(sums, jnp.float32), VM
    return pl.pallas_call(
        functools.partial(attend_kernel, blocks, heads, frames, resumed, last),
        out_shape=out_shape,
        in_specs=[SM, VM, VM] + [VM] * resumed + [ANY] * (2 * blocks),
        out_specs=out_specs,
        scratch_shapes=[
            pltpu.VMEM((blocks, rows, cols), jnp.bfloat16),
            pltpu.VMEM((heads, keys, HD), jnp.bfloat16),
            pltpu.VMEM((heads, keys, HD), jnp.bfloat16),
            pltpu.VMEM((rows, keys), jnp.float32),
            pltpu.VMEM((rows, keys), jnp.float32),
            pltpu.VMEM((rows, 128), jnp.float32),
            pltpu.VMEM((rows, 128), jnp.float32),
            pltpu.SemaphoreType.DMA((heads, 2)),
            pltpu.SemaphoreType.DMA,
        ]
        + [pltpu.VMEM(sums, jnp.float32)] * last,
        cost_estimate=pl.CostEstimate(
            flops=4 * blocks * rows * keys * cols,
            bytes_accessed=4 * keys * cols,
            transcendentals=blocks * rows * keys * heads,
        ),
        name="attend",
    )(steps, scale, weight, *([previous] if resumed else []), *near, *far)


WINDOW = ((-1, 1), (0, 0), (0, 1), (1, 0))


def move_matrix(di, dj):
    m = np.zeros((PATCH, PATCH), np.float32)
    for i in range(GRID_H):
        for j in range(GRID_W):
            if 0 <= i + di < GRID_H and 0 <= j + dj < GRID_W:
                m[i * GRID_W + j, (i + di) * GRID_W + j + dj] = 1.0
    return m


OFFSETS = [(di, dj) for di in (-1, 0, 1) for dj in (-1, 0, 1)]


def gather_constants():
    move = np.concatenate([move_matrix(di, dj) for di, dj in OFFSETS], axis=1)
    place = np.zeros((LAT, len(OFFSETS), 16 * LAT_C), np.float32)
    for u, (di, a) in enumerate(WINDOW):
        for w, (dj, b) in enumerate(WINDOW):
            for c in range(LAT_C):
                place[(2 * a + b) * LAT_C + c, OFFSETS.index((di, dj)), (4 * u + w) * LAT_C + c] = 1.0
    return (
        jnp.asarray(move, jnp.bfloat16),
        jnp.asarray(place.reshape(LAT, -1), jnp.bfloat16),
    )


def plane_moves():
    planes = []
    for a in (0, 1):
        for b in (0, 1):
            da, db = (1, -1)[a], (1, -1)[b]
            planes.append(
                np.concatenate([move_matrix(da, 0), move_matrix(0, db), move_matrix(da, db)], axis=0)
            )
    return jnp.asarray(np.stack(planes), jnp.bfloat16)


def pixel_order():
    m = np.zeros((4 * PATCH, 4 * PATCH), np.float32)
    for i in range(GRID_H):
        for j in range(GRID_W):
            for a in (0, 1):
                for b in (0, 1):
                    row = (2 * i + a) * 2 * GRID_W + 2 * j + b
                    m[row, (2 * a + b) * PATCH + i * GRID_W + j] = 1.0
    return jnp.asarray(m, jnp.bfloat16)


def latent_kernel(parts, width, frames, dt_ref, *refs):
    part_refs, refs = refs[:parts], refs[parts:]
    lat_ref, base_ref, move_ref, place_ref, next_ref, win_ref = refs
    total = part_refs[0][...].astype(jnp.float32)
    for r in part_refs[1:]:
        total = total + r[...].astype(jnp.float32)
    half = LAT // 2
    square = total[:, LAT : LAT + half] + total[:, LAT + half :]
    inverse = lax.rsqrt(square * np.float32(1.0 / width) + 1e-06)
    scaled = total[:, :LAT] * jnp.concatenate([inverse, inverse], axis=1)
    for f in range(frames):
        at = slice(f * PATCH, (f + 1) * PATCH)
        value = lat_ref[at] + dt_ref[f] * (scaled[at] + base_ref[f : f + 1])
        next_ref[at] = value
        spread = jnp.dot(
            value.astype(jnp.bfloat16), place_ref[...], preferred_element_type=jnp.float32
        ).astype(jnp.bfloat16)
        cols = 16 * LAT_C
        stacked = jnp.concatenate(
            [spread[:, o * cols : (o + 1) * cols] for o in range(len(OFFSETS))], axis=0
        )
        win_ref[at] = jnp.dot(
            move_ref[...], stacked, preferred_element_type=jnp.float32
        ).astype(jnp.bfloat16)


def step_latent(parts, latent_in, base, step_dt, width):
    rows = latent_in.shape[0]
    move, place = gather_constants()
    return pl.pallas_call(
        functools.partial(latent_kernel, len(parts), width, rows // PATCH),
        out_shape=[
            jax.ShapeDtypeStruct((rows, LAT), jnp.float32),
            jax.ShapeDtypeStruct((rows, 16 * LAT_C), jnp.bfloat16),
        ],
        in_specs=[SM] + [VM] * (len(parts) + 4),
        out_specs=[VM, VM],
        name="latent",
    )(step_dt, *parts, latent_in, base, move, place)


def decode_kernel(
    frames,
    lead_ref,
    far_ref,
    near_ref,
    own_ref,
    w1_ref,
    b1_ref,
    gain_ref,
    b2_ref,
    pg_ref,
    post_ref,
    text_ref,
    moves_ref,
    order_ref,
    w2_hbm,
    pw_hbm,
    proj_hbm,
    out_ref,
    sent_ref,
    w2_s,
    pw_s,
    proj_s,
    win_s,
    x_s,
    sem,
):
    taps = 9 * CH
    w2_copy = pltpu.make_async_copy(w2_hbm, w2_s, sem.at[0])
    pw_copy = pltpu.make_async_copy(pw_hbm, pw_s, sem.at[1])
    w2_copy.start()
    pw_copy.start()
    proj_copy = pltpu.make_async_copy(proj_hbm, proj_s, sem.at[2])
    proj_copy.start()
    rows = frames * PATCH
    for n, r in enumerate((far_ref, near_ref, own_ref)):
        win_s[n * rows : (n + 1) * rows] = r[...]
    wide = frames + 2
    skip = 3 * frames - wide - 2
    cols = 16 * LAT_C
    firsts = []
    for q in range(4):
        acc = jnp.zeros((wide * PATCH, CH), jnp.float32)
        for t in range(3):
            acc = acc + jnp.dot(
                win_s[(skip + t) * PATCH : (skip + t + wide) * PATCH],
                w1_ref[t * cols : (t + 1) * cols, q * CH : (q + 1) * CH],
                preferred_element_type=jnp.float32,
            )
        first = (acc + b1_ref[...]).astype(jnp.bfloat16).astype(jnp.float32)
        firsts.append(first[2 * PATCH :])
        mean = jnp.mean(first * first, axis=-1, keepdims=True)
        v = first * lax.rsqrt(mean + 1e-06) * gain_ref[...]
        act = v / (1.0 + jnp.exp(-v))
        row = lax.broadcasted_iota(jnp.int32, (wide * PATCH, 1), 0)
        act = jnp.where((row >= 2 * PATCH) | (lead_ref[0] == 0), act, 0.0).astype(jnp.bfloat16)
        a, b = q // 2, q % 2
        for f in range(wide):
            plane = act[f * PATCH : (f + 1) * PATCH]
            moved = jnp.dot(
                moves_ref[q], plane, preferred_element_type=jnp.float32
            ).astype(jnp.bfloat16)
            pieces = {
                (0, 0): plane,
                (1, 0): moved[:PATCH],
                (0, 1): moved[PATCH : 2 * PATCH],
                (1, 1): moved[2 * PATCH :],
            }
            for (ma, mb), piece in pieces.items():
                u = WINDOW.index(((1, -1)[a] if ma else 0, a))
                w = WINDOW.index(((1, -1)[b] if mb else 0, b))
                for oa in (0, 1):
                    for ob in (0, 1):
                        dy, dz = u - oa, w - ob
                        if 0 <= dy < 3 and 0 <= dz < 3:
                            at = (f * 4 + 2 * oa + ob) * PATCH
                            tap = (3 * dy + dz) * CH
                            x_s[at : at + PATCH, tap : tap + CH] = piece
    w2_copy.wait()
    block = 4 * PATCH
    out = jnp.zeros((frames * block, CH), jnp.float32)
    for t in range(3):
        out = out + jnp.dot(
            x_s[t * block : (t + frames) * block],
            w2_s[t * taps : (t + 1) * taps],
            preferred_element_type=jnp.float32,
        )
    first = jnp.concatenate(
        [firsts[q][f * PATCH : (f + 1) * PATCH] for f in range(frames) for q in range(4)], axis=0
    )
    dec = (out + b2_ref[...] + first).astype(jnp.bfloat16)
    for f in range(frames):
        out_ref[f * block : (f + 1) * block] = jnp.dot(
            order_ref[...], dec[f * block : (f + 1) * block], preferred_element_type=jnp.float32
        ).astype(jnp.bfloat16)
    pw_copy.wait()
    emb = jnp.zeros((rows, pw_s.shape[1]), jnp.float32)
    for q in range(4):
        lhs = jnp.concatenate(
            [dec[(f * 4 + q) * PATCH : (f * 4 + q + 1) * PATCH] for f in range(frames)], axis=0
        )
        emb = emb + jnp.dot(
            lhs, pw_s[q * CH : (q + 1) * CH], preferred_element_type=jnp.float32
        )
    emb = emb.astype(jnp.bfloat16).astype(jnp.float32)
    centered = emb - jnp.mean(emb, axis=-1, keepdims=True)
    variance = jnp.mean(centered * centered, axis=-1, keepdims=True)
    normed = centered * lax.rsqrt(variance + 1e-05) * pg_ref[...]
    pooled = jnp.concatenate(
        [
            jnp.mean(normed[f * PATCH : (f + 1) * PATCH], axis=0, keepdims=True)
            for f in range(frames)
        ],
        axis=0,
    )
    centered = pooled - jnp.mean(pooled, axis=-1, keepdims=True)
    variance = jnp.mean(centered * centered, axis=-1, keepdims=True)
    vec = centered * lax.rsqrt(variance + 1e-05) * post_ref[...]
    columns = jnp.transpose(
        jnp.concatenate([vec, jnp.zeros((8 - frames, vec.shape[1]), jnp.float32)], axis=0)
    )
    proj_copy.wait()
    for f in range(frames):
        row = jnp.sum(columns[:, f : f + 1] * proj_s[...], axis=0, keepdims=True)
        for n in range(sent_ref.shape[0]):
            sent_ref[n, f : f + 1, :] = row
    for n in range(sent_ref.shape[0]):
        sent_ref[n, frames : frames + 1, :] = text_ref[...]


def window_weight(weight):
    taps = weight.reshape(3, 3, 3, LAT_C, CH)
    grown = [
        jnp.pad(taps, ((0, 0), (a, 1 - a), (b, 1 - b), (0, 0), (0, 0))).reshape(-1, CH)
        for a in (0, 1)
        for b in (0, 1)
    ]
    return jnp.concatenate(grown, axis=1)


def decode(lead, far, near, own, w1, b1, gain, w2, b2, pw, patch_gain, post_gain, proj, text, devices):
    rows = own.shape[0]
    frames = rows // PATCH
    wide = frames + 2
    return pl.pallas_call(
        functools.partial(decode_kernel, frames),
        out_shape=[
            jax.ShapeDtypeStruct((frames * 4 * PATCH, CH), jnp.bfloat16),
            jax.ShapeDtypeStruct((devices, frames + 1, proj.shape[1]), jnp.float32),
        ],
        in_specs=[SM] + [VM] * 12 + [ANY, ANY, ANY],
        out_specs=[VM, VM],
        scratch_shapes=[
            pltpu.VMEM(w2.shape, jnp.bfloat16),
            pltpu.VMEM(pw.shape, jnp.bfloat16),
            pltpu.VMEM(proj.shape, jnp.float32),
            pltpu.VMEM((3 * rows, 16 * LAT_C), jnp.bfloat16),
            pltpu.VMEM((wide * 4 * PATCH, 9 * CH), jnp.bfloat16),
            pltpu.SemaphoreType.DMA((3,)),
        ],
        name="decode",
    )(
        lead,
        far,
        near,
        own,
        w1,
        b1,
        gain,
        b2,
        patch_gain,
        post_gain,
        text,
        plane_moves(),
        pixel_order(),
        w2,
        pw,
        proj,
    )


def rate_kernel(frames, slot_ref, got_ref, vec_ref, score_ref):
    text = jnp.sum(got_ref[:, frames, :], axis=0, keepdims=True)
    text_rms = jnp.sqrt(jnp.mean(text * text) + 1e-06)
    for f in range(frames):
        slot = slot_ref[f]
        block = got_ref[slot // frames]
        row = block[:1]
        for n in range(1, frames):
            row = jnp.where(slot % frames == n, block[n : n + 1], row)
        vec_ref[f : f + 1] = row
        inner = jnp.sum(row * text)
        image_rms = jnp.sqrt(jnp.mean(row * row) + 1e-06)
        score_ref[f] = 100.0 * inner / (TEXT_W * image_rms * text_rms)


def rate(slots, got):
    frames = slots.shape[0]
    return pl.pallas_call(
        functools.partial(rate_kernel, frames),
        out_shape=[
            jax.ShapeDtypeStruct((frames, got.shape[2]), jnp.float32),
            jax.ShapeDtypeStruct((frames,), jnp.float32),
        ],
        in_specs=[SM, VM],
        out_specs=[VM, SM],
        name="rate",
    )(slots, got)


def local(
    queries,
    keys,
    values,
    latent_in,
    mod_table,
    step_size,
    timestep,
    head_weight,
    conv_in_weight,
    conv_in_bias,
    norm_gain,
    conv_weight,
    conv_bias,
    patch_weight,
    patch_gain,
    post_gain,
    proj_weight,
    text_table,
    prompt_ids,
    frame_order,
):
    rows, width = queries.shape
    devices = lax.axis_size("seq")
    chips = devices // 2
    cols = width // chips
    heads = cols // HD
    frames = rows // PATCH
    me = lax.axis_index("seq")
    chip, core = me // 2, me % 2

    scale = lax.dynamic_slice_in_dim(mod_table[:, 1, :], chip * cols, cols, 1)
    scale = scale.reshape(-1, heads, 1, HD)
    weight = lax.dynamic_slice_in_dim(head_weight, chip * cols, cols, 0).reshape(heads, HD, LAT)
    weight = jnp.pad(weight, ((0, 0), (0, 0), (0, 128 - LAT)))
    origin = 2 * ((chip - jnp.arange(chips)) % chips) + core
    steps = jnp.take(timestep.reshape(devices, frames), origin, axis=0).reshape(-1)
    own_steps = lax.dynamic_slice_in_dim(timestep, me * frames, frames, 0)
    base = jnp.dot(jnp.take(mod_table[:, 0, :], own_steps, axis=0), head_weight, precision=highest)
    step_dt = jnp.take(step_size, own_steps)
    own_text = jnp.mean(jnp.take(text_table, prompt_ids, axis=0).astype(jnp.float32), axis=0)
    text_row = lax.dynamic_update_slice_in_dim(
        jnp.zeros((TEXT_W,), jnp.float32), own_text, me * own_text.shape[0], 0
    )
    slots = lax.dynamic_slice_in_dim(frame_order, me * frames, frames, 0)
    prepared = (
        scale,
        weight,
        steps,
        base,
        step_dt,
        text_row.reshape(1, -1),
        slots,
        window_weight(conv_in_weight),
        conv_in_bias.reshape(1, -1),
        norm_gain.reshape(1, -1),
        conv_bias.reshape(1, -1),
        patch_gain.reshape(1, -1),
        post_gain.reshape(1, -1),
        (me == 0).astype(jnp.int32).reshape(1),
        latent_in,
    )
    (
        scale,
        weight,
        steps,
        base,
        step_dt,
        text_row,
        slots,
        w1,
        b1,
        gain,
        b2,
        patch_gain,
        post_gain,
        lead,
        latent_in,
    ) = lax.optimization_barrier(prepared)

    tail = max(1, heads // 4)
    phases = (heads - tail, tail) if heads > tail else (tail,)
    order = sorted(range(1, chips), key=lambda t: abs(2 * t - chips))
    arrived, first, phase_blocks = None, 0, []
    for count in phases:
        starts = ((chip + jnp.arange(chips)) % chips) * cols + first * HD
        blocks = pack(keys, values, queries, starts.astype(jnp.int32), count * HD)
        got = [blocks[0]] * chips
        for turn in order:
            block = blocks[turn]
            if arrived is not None:
                block, _ = lax.optimization_barrier((block, arrived[turn]))
            got[turn] = rotate(block, "seq", turn)
        phase_blocks.append((first, count, got))
        arrived = got
        first += count
    sums = None
    for first, count, got in phase_blocks:
        if sums is not None:
            sums, *got = lax.optimization_barrier((sums, *got))
        sums = attend(
            got,
            [swap_core(block, "seq") for block in got],
            steps,
            scale[:, first : first + count],
            weight[first : first + count],
            sums,
            first + count == heads,
        )
    parts = [sums[0]] + [rotate(sums[t], "seq", chips - t) for t in order]

    latent_next, window = step_latent(parts, latent_in, base, step_dt, width)
    near = shifted(window, "seq", 1)
    far = shifted(window, "seq", 2)
    decoded, sent = decode(
        lead,
        far,
        near,
        window,
        w1,
        b1,
        gain,
        conv_weight.reshape(-1, CH),
        b2,
        patch_weight,
        patch_gain,
        post_gain,
        proj_weight,
        text_row,
        devices,
    )
    decoded = decoded.reshape(frames, 2 * GRID_H, 2 * GRID_W, CH)
    spread = lax.all_to_all(sent, "seq", split_axis=0, concat_axis=0, tiled=True)
    image_vec, scores = rate(slots, spread)
    return (latent_next, decoded, image_vec, scores)


def solution(mesh):
    in_specs = (
        P(("grp", "seq"), None),
        P(("grp", "seq"), None),
        P(("grp", "seq"), None),
        P(("grp", "seq"), None),
        P(),
        P(),
        P("grp"),
        P(),
        P(),
        P(),
        P(),
        P(),
        P(),
        P(),
        P(),
        P(),
        P(),
        P(None, "seq"),
        P("grp"),
        P("grp"),
    )
    out_specs = (
        P(("grp", "seq"), None),
        P(("grp", "seq"), None, None, None),
        P(("grp", "seq"), None),
        P(("grp", "seq")),
    )
    return jax.shard_map(local, mesh=mesh, in_specs=in_specs, out_specs=out_specs, check_vma=False)
```

```python
import functools

import jax
import jax.numpy as jnp
import numpy as np
from jax import lax
from jax.experimental import pallas as pl
from jax.experimental.pallas import tpu as pltpu
from jax.sharding import PartitionSpec as P

GRID_H = 8
GRID_W = 12
PATCH = GRID_H * GRID_W
HD = 128
LAT = 64
LAT_C = 16
CH = 384
TEXT_W = 768
KEY_CHUNK = 512


highest = lax.Precision.HIGHEST
VM = pl.BlockSpec(memory_space=pltpu.VMEM)
SM = pl.BlockSpec(memory_space=pltpu.SMEM)
ANY = pl.BlockSpec(memory_space=pl.ANY)


def shifted(value, axis, steps):
    count = lax.axis_size(axis)
    initial, last = (max(0, -steps), min(count, count - steps))
    return lax.ppermute(value, axis, [(source, source + steps) for source in range(initial, last)])


def rotate(value, axis, steps):
    count = lax.axis_size(axis)
    return lax.ppermute(value, axis, [(i, (i + 2 * steps) % count) for i in range(count)])


def swap_core(value, axis):
    count = lax.axis_size(axis)
    return lax.ppermute(value, axis, [(i, i ^ 1) for i in range(count)])


def pack_kernel(blocks, at_ref, k_hbm, v_hbm, q_hbm, *refs):
    out_refs, (buf, in_sem, out_sem) = refs[:blocks], refs[blocks:]
    width = buf.shape[3]
    gets = []
    for n in range(blocks):
        at = pl.multiple_of(at_ref[n], HD)
        gets.append(
            [
                pltpu.make_async_copy(src.at[:, pl.ds(at, width)], buf.at[n, i], in_sem.at[n, i])
                for i, src in enumerate((k_hbm, v_hbm, q_hbm))
            ]
        )
        for get in gets[-1]:
            get.start()
    puts = [
        pltpu.make_async_copy(buf.at[n], out_refs[n], out_sem.at[n]) for n in range(blocks)
    ]
    for n in range(blocks):
        for get in gets[n]:
            get.wait()
        puts[n].start()
    for put in puts:
        put.wait()


def pack(keys, values, queries, starts, width):
    rows, blocks = keys.shape[0], starts.shape[0]
    return pl.pallas_call(
        functools.partial(pack_kernel, blocks),
        out_shape=[jax.ShapeDtypeStruct((3, rows, width), jnp.bfloat16)] * blocks,
        in_specs=[SM, ANY, ANY, ANY],
        out_specs=[ANY] * blocks,
        scratch_shapes=[
            pltpu.VMEM((blocks, 3, rows, width), jnp.bfloat16),
            pltpu.SemaphoreType.DMA((blocks, 3)),
            pltpu.SemaphoreType.DMA((blocks,)),
        ],
        name="pack",
    )(starts, keys, values, queries)


def attend_kernel(blocks, heads, frames, resumed, last, t_ref, sc_ref, w_ref, *refs):
    if resumed:
        prev_ref, refs = refs[0], refs[1:]
    near_refs, far_refs, refs = refs[:blocks], refs[blocks : 2 * blocks], refs[2 * blocks :]
    if last:
        out_refs, refs = refs[:blocks], refs[blocks:]
    else:
        sum_ref, refs = refs[0], refs[1:]
    q_s, k_s, v_s, s_a, s_b, m_a, m_b, acc_s, tot_s, sem, q_sem = refs[:11]
    if last:
        sum_ref = refs[11]
    sources = near_refs + far_refs
    rows = near_refs[0].shape[1]
    keys = len(sources) * rows
    scale = np.float32(HD**-0.5 * np.log2(np.e))

    def fetch(h, which):
        dst = (k_s, v_s)[which]
        for j, src in enumerate(sources):
            pltpu.make_async_copy(
                src.at[which, :, pl.ds(h * HD, HD)],
                dst.at[h, pl.ds(j * rows, rows), :],
                sem.at[h, which],
            ).start()

    fetch(0, 0)
    for b in range(blocks):
        pltpu.make_async_copy(near_refs[b].at[2], q_s.at[b], q_sem).start()
    fetch(0, 1)
    for h in range(1, heads):
        fetch(h, 0)
        fetch(h, 1)
    if resumed:
        sum_ref[...] = prev_ref[...]
    else:
        sum_ref[...] = jnp.zeros(sum_ref.shape, jnp.float32)

    def arrived(h, which):
        whole = (k_s, v_s)[which].at[h]
        pltpu.make_async_copy(whole, whole, sem.at[h, which]).wait()

    def logits(h, b, at, s_ref, peak):
        q = q_s[b, :, pl.ds(pl.multiple_of(h * HD, HD), HD)]
        s = lax.dot_general(
            q,
            k_s[h, at : at + KEY_CHUNK, :],
            (((1,), (1,)), ((), ())),
            preferred_element_type=jnp.float32,
        )
        s_ref[:, at : at + KEY_CHUNK] = s
        folded = functools.reduce(
            jnp.maximum, [s[:, i : i + 128] for i in range(0, KEY_CHUNK, 128)]
        )
        return folded if peak is None else jnp.maximum(peak, folded)

    def keep_peak(peak, m_ref):
        m_ref[...] = jnp.broadcast_to(jnp.max(peak, axis=-1, keepdims=True) * scale, m_ref.shape)

    def finish(h, b, acc, total):
        o = acc / jnp.sum(total, axis=-1, keepdims=True)
        o = o.astype(jnp.bfloat16).astype(jnp.float32)
        square = jnp.sum(o * o, axis=-1, keepdims=True)
        per = rows // frames
        scaled = jnp.concatenate(
            [
                o[f * per : (f + 1) * per] * (1.0 + sc_ref[t_ref[b * frames + f], h])
                for f in range(frames)
            ],
            axis=0,
        )
        part = jnp.dot(scaled, w_ref[h], precision=highest, preferred_element_type=jnp.float32)
        lane = lax.broadcasted_iota(jnp.int32, part.shape, 1)
        return part + jnp.where(lane >= LAT, square, 0.0)

    def one_unit(h, now, top_ref, next_h, next_b, later, later_top_ref):
        top = top_ref[:, :1]
        peak, total = None, None
        acc = jnp.zeros((rows, HD), jnp.float32)
        for at in chunks:
            peak = logits(next_h, next_b, at, later, peak)
            e = jnp.exp2(now[:, at : at + KEY_CHUNK] * scale - top)
            folded = functools.reduce(jnp.add, [e[:, i : i + 128] for i in range(0, KEY_CHUNK, 128)])
            total = folded if total is None else total + folded
            acc = acc + jnp.dot(
                e.astype(jnp.bfloat16),
                v_s[h, at : at + KEY_CHUNK, :],
                preferred_element_type=jnp.float32,
            )
        keep_peak(peak, later_top_ref)
        return acc, total

    chunks = range(0, keys, KEY_CHUNK)
    pltpu.make_async_copy(q_s, q_s, q_sem).wait()
    arrived(0, 0)
    peak = None
    for at in chunks:
        peak = logits(0, 0, at, s_a, peak)
    keep_peak(peak, m_a)
    pairs = blocks // 2
    acc_s[...] = jnp.zeros(acc_s.shape, jnp.float32)
    tot_s[...] = jnp.ones(tot_s.shape, jnp.float32)

    def one_pair(n, carry):
        h, p = n // pairs, n % pairs
        after = jnp.minimum(n + 1, heads * pairs - 1)
        after_h, after_p = after // pairs, after % pairs
        before = jnp.maximum(n - 1, 0)
        before_h, before_p = before // pairs, before % pairs

        @pl.when(p == 0)
        def _():
            arrived(h, 1)

        @pl.when(after_h > h)
        def _():
            arrived(after_h, 0)

        late = finish(before_h, 2 * before_p + 1, acc_s[...], tot_s[...])
        sum_ref[2 * before_p + 1] = sum_ref[2 * before_p + 1] + late
        even = one_unit(h, s_a, m_a, h, 2 * p + 1, s_b, m_b)
        sum_ref[2 * p] = sum_ref[2 * p] + finish(h, 2 * p, *even)
        acc, total = one_unit(h, s_b, m_b, after_h, 2 * after_p, s_a, m_a)
        acc_s[...] = acc
        tot_s[...] = total
        return carry

    lax.fori_loop(0, heads * pairs, one_pair, 0)
    sum_ref[blocks - 1] = sum_ref[blocks - 1] + finish(
        heads - 1, blocks - 1, acc_s[...], tot_s[...]
    )
    if last:
        for b in range(blocks):
            share = sum_ref[b]
            high = share.astype(jnp.bfloat16)
            rest = (share - high.astype(jnp.float32)).astype(jnp.bfloat16)
            lane = lax.broadcasted_iota(jnp.int32, share.shape, 1)
            out_refs[b][...] = jnp.where(lane < 3 * LAT // 2, high, rest)


def attend(near, far, steps, scale, weight, previous, last):
    blocks = len(near)
    _, rows, cols = near[0].shape
    heads, keys = cols // HD, 2 * blocks * rows
    frames = rows // PATCH
    resumed = previous is not None
    sums = (blocks, rows, 128)
    if last:
        out_shape = [jax.ShapeDtypeStruct(sums[1:], jnp.bfloat16)] * blocks
        out_specs = [VM] * blocks
    else:
        out_shape, out_specs = jax.ShapeDtypeStruct(sums, jnp.float32), VM
    return pl.pallas_call(
        functools.partial(attend_kernel, blocks, heads, frames, resumed, last),
        out_shape=out_shape,
        in_specs=[SM, VM, VM] + [VM] * resumed + [ANY] * (2 * blocks),
        out_specs=out_specs,
        scratch_shapes=[
            pltpu.VMEM((blocks, rows, cols), jnp.bfloat16),
            pltpu.VMEM((heads, keys, HD), jnp.bfloat16),
            pltpu.VMEM((heads, keys, HD), jnp.bfloat16),
            pltpu.VMEM((rows, keys), jnp.float32),
            pltpu.VMEM((rows, keys), jnp.float32),
            pltpu.VMEM((rows, 128), jnp.float32),
            pltpu.VMEM((rows, 128), jnp.float32),
            pltpu.VMEM((rows, HD), jnp.float32),
            pltpu.VMEM((rows, 128), jnp.float32),
            pltpu.SemaphoreType.DMA((heads, 2)),
            pltpu.SemaphoreType.DMA,
        ]
        + [pltpu.VMEM(sums, jnp.float32)] * last,
        cost_estimate=pl.CostEstimate(
            flops=4 * blocks * rows * keys * cols,
            bytes_accessed=4 * keys * cols,
            transcendentals=blocks * rows * keys * heads,
        ),
        name="attend",
    )(steps, scale, weight, *([previous] if resumed else []), *near, *far)


WINDOW = ((-1, 1), (0, 0), (0, 1), (1, 0))


OFFSETS = [(di, dj) for di in (-1, 0, 1) for dj in (-1, 0, 1)]


def one_hot(index, count):
    hit = jnp.asarray(index, jnp.int32)[..., None] == jnp.arange(count, dtype=jnp.int32)
    return hit.astype(jnp.bfloat16)


def moved(di, dj):
    seen = np.full((GRID_H, GRID_W), -1)
    for i in range(GRID_H):
        for j in range(GRID_W):
            if 0 <= i + di < GRID_H and 0 <= j + dj < GRID_W:
                seen[i, j] = (i + di) * GRID_W + j + dj
    return seen.reshape(-1)


def gather_matrices():
    move = one_hot(np.stack([moved(di, dj) for di, dj in OFFSETS], axis=1), PATCH)
    place = np.full((len(OFFSETS), 4, 4, LAT_C), -1)
    for u, (di, a) in enumerate(WINDOW):
        for w, (dj, b) in enumerate(WINDOW):
            place[OFFSETS.index((di, dj)), u, w] = (2 * a + b) * LAT_C + np.arange(LAT_C)
    source = jnp.asarray(place.reshape(1, -1), jnp.int32)
    placed = (jnp.arange(LAT, dtype=jnp.int32)[:, None] == source).astype(jnp.bfloat16)
    return move.reshape(PATCH, -1), placed


def plane_moves():
    planes = []
    for a in (0, 1):
        for b in (0, 1):
            da, db = (1, -1)[a], (1, -1)[b]
            planes.append(np.concatenate([moved(da, 0), moved(0, db), moved(da, db)]))
    return one_hot(np.stack(planes), PATCH)


def pixel_order():
    index = np.zeros((GRID_H, 2, GRID_W, 2), np.int64)
    for a in (0, 1):
        for b in (0, 1):
            index[:, a, :, b] = (2 * a + b) * PATCH + np.arange(PATCH).reshape(GRID_H, GRID_W)
    return one_hot(index.reshape(-1), 4 * PATCH)


def latent_kernel(parts, width, frames, dt_ref, *refs):
    part_refs, refs = refs[:parts], refs[parts:]
    lat_ref, base_ref, move_ref, place_ref, next_ref, win_ref = refs
    total = part_refs[0][...].astype(jnp.float32)
    for r in part_refs[1:]:
        total = total + r[...].astype(jnp.float32)
    half = LAT // 2
    square = total[:, LAT : LAT + half] + total[:, LAT + half :]
    inverse = lax.rsqrt(square * np.float32(1.0 / width) + 1e-06)
    scaled = total[:, :LAT] * jnp.concatenate([inverse, inverse], axis=1)
    for f in range(frames):
        at = slice(f * PATCH, (f + 1) * PATCH)
        value = lat_ref[at] + dt_ref[f] * (scaled[at] + base_ref[f : f + 1])
        next_ref[at] = value
        spread = jnp.dot(
            value.astype(jnp.bfloat16), place_ref[...], preferred_element_type=jnp.float32
        ).astype(jnp.bfloat16)
        cols = 16 * LAT_C
        stacked = jnp.concatenate(
            [spread[:, o * cols : (o + 1) * cols] for o in range(len(OFFSETS))], axis=0
        )
        win_ref[at] = jnp.dot(
            move_ref[...], stacked, preferred_element_type=jnp.float32
        ).astype(jnp.bfloat16)


def step_latent(parts, latent_in, base, step_dt, width, move, place):
    rows = latent_in.shape[0]
    return pl.pallas_call(
        functools.partial(latent_kernel, len(parts), width, rows // PATCH),
        out_shape=[
            jax.ShapeDtypeStruct((rows, LAT), jnp.float32),
            jax.ShapeDtypeStruct((rows, 16 * LAT_C), jnp.bfloat16),
        ],
        in_specs=[SM] + [VM] * (len(parts) + 4),
        out_specs=[VM, VM],
        name="latent",
    )(step_dt, *parts, latent_in, base, move, place)


def decode_kernel(
    frames,
    lead_ref,
    far_ref,
    near_ref,
    own_ref,
    w1_ref,
    b1_ref,
    gain_ref,
    b2_ref,
    pg_ref,
    post_ref,
    text_ref,
    moves_ref,
    order_ref,
    w2_hbm,
    pw_hbm,
    proj_hbm,
    out_ref,
    sent_ref,
    w2_s,
    pw_s,
    proj_s,
    win_s,
    x_s,
    sem,
):
    taps = 9 * CH
    w2_copy = pltpu.make_async_copy(w2_hbm, w2_s, sem.at[0])
    pw_copy = pltpu.make_async_copy(pw_hbm, pw_s, sem.at[1])
    w2_copy.start()
    pw_copy.start()
    proj_copy = pltpu.make_async_copy(proj_hbm, proj_s, sem.at[2])
    proj_copy.start()
    rows = frames * PATCH
    for n, r in enumerate((far_ref, near_ref, own_ref)):
        win_s[n * rows : (n + 1) * rows] = r[...]
    wide = frames + 2
    skip = 3 * frames - wide - 2
    cols = 16 * LAT_C
    firsts = []
    for q in range(4):
        acc = jnp.zeros((wide * PATCH, CH), jnp.float32)
        for t in range(3):
            acc = acc + jnp.dot(
                win_s[(skip + t) * PATCH : (skip + t + wide) * PATCH],
                w1_ref[t * cols : (t + 1) * cols, q * CH : (q + 1) * CH],
                preferred_element_type=jnp.float32,
            )
        first = (acc + b1_ref[...]).astype(jnp.bfloat16).astype(jnp.float32)
        firsts.append(first[2 * PATCH :])
        mean = jnp.mean(first * first, axis=-1, keepdims=True)
        v = first * lax.rsqrt(mean + 1e-06) * gain_ref[...]
        act = v / (1.0 + jnp.exp(-v))
        row = lax.broadcasted_iota(jnp.int32, (wide * PATCH, 1), 0)
        act = jnp.where((row >= 2 * PATCH) | (lead_ref[0] == 0), act, 0.0).astype(jnp.bfloat16)
        a, b = q // 2, q % 2
        for f in range(wide):
            plane = act[f * PATCH : (f + 1) * PATCH]
            moved = jnp.dot(
                moves_ref[q], plane, preferred_element_type=jnp.float32
            ).astype(jnp.bfloat16)
            pieces = {
                (0, 0): plane,
                (1, 0): moved[:PATCH],
                (0, 1): moved[PATCH : 2 * PATCH],
                (1, 1): moved[2 * PATCH :],
            }
            for (ma, mb), piece in pieces.items():
                u = WINDOW.index(((1, -1)[a] if ma else 0, a))
                w = WINDOW.index(((1, -1)[b] if mb else 0, b))
                for oa in (0, 1):
                    for ob in (0, 1):
                        dy, dz = u - oa, w - ob
                        if 0 <= dy < 3 and 0 <= dz < 3:
                            at = (f * 4 + 2 * oa + ob) * PATCH
                            tap = (3 * dy + dz) * CH
                            x_s[at : at + PATCH, tap : tap + CH] = piece
    w2_copy.wait()
    block = 4 * PATCH
    out = jnp.zeros((frames * block, CH), jnp.float32)
    for t in range(3):
        out = out + jnp.dot(
            x_s[t * block : (t + frames) * block],
            w2_s[t * taps : (t + 1) * taps],
            preferred_element_type=jnp.float32,
        )
    first = jnp.concatenate(
        [firsts[q][f * PATCH : (f + 1) * PATCH] for f in range(frames) for q in range(4)], axis=0
    )
    dec = (out + b2_ref[...] + first).astype(jnp.bfloat16)
    for f in range(frames):
        out_ref[f * block : (f + 1) * block] = jnp.dot(
            order_ref[...], dec[f * block : (f + 1) * block], preferred_element_type=jnp.float32
        ).astype(jnp.bfloat16)
    pw_copy.wait()
    emb = jnp.zeros((rows, pw_s.shape[1]), jnp.float32)
    for q in range(4):
        lhs = jnp.concatenate(
            [dec[(f * 4 + q) * PATCH : (f * 4 + q + 1) * PATCH] for f in range(frames)], axis=0
        )
        emb = emb + jnp.dot(
            lhs, pw_s[q * CH : (q + 1) * CH], preferred_element_type=jnp.float32
        )
    emb = emb.astype(jnp.bfloat16).astype(jnp.float32)
    centered = emb - jnp.mean(emb, axis=-1, keepdims=True)
    variance = jnp.mean(centered * centered, axis=-1, keepdims=True)
    normed = centered * lax.rsqrt(variance + 1e-05) * pg_ref[...]
    pooled = jnp.concatenate(
        [
            jnp.mean(normed[f * PATCH : (f + 1) * PATCH], axis=0, keepdims=True)
            for f in range(frames)
        ],
        axis=0,
    )
    centered = pooled - jnp.mean(pooled, axis=-1, keepdims=True)
    variance = jnp.mean(centered * centered, axis=-1, keepdims=True)
    vec = centered * lax.rsqrt(variance + 1e-05) * post_ref[...]
    columns = jnp.transpose(
        jnp.concatenate([vec, jnp.zeros((8 - frames, vec.shape[1]), jnp.float32)], axis=0)
    )
    proj_copy.wait()
    for f in range(frames):
        row = jnp.sum(columns[:, f : f + 1] * proj_s[...], axis=0, keepdims=True)
        for n in range(sent_ref.shape[0]):
            sent_ref[n, f : f + 1, :] = row
    for n in range(sent_ref.shape[0]):
        sent_ref[n, frames : frames + 1, :] = text_ref[...]


def window_weight(weight):
    taps = weight.reshape(3, 3, 3, LAT_C, CH)
    grown = [
        jnp.pad(taps, ((0, 0), (a, 1 - a), (b, 1 - b), (0, 0), (0, 0))).reshape(-1, CH)
        for a in (0, 1)
        for b in (0, 1)
    ]
    return jnp.concatenate(grown, axis=1)


def decode(
    lead, far, near, own, w1, b1, gain, w2, b2, pw, patch_gain, post_gain, proj, text, moves, order, devices
):
    rows = own.shape[0]
    frames = rows // PATCH
    wide = frames + 2
    return pl.pallas_call(
        functools.partial(decode_kernel, frames),
        out_shape=[
            jax.ShapeDtypeStruct((frames * 4 * PATCH, CH), jnp.bfloat16),
            jax.ShapeDtypeStruct((devices, frames + 1, proj.shape[1]), jnp.float32),
        ],
        in_specs=[SM] + [VM] * 12 + [ANY, ANY, ANY],
        out_specs=[VM, VM],
        scratch_shapes=[
            pltpu.VMEM(w2.shape, jnp.bfloat16),
            pltpu.VMEM(pw.shape, jnp.bfloat16),
            pltpu.VMEM(proj.shape, jnp.float32),
            pltpu.VMEM((3 * rows, 16 * LAT_C), jnp.bfloat16),
            pltpu.VMEM((wide * 4 * PATCH, 9 * CH), jnp.bfloat16),
            pltpu.SemaphoreType.DMA((3,)),
        ],
        name="decode",
    )(
        lead,
        far,
        near,
        own,
        w1,
        b1,
        gain,
        b2,
        patch_gain,
        post_gain,
        text,
        moves,
        order,
        w2,
        pw,
        proj,
    )


def rate_kernel(frames, slot_ref, got_ref, vec_ref, score_ref):
    text = jnp.sum(got_ref[:, frames, :], axis=0, keepdims=True)
    text_rms = jnp.sqrt(jnp.mean(text * text) + 1e-06)
    for f in range(frames):
        slot = slot_ref[f]
        block = got_ref[slot // frames]
        row = block[:1]
        for n in range(1, frames):
            row = jnp.where(slot % frames == n, block[n : n + 1], row)
        vec_ref[f : f + 1] = row
        inner = jnp.sum(row * text)
        image_rms = jnp.sqrt(jnp.mean(row * row) + 1e-06)
        score_ref[f] = 100.0 * inner / (TEXT_W * image_rms * text_rms)


def rate(slots, got):
    frames = slots.shape[0]
    return pl.pallas_call(
        functools.partial(rate_kernel, frames),
        out_shape=[
            jax.ShapeDtypeStruct((frames, got.shape[2]), jnp.float32),
            jax.ShapeDtypeStruct((frames,), jnp.float32),
        ],
        in_specs=[SM, VM],
        out_specs=[VM, SM],
        name="rate",
    )(slots, got)


def local(
    queries,
    keys,
    values,
    latent_in,
    mod_table,
    step_size,
    timestep,
    head_weight,
    conv_in_weight,
    conv_in_bias,
    norm_gain,
    conv_weight,
    conv_bias,
    patch_weight,
    patch_gain,
    post_gain,
    proj_weight,
    text_table,
    prompt_ids,
    frame_order,
):
    rows, width = queries.shape
    devices = lax.axis_size("seq")
    chips = devices // 2
    cols = width // chips
    heads = cols // HD
    frames = rows // PATCH
    me = lax.axis_index("seq")
    chip, core = me // 2, me % 2

    tail = max(1, heads // 4)
    phases = tuple(n for n in (heads - 2 * tail, tail, tail) if n > 0) if heads > tail else (tail,)
    firsts = [sum(phases[:n]) for n in range(len(phases))]

    order = sorted(range(1, chips), key=lambda t: abs(2 * t - chips))

    def packed(first, count):
        at = ((chip + jnp.arange(chips)) % chips) * cols + first * HD
        return pack(keys, values, queries, at.astype(jnp.int32), count * HD)

    blocks = packed(firsts[0], phases[0])
    got = [blocks[0]] * chips
    got[order[0]] = rotate(blocks[order[0]], "seq", order[0])
    for turn in order[1:]:
        got[turn] = rotate(blocks[turn], "seq", turn)
    move, place = gather_matrices()
    scale = lax.dynamic_slice_in_dim(mod_table[:, 1, :], chip * cols, cols, 1)
    scale = scale.reshape(-1, heads, 1, HD)
    weight = lax.dynamic_slice_in_dim(head_weight, chip * cols, cols, 0).reshape(heads, HD, LAT)
    weight = jnp.pad(weight, ((0, 0), (0, 0), (0, 128 - LAT)))
    origin = 2 * ((chip - jnp.arange(chips)) % chips) + core
    steps = jnp.take(timestep.reshape(devices, frames), origin, axis=0).reshape(-1)
    own_steps = lax.dynamic_slice_in_dim(timestep, me * frames, frames, 0)
    base = jnp.dot(jnp.take(mod_table[:, 0, :], own_steps, axis=0), head_weight, precision=highest)
    step_dt = jnp.take(step_size, own_steps)
    own_text = jnp.mean(jnp.take(text_table, prompt_ids, axis=0).astype(jnp.float32), axis=0)
    text_row = lax.dynamic_update_slice_in_dim(
        jnp.zeros((TEXT_W,), jnp.float32), own_text, me * own_text.shape[0], 0
    )
    slots = lax.dynamic_slice_in_dim(frame_order, me * frames, frames, 0)
    prepared = dict(
        scales=[scale[:, f : f + n] for f, n in zip(firsts, phases)],
        weights=[weight[f : f + n] for f, n in zip(firsts, phases)],
        steps=steps,
        base=base,
        step_dt=step_dt,
        text=text_row.reshape(1, -1),
        slots=slots,
        w1=window_weight(conv_in_weight),
        b1=conv_in_bias.reshape(1, -1),
        gain=norm_gain.reshape(1, -1),
        b2=conv_bias.reshape(1, -1),
        patch_gain=patch_gain.reshape(1, -1),
        post_gain=post_gain.reshape(1, -1),
        lead=(me == 0).astype(jnp.int32).reshape(1),
        latent_in=latent_in,
        move=move,
        place=place,
        moves=plane_moves(),
        order=pixel_order(),
        later=[packed(f, n) for f, n in zip(firsts[1:], phases[1:])],
    )
    phase_blocks = [got]
    for blocks in prepared["later"]:
        got = [blocks[0]] * chips
        for turn in order:
            got[turn] = rotate(blocks[turn], "seq", turn)
        phase_blocks.append(got)
    sums = None
    for n, got in enumerate(phase_blocks):
        if sums is not None:
            sums, *got = lax.optimization_barrier((sums, *got))
        other = [swap_core(block, "seq") for block in got]
        sums = attend(
            got,
            other,
            prepared["steps"],
            prepared["scales"][n],
            prepared["weights"][n],
            sums,
            n + 1 == len(phase_blocks),
        )
    parts = [sums[0]] + [rotate(sums[t], "seq", chips - t) for t in order]

    latent_next, window = step_latent(
        parts,
        prepared["latent_in"],
        prepared["base"],
        prepared["step_dt"],
        width,
        prepared["move"],
        prepared["place"],
    )
    near = shifted(window, "seq", 1)
    far = shifted(window, "seq", 2)
    decoded, sent = decode(
        prepared["lead"],
        far,
        near,
        window,
        prepared["w1"],
        prepared["b1"],
        prepared["gain"],
        conv_weight.reshape(-1, CH),
        prepared["b2"],
        patch_weight,
        prepared["patch_gain"],
        prepared["post_gain"],
        proj_weight,
        prepared["text"],
        prepared["moves"],
        prepared["order"],
        devices,
    )
    decoded = decoded.reshape(frames, 2 * GRID_H, 2 * GRID_W, CH)
    spread = lax.all_to_all(sent, "seq", split_axis=0, concat_axis=0, tiled=True)
    image_vec, scores = rate(prepared["slots"], spread)
    return (latent_next, decoded, image_vec, scores)


def solution(mesh):
    in_specs = (
        P(("grp", "seq"), None),
        P(("grp", "seq"), None),
        P(("grp", "seq"), None),
        P(("grp", "seq"), None),
        P(),
        P(),
        P("grp"),
        P(),
        P(),
        P(),
        P(),
        P(),
        P(),
        P(),
        P(),
        P(),
        P(),
        P(None, "seq"),
        P("grp"),
        P("grp"),
    )
    out_specs = (
        P(("grp", "seq"), None),
        P(("grp", "seq"), None, None, None),
        P(("grp", "seq"), None),
        P(("grp", "seq")),
    )

    return jax.shard_map(local, mesh=mesh, in_specs=in_specs, out_specs=out_specs, check_vma=False)
```

```python
import functools

import jax
import jax.numpy as jnp
import numpy as np
from jax import lax
from jax.experimental import pallas as pl
from jax.experimental.pallas import tpu as pltpu
from jax.sharding import PartitionSpec as P

GRID_H = 8
GRID_W = 12
PATCH = GRID_H * GRID_W
HD = 128
LAT = 64
LAT_C = 16
CH = 384
TEXT_W = 768
KEY_CHUNK = 512


highest = lax.Precision.HIGHEST
VM = pl.BlockSpec(memory_space=pltpu.VMEM)
SM = pl.BlockSpec(memory_space=pltpu.SMEM)
ANY = pl.BlockSpec(memory_space=pl.ANY)


def shifted(value, axis, steps):
    count = lax.axis_size(axis)
    initial, last = (max(0, -steps), min(count, count - steps))
    return lax.ppermute(value, axis, [(source, source + steps) for source in range(initial, last)])


def rotate(value, axis, steps):
    count = lax.axis_size(axis)
    return lax.ppermute(value, axis, [(i, (i + 2 * steps) % count) for i in range(count)])


def swap_core(value, axis):
    count = lax.axis_size(axis)
    return lax.ppermute(value, axis, [(i, i ^ 1) for i in range(count)])


def pack_kernel(blocks, at_ref, k_hbm, v_hbm, q_hbm, *refs):
    out_refs, (buf, in_sem, out_sem) = refs[:blocks], refs[blocks:]
    width = buf.shape[3]
    gets = []
    for n in range(blocks):
        at = pl.multiple_of(at_ref[n], HD)
        gets.append(
            [
                pltpu.make_async_copy(src.at[:, pl.ds(at, width)], buf.at[n, i], in_sem.at[n, i])
                for i, src in enumerate((k_hbm, v_hbm, q_hbm))
            ]
        )
        for get in gets[-1]:
            get.start()
    puts = [
        pltpu.make_async_copy(buf.at[n], out_refs[n], out_sem.at[n]) for n in range(blocks)
    ]
    for n in range(blocks):
        for get in gets[n]:
            get.wait()
        puts[n].start()
    for put in puts:
        put.wait()


def pack(keys, values, queries, starts, width):
    rows, blocks = keys.shape[0], starts.shape[0]
    return pl.pallas_call(
        functools.partial(pack_kernel, blocks),
        out_shape=[jax.ShapeDtypeStruct((3, rows, width), jnp.bfloat16)] * blocks,
        in_specs=[SM, ANY, ANY, ANY],
        out_specs=[ANY] * blocks,
        scratch_shapes=[
            pltpu.VMEM((blocks, 3, rows, width), jnp.bfloat16),
            pltpu.SemaphoreType.DMA((blocks, 3)),
            pltpu.SemaphoreType.DMA((blocks,)),
        ],
        name="pack",
    )(starts, keys, values, queries)


def attend_kernel(blocks, heads, frames, earlier, last, t_ref, sc_ref, w_ref, *refs):
    prev_refs, refs = refs[:earlier], refs[earlier:]
    near_refs, far_refs, refs = refs[:blocks], refs[blocks : 2 * blocks], refs[2 * blocks :]
    if last:
        out_refs, refs = refs[:blocks], refs[blocks:]
    else:
        sum_ref, refs = refs[0], refs[1:]
    q_s, k_s, v_s, s_a, s_b, m_a, m_b, acc_s, tot_s, sem, q_sem = refs[:11]
    if last:
        sum_ref, prev_s, prev_sem = refs[11:]
    sources = near_refs + far_refs
    rows = near_refs[0].shape[1]
    keys = len(sources) * rows
    scale = np.float32(HD**-0.5 * np.log2(np.e))

    def fetch(h, which):
        dst = (k_s, v_s)[which]
        for j, src in enumerate(sources):
            pltpu.make_async_copy(
                src.at[which, :, pl.ds(h * HD, HD)],
                dst.at[h, pl.ds(j * rows, rows), :],
                sem.at[h, which],
            ).start()

    fetch(0, 0)
    for b in range(blocks):
        pltpu.make_async_copy(near_refs[b].at[2], q_s.at[b], q_sem).start()
    fetch(0, 1)
    for h in range(1, heads):
        fetch(h, 0)
        fetch(h, 1)
    gets = []
    for n, prev in enumerate(prev_refs):
        gets.append(pltpu.make_async_copy(prev, prev_s.at[n], prev_sem.at[n]))
        gets[-1].start()
    sum_ref[...] = jnp.zeros(sum_ref.shape, jnp.float32)

    def arrived(h, which):
        whole = (k_s, v_s)[which].at[h]
        pltpu.make_async_copy(whole, whole, sem.at[h, which]).wait()

    def logits(h, b, at, s_ref, peak):
        q = q_s[b, :, pl.ds(pl.multiple_of(h * HD, HD), HD)]
        s = lax.dot_general(
            q,
            k_s[h, at : at + KEY_CHUNK, :],
            (((1,), (1,)), ((), ())),
            preferred_element_type=jnp.float32,
        )
        s_ref[:, at : at + KEY_CHUNK] = s
        folded = functools.reduce(
            jnp.maximum, [s[:, i : i + 128] for i in range(0, KEY_CHUNK, 128)]
        )
        return folded if peak is None else jnp.maximum(peak, folded)

    def keep_peak(peak, m_ref):
        m_ref[...] = jnp.broadcast_to(jnp.max(peak, axis=-1, keepdims=True) * scale, m_ref.shape)

    def finish(h, b, acc, total):
        o = acc / jnp.sum(total, axis=-1, keepdims=True)
        o = o.astype(jnp.bfloat16).astype(jnp.float32)
        square = jnp.sum(o * o, axis=-1, keepdims=True)
        per = rows // frames
        scaled = jnp.concatenate(
            [
                o[f * per : (f + 1) * per] * (1.0 + sc_ref[t_ref[b * frames + f], h])
                for f in range(frames)
            ],
            axis=0,
        )
        part = jnp.dot(scaled, w_ref[h], precision=highest, preferred_element_type=jnp.float32)
        lane = lax.broadcasted_iota(jnp.int32, part.shape, 1)
        return part + jnp.where(lane >= LAT, square, 0.0)

    def one_unit(h, now, top_ref, next_h, next_b, later, later_top_ref):
        top = top_ref[:, :1]
        peak, total = None, None
        acc = jnp.zeros((rows, HD), jnp.float32)
        for at in chunks:
            peak = logits(next_h, next_b, at, later, peak)
            e = jnp.exp2(now[:, at : at + KEY_CHUNK] * scale - top)
            folded = functools.reduce(jnp.add, [e[:, i : i + 128] for i in range(0, KEY_CHUNK, 128)])
            total = folded if total is None else total + folded
            acc = acc + jnp.dot(
                e.astype(jnp.bfloat16),
                v_s[h, at : at + KEY_CHUNK, :],
                preferred_element_type=jnp.float32,
            )
        keep_peak(peak, later_top_ref)
        return acc, total

    chunks = range(0, keys, KEY_CHUNK)
    pltpu.make_async_copy(q_s, q_s, q_sem).wait()
    arrived(0, 0)
    peak = None
    for at in chunks:
        peak = logits(0, 0, at, s_a, peak)
    keep_peak(peak, m_a)
    pairs = blocks // 2
    acc_s[...] = jnp.zeros(acc_s.shape, jnp.float32)
    tot_s[...] = jnp.ones(tot_s.shape, jnp.float32)

    def one_pair(n, carry):
        h, p = n // pairs, n % pairs
        after = jnp.minimum(n + 1, heads * pairs - 1)
        after_h, after_p = after // pairs, after % pairs
        before = jnp.maximum(n - 1, 0)
        before_h, before_p = before // pairs, before % pairs

        @pl.when(p == 0)
        def _():
            arrived(h, 1)

        @pl.when(after_h > h)
        def _():
            arrived(after_h, 0)

        late = finish(before_h, 2 * before_p + 1, acc_s[...], tot_s[...])
        sum_ref[2 * before_p + 1] = sum_ref[2 * before_p + 1] + late
        even = one_unit(h, s_a, m_a, h, 2 * p + 1, s_b, m_b)
        sum_ref[2 * p] = sum_ref[2 * p] + finish(h, 2 * p, *even)
        acc, total = one_unit(h, s_b, m_b, after_h, 2 * after_p, s_a, m_a)
        acc_s[...] = acc
        tot_s[...] = total
        return carry

    lax.fori_loop(0, heads * pairs, one_pair, 0)
    sum_ref[blocks - 1] = sum_ref[blocks - 1] + finish(
        heads - 1, blocks - 1, acc_s[...], tot_s[...]
    )
    if last:
        for get in gets:
            get.wait()
        row, lane = grid_iota(8, 128)
        pick = jnp.where(lane == LAT, 1.0, 0.0)
        for b in range(blocks):
            share = sum_ref[b]
            for n in range(earlier):
                share = share + prev_s[n, b]
            out_refs[b][:PATCH] = jnp.concatenate(
                [share[f * PATCH : (f + 1) * PATCH, :LAT] for f in range(frames)], axis=1
            ).astype(jnp.bfloat16)
            for f in range(frames):
                square = lax.dot_general(
                    pick,
                    share[f * PATCH : (f + 1) * PATCH],
                    (((1,), (1,)), ((), ())),
                    precision=highest,
                    preferred_element_type=jnp.float32,
                )
                square = jnp.concatenate(
                    [square, jnp.zeros((8, 128 - PATCH), jnp.float32)], axis=1
                )
                high = square.astype(jnp.bfloat16).astype(jnp.float32)
                both = jnp.where(row == 0, high, jnp.where(row == 1, square - high, 0.0))
                out_refs[b][PATCH + 8 * f : PATCH + 8 * (f + 1)] = both.astype(jnp.bfloat16)


def attend(near, far, steps, scale, weight, earlier, last):
    blocks = len(near)
    _, rows, cols = near[0].shape
    heads, keys = cols // HD, 2 * blocks * rows
    frames = rows // PATCH
    sums = (blocks, rows, 128)
    if last:
        share = (PATCH + 8 * frames, frames * LAT)
        out_shape = [jax.ShapeDtypeStruct(share, jnp.bfloat16)] * blocks
        out_specs = [VM] * blocks
    else:
        out_shape, out_specs = jax.ShapeDtypeStruct(sums, jnp.float32), VM
    return pl.pallas_call(
        functools.partial(attend_kernel, blocks, heads, frames, len(earlier), last),
        out_shape=out_shape,
        in_specs=[SM, VM, VM] + [ANY] * (len(earlier) + 2 * blocks),
        out_specs=out_specs,
        scratch_shapes=[
            pltpu.VMEM((blocks, rows, cols), jnp.bfloat16),
            pltpu.VMEM((heads, keys, HD), jnp.bfloat16),
            pltpu.VMEM((heads, keys, HD), jnp.bfloat16),
            pltpu.VMEM((rows, keys), jnp.float32),
            pltpu.VMEM((rows, keys), jnp.float32),
            pltpu.VMEM((rows, 128), jnp.float32),
            pltpu.VMEM((rows, 128), jnp.float32),
            pltpu.VMEM((rows, HD), jnp.float32),
            pltpu.VMEM((rows, 128), jnp.float32),
            pltpu.SemaphoreType.DMA((heads, 2)),
            pltpu.SemaphoreType.DMA,
        ]
        + [
            pltpu.VMEM(sums, jnp.float32),
            pltpu.VMEM((max(1, len(earlier)),) + sums, jnp.float32),
            pltpu.SemaphoreType.DMA((max(1, len(earlier)),)),
        ]
        * last,
        cost_estimate=pl.CostEstimate(
            flops=4 * blocks * rows * keys * cols,
            bytes_accessed=4 * keys * cols,
            transcendentals=blocks * rows * keys * heads,
        ),
        name="attend",
    )(steps, scale, weight, *earlier, *near, *far)


WINDOW = ((-1, 1), (0, 0), (0, 1), (1, 0))


OFFSETS = [(di, dj) for di in (-1, 0, 1) for dj in (-1, 0, 1)]


def grid_iota(rows, cols):
    shape = (rows, cols)
    return lax.broadcasted_iota(jnp.int32, shape, 0), lax.broadcasted_iota(jnp.int32, shape, 1)


def over(value, count):
    return jnp.floor((value.astype(jnp.float32) + 0.5) * np.float32(1.0 / count)).astype(jnp.int32)


def as_matrix(hit):
    return jnp.where(hit, 1.0, 0.0).astype(jnp.bfloat16)


def move_matrix(di, dj, cols=PATCH):
    row, col = grid_iota(PATCH, cols)
    j = row - GRID_W * over(row, GRID_W)
    inside = (j + dj >= 0) & (j + dj < GRID_W) & (col < PATCH)
    return as_matrix((col - row == GRID_W * di + dj) & inside)


def place_matrix(di, dj):
    row, col = grid_iota(LAT, 16 * LAT_C)
    u, w, c = col >> 6, (col >> 4) & 3, col & 15
    source = 2 * LAT_C * (1 - (u & 1)) + LAT_C * (1 - (w & 1)) + c

    def seen(at, step):
        return {-1: at == 0, 0: (at == 1) | (at == 2), 1: at == 3}[step]

    return as_matrix((row == source) & seen(u, di) & seen(w, dj))


def order_matrix():
    row, col = grid_iota(4 * PATCH, 4 * PATCH)
    y = over(row, 2 * GRID_W)
    z = row - 2 * GRID_W * y
    source = (2 * (y & 1) + (z & 1)) * PATCH + (y >> 1) * GRID_W + (z >> 1)
    return as_matrix(col == source)


def latent_kernel(parts, width, frames, dt_ref, *refs):
    part_refs, refs = refs[:parts], refs[parts:]
    lat_ref, base_ref, next_ref, win_ref = refs
    total = part_refs[0][...].astype(jnp.float32)
    for r in part_refs[1:]:
        total = total + r[...].astype(jnp.float32)
    row, _ = grid_iota(8, 128)
    pick = jnp.where(row < 2, 1.0, 0.0)
    cols = 16 * LAT_C
    moves = jnp.concatenate([move_matrix(di, dj, 128) for di, dj in OFFSETS], axis=1)
    places = jnp.concatenate([place_matrix(di, dj) for di, dj in OFFSETS], axis=1)
    none = jnp.zeros((128 - PATCH, cols), jnp.bfloat16)
    for f in range(frames):
        at = slice(f * PATCH, (f + 1) * PATCH)
        squares = total[PATCH + 8 * f : PATCH + 8 * (f + 1)]
        square = lax.dot_general(
            squares,
            pick,
            (((0,), (0,)), ((), ())),
            precision=highest,
            preferred_element_type=jnp.float32,
        )[:PATCH, :LAT]
        inverse = lax.rsqrt(square * np.float32(1.0 / width) + 1e-06)
        scaled = total[:PATCH, f * LAT : (f + 1) * LAT] * inverse
        value = lat_ref[at] + dt_ref[f] * (scaled + base_ref[f : f + 1])
        next_ref[at] = value
        spread = jnp.dot(
            value.astype(jnp.bfloat16), places, preferred_element_type=jnp.float32
        ).astype(jnp.bfloat16)
        stacked = jnp.concatenate(
            [x for o in range(len(OFFSETS)) for x in (spread[:, o * cols : (o + 1) * cols], none)],
            axis=0,
        )
        win_ref[at] = jnp.dot(moves, stacked, preferred_element_type=jnp.float32).astype(
            jnp.bfloat16
        )


def step_latent(parts, latent_in, base, step_dt, width):
    rows = latent_in.shape[0]
    return pl.pallas_call(
        functools.partial(latent_kernel, len(parts), width, rows // PATCH),
        out_shape=[
            jax.ShapeDtypeStruct((rows, LAT), jnp.float32),
            jax.ShapeDtypeStruct((rows, 16 * LAT_C), jnp.bfloat16),
        ],
        in_specs=[SM] + [VM] * (len(parts) + 2),
        out_specs=[VM, VM],
        name="latent",
    )(step_dt, *parts, latent_in, base)


def text_kernel(at_ref, id_ref, table_hbm, out_ref, buf, sem):
    count = id_ref.shape[0]

    def block(n):
        start = pl.multiple_of((id_ref[n] // 128) * 128, 128)
        return pltpu.make_async_copy(table_hbm.at[:, pl.ds(start, 128)], buf.at[n], sem)

    def fetch(n, carry):
        block(n).start()
        return carry

    lax.fori_loop(0, count, fetch, 0)
    pltpu.make_async_copy(buf, buf, sem).wait()
    width = buf.shape[1]
    _, lane = grid_iota(width, 128)

    def add(n, acc):
        return acc + jnp.where(lane == id_ref[n] % 128, buf[n].astype(jnp.float32), 0.0)

    acc = lax.fori_loop(0, count, add, jnp.zeros((width, 128), jnp.float32))
    own = lax.dot_general(
        jnp.ones((8, 128), jnp.float32),
        acc,
        (((1,), (1,)), ((), ())),
        precision=highest,
        preferred_element_type=jnp.float32,
    )
    row, col = grid_iota(width, out_ref.shape[1])
    spot = jnp.where(col == row + at_ref[0], 1.0, 0.0)
    placed = jnp.dot(own, spot, precision=highest, preferred_element_type=jnp.float32)
    out_ref[...] = placed[:1] * np.float32(1.0 / count)


def text_mean(at, ids, table):
    width = table.shape[0]
    return pl.pallas_call(
        text_kernel,
        out_shape=jax.ShapeDtypeStruct((1, TEXT_W), jnp.float32),
        in_specs=[SM, SM, ANY],
        out_specs=VM,
        scratch_shapes=[
            pltpu.VMEM((ids.shape[0], width, 128), jnp.bfloat16),
            pltpu.SemaphoreType.DMA,
        ],
        name="text",
    )(at, ids, table)


def decode_kernel(
    frames,
    lead_ref,
    far_ref,
    near_ref,
    own_ref,
    w1_ref,
    b1_ref,
    gain_ref,
    b2_ref,
    pg_ref,
    post_ref,
    text_ref,
    w2_hbm,
    pw_hbm,
    proj_hbm,
    out_ref,
    sent_ref,
    w2_s,
    pw_s,
    proj_s,
    win_s,
    x_s,
    sem,
):
    taps = 9 * CH
    w2_copy = pltpu.make_async_copy(w2_hbm, w2_s, sem.at[0])
    pw_copy = pltpu.make_async_copy(pw_hbm, pw_s, sem.at[1])
    w2_copy.start()
    pw_copy.start()
    proj_copy = pltpu.make_async_copy(proj_hbm, proj_s, sem.at[2])
    proj_copy.start()
    rows = frames * PATCH
    for n, r in enumerate((far_ref, near_ref, own_ref)):
        win_s[n * rows : (n + 1) * rows] = r[...]
    wide = frames + 2
    skip = 3 * frames - wide - 2
    cols = 16 * LAT_C
    firsts = []
    for q in range(4):
        acc = jnp.zeros((wide * PATCH, CH), jnp.float32)
        for t in range(3):
            acc = acc + jnp.dot(
                win_s[(skip + t) * PATCH : (skip + t + wide) * PATCH],
                w1_ref[t * cols : (t + 1) * cols, q * CH : (q + 1) * CH],
                preferred_element_type=jnp.float32,
            )
        first = (acc + b1_ref[...]).astype(jnp.bfloat16).astype(jnp.float32)
        firsts.append(first[2 * PATCH :])
        mean = jnp.mean(first * first, axis=-1, keepdims=True)
        v = first * lax.rsqrt(mean + 1e-06) * gain_ref[...]
        act = v / (1.0 + jnp.exp(-v))
        row = lax.broadcasted_iota(jnp.int32, (wide * PATCH, 1), 0)
        act = jnp.where((row >= 2 * PATCH) | (lead_ref[0] == 0), act, 0.0).astype(jnp.bfloat16)
        a, b = q // 2, q % 2
        da, db = (1, -1)[a], (1, -1)[b]
        moves = jnp.concatenate(
            [move_matrix(da, 0), move_matrix(0, db), move_matrix(da, db)], axis=0
        )
        for f in range(wide):
            plane = act[f * PATCH : (f + 1) * PATCH]
            moved = jnp.dot(
                moves, plane, preferred_element_type=jnp.float32
            ).astype(jnp.bfloat16)
            pieces = {
                (0, 0): plane,
                (1, 0): moved[:PATCH],
                (0, 1): moved[PATCH : 2 * PATCH],
                (1, 1): moved[2 * PATCH :],
            }
            for (ma, mb), piece in pieces.items():
                u = WINDOW.index(((1, -1)[a] if ma else 0, a))
                w = WINDOW.index(((1, -1)[b] if mb else 0, b))
                for oa in (0, 1):
                    for ob in (0, 1):
                        dy, dz = u - oa, w - ob
                        if 0 <= dy < 3 and 0 <= dz < 3:
                            at = (f * 4 + 2 * oa + ob) * PATCH
                            tap = (3 * dy + dz) * CH
                            x_s[at : at + PATCH, tap : tap + CH] = piece
    w2_copy.wait()
    block = 4 * PATCH
    out = jnp.zeros((frames * block, CH), jnp.float32)
    for t in range(3):
        out = out + jnp.dot(
            x_s[t * block : (t + frames) * block],
            w2_s[t * taps : (t + 1) * taps],
            preferred_element_type=jnp.float32,
        )
    first = jnp.concatenate(
        [firsts[q][f * PATCH : (f + 1) * PATCH] for f in range(frames) for q in range(4)], axis=0
    )
    dec = (out + b2_ref[...] + first).astype(jnp.bfloat16)
    order = order_matrix()
    for f in range(frames):
        out_ref[f * block : (f + 1) * block] = jnp.dot(
            order, dec[f * block : (f + 1) * block], preferred_element_type=jnp.float32
        ).astype(jnp.bfloat16)
    pw_copy.wait()
    emb = jnp.zeros((rows, pw_s.shape[1]), jnp.float32)
    for q in range(4):
        lhs = jnp.concatenate(
            [dec[(f * 4 + q) * PATCH : (f * 4 + q + 1) * PATCH] for f in range(frames)], axis=0
        )
        emb = emb + jnp.dot(
            lhs, pw_s[q * CH : (q + 1) * CH], preferred_element_type=jnp.float32
        )
    emb = emb.astype(jnp.bfloat16).astype(jnp.float32)
    centered = emb - jnp.mean(emb, axis=-1, keepdims=True)
    variance = jnp.mean(centered * centered, axis=-1, keepdims=True)
    normed = centered * lax.rsqrt(variance + 1e-05) * pg_ref[...]
    pooled = jnp.concatenate(
        [
            jnp.mean(normed[f * PATCH : (f + 1) * PATCH], axis=0, keepdims=True)
            for f in range(frames)
        ],
        axis=0,
    )
    centered = pooled - jnp.mean(pooled, axis=-1, keepdims=True)
    variance = jnp.mean(centered * centered, axis=-1, keepdims=True)
    vec = centered * lax.rsqrt(variance + 1e-05) * post_ref[...]
    columns = jnp.transpose(
        jnp.concatenate([vec, jnp.zeros((8 - frames, vec.shape[1]), jnp.float32)], axis=0)
    )
    proj_copy.wait()
    for f in range(frames):
        row = jnp.sum(columns[:, f : f + 1] * proj_s[...], axis=0, keepdims=True)
        for n in range(sent_ref.shape[0]):
            sent_ref[n, f : f + 1, :] = row
    for n in range(sent_ref.shape[0]):
        sent_ref[n, frames : frames + 1, :] = text_ref[...]


def window_weight(weight):
    taps = weight.reshape(3, 3, 3, LAT_C, CH)
    grown = [
        jnp.pad(taps, ((0, 0), (a, 1 - a), (b, 1 - b), (0, 0), (0, 0))).reshape(-1, CH)
        for a in (0, 1)
        for b in (0, 1)
    ]
    return jnp.concatenate(grown, axis=1)


def decode(
    lead, far, near, own, w1, b1, gain, w2, b2, pw, patch_gain, post_gain, proj, text, devices
):
    rows = own.shape[0]
    frames = rows // PATCH
    wide = frames + 2
    return pl.pallas_call(
        functools.partial(decode_kernel, frames),
        out_shape=[
            jax.ShapeDtypeStruct((frames * 4 * PATCH, CH), jnp.bfloat16),
            jax.ShapeDtypeStruct((devices, frames + 1, proj.shape[1]), jnp.float32),
        ],
        in_specs=[SM] + [VM] * 10 + [ANY, ANY, ANY],
        out_specs=[VM, VM],
        scratch_shapes=[
            pltpu.VMEM(w2.shape, jnp.bfloat16),
            pltpu.VMEM(pw.shape, jnp.bfloat16),
            pltpu.VMEM(proj.shape, jnp.float32),
            pltpu.VMEM((3 * rows, 16 * LAT_C), jnp.bfloat16),
            pltpu.VMEM((wide * 4 * PATCH, 9 * CH), jnp.bfloat16),
            pltpu.SemaphoreType.DMA((3,)),
        ],
        name="decode",
    )(
        lead,
        far,
        near,
        own,
        w1,
        b1,
        gain,
        b2,
        patch_gain,
        post_gain,
        text,
        w2,
        pw,
        proj,
    )


def rate_kernel(frames, slot_ref, got_ref, vec_ref, score_ref):
    text = jnp.sum(got_ref[:, frames, :], axis=0, keepdims=True)
    text_rms = jnp.sqrt(jnp.mean(text * text) + 1e-06)
    for f in range(frames):
        slot = slot_ref[f]
        block = got_ref[slot // frames]
        row = block[:1]
        for n in range(1, frames):
            row = jnp.where(slot % frames == n, block[n : n + 1], row)
        vec_ref[f : f + 1] = row
        inner = jnp.sum(row * text)
        image_rms = jnp.sqrt(jnp.mean(row * row) + 1e-06)
        score_ref[f] = 100.0 * inner / (TEXT_W * image_rms * text_rms)


def rate(slots, got):
    frames = slots.shape[0]
    return pl.pallas_call(
        functools.partial(rate_kernel, frames),
        out_shape=[
            jax.ShapeDtypeStruct((frames, got.shape[2]), jnp.float32),
            jax.ShapeDtypeStruct((frames,), jnp.float32),
        ],
        in_specs=[SM, VM],
        out_specs=[VM, SM],
        name="rate",
    )(slots, got)


def local(
    queries,
    keys,
    values,
    latent_in,
    mod_table,
    step_size,
    timestep,
    head_weight,
    conv_in_weight,
    conv_in_bias,
    norm_gain,
    conv_weight,
    conv_bias,
    patch_weight,
    patch_gain,
    post_gain,
    proj_weight,
    text_table,
    prompt_ids,
    frame_order,
):
    rows, width = queries.shape
    devices = lax.axis_size("seq")
    chips = devices // 2
    cols = width // chips
    heads = cols // HD
    frames = rows // PATCH
    me = lax.axis_index("seq")
    chip, core = me // 2, me % 2

    tail = max(1, heads // 4)
    phases = tuple(n for n in (heads - 2 * tail, tail, tail) if n > 0) if heads > tail else (tail,)
    firsts = [sum(phases[:n]) for n in range(len(phases))]

    order = sorted(range(1, chips), key=lambda t: abs(2 * t - chips))

    def packed(first, count):
        at = ((chip + jnp.arange(chips)) % chips) * cols + first * HD
        return pack(keys, values, queries, at.astype(jnp.int32), count * HD)

    blocks = packed(firsts[0], phases[0])
    got = [blocks[0]] * chips
    got[order[0]] = rotate(blocks[order[0]], "seq", order[0])
    for turn in order[1:]:
        got[turn] = rotate(blocks[turn], "seq", turn)
    scale = lax.dynamic_slice_in_dim(mod_table[:, 1, :], chip * cols, cols, 1)
    scale = scale.reshape(-1, heads, 1, HD)
    weight = lax.dynamic_slice_in_dim(head_weight, chip * cols, cols, 0).reshape(heads, HD, LAT)
    weight = jnp.pad(weight, ((0, 0), (0, 0), (0, 128 - LAT)))
    origin = 2 * ((chip - jnp.arange(chips)) % chips) + core
    steps = jnp.take(timestep.reshape(devices, frames), origin, axis=0).reshape(-1)
    own_steps = lax.dynamic_slice_in_dim(timestep, me * frames, frames, 0)
    base = jnp.dot(jnp.take(mod_table[:, 0, :], own_steps, axis=0), head_weight, precision=highest)
    step_dt = jnp.take(step_size, own_steps)
    text_row = text_mean(
        (me * text_table.shape[1]).astype(jnp.int32).reshape(1), prompt_ids, text_table.T
    )
    slots = lax.dynamic_slice_in_dim(frame_order, me * frames, frames, 0)
    prepared = dict(
        scales=[scale[:, f : f + n] for f, n in zip(firsts, phases)],
        weights=[weight[f : f + n] for f, n in zip(firsts, phases)],
        steps=steps,
        base=base,
        step_dt=step_dt,
        text=text_row,
        slots=slots,
        w1=window_weight(conv_in_weight),
        b1=conv_in_bias.reshape(1, -1),
        gain=norm_gain.reshape(1, -1),
        b2=conv_bias.reshape(1, -1),
        patch_gain=patch_gain.reshape(1, -1),
        post_gain=post_gain.reshape(1, -1),
        lead=(me == 0).astype(jnp.int32).reshape(1),
        latent_in=latent_in,
        later=[packed(f, n) for f, n in zip(firsts[1:], phases[1:])],
    )
    phase_blocks = [got]
    for blocks in prepared["later"]:
        got = [blocks[0]] * chips
        for turn in order:
            got[turn] = rotate(blocks[turn], "seq", turn)
        phase_blocks.append(got)
    sums = []
    for n, got in enumerate(phase_blocks):
        if n:
            sums[-1], *got = lax.optimization_barrier((sums[-1], *got))
        other = [swap_core(block, "seq") for block in got]
        last = n + 1 == len(phase_blocks)
        shares = attend(
            got,
            other,
            prepared["steps"],
            prepared["scales"][n],
            prepared["weights"][n],
            sums if last else [],
            last,
        )
        if not last:
            sums.append(shares)
    parts = [shares[0]] + [rotate(shares[t], "seq", chips - t) for t in order]

    latent_next, window = step_latent(
        parts,
        prepared["latent_in"],
        prepared["base"],
        prepared["step_dt"],
        width,
    )
    near = shifted(window, "seq", 1)
    far = shifted(window, "seq", 2)
    decoded, sent = decode(
        prepared["lead"],
        far,
        near,
        window,
        prepared["w1"],
        prepared["b1"],
        prepared["gain"],
        conv_weight.reshape(-1, CH),
        prepared["b2"],
        patch_weight,
        prepared["patch_gain"],
        prepared["post_gain"],
        proj_weight,
        prepared["text"],
        devices,
    )
    decoded = decoded.reshape(frames, 2 * GRID_H, 2 * GRID_W, CH)
    spread = lax.all_to_all(sent, "seq", split_axis=0, concat_axis=0, tiled=True)
    image_vec, scores = rate(prepared["slots"], spread)
    return (latent_next, decoded, image_vec, scores)


def solution(mesh):
    in_specs = (
        P(("grp", "seq"), None),
        P(("grp", "seq"), None),
        P(("grp", "seq"), None),
        P(("grp", "seq"), None),
        P(),
        P(),
        P("grp"),
        P(),
        P(),
        P(),
        P(),
        P(),
        P(),
        P(),
        P(),
        P(),
        P(),
        P(None, "seq"),
        P("grp"),
        P("grp"),
    )
    out_specs = (
        P(("grp", "seq"), None),
        P(("grp", "seq"), None, None, None),
        P(("grp", "seq"), None),
        P(("grp", "seq")),
    )

    return jax.shard_map(local, mesh=mesh, in_specs=in_specs, out_specs=out_specs, check_vma=False)
```

```python
import functools

import jax
import jax.numpy as jnp
import numpy as np
from jax import lax
from jax.experimental import pallas as pl
from jax.experimental.pallas import tpu as pltpu
from jax.sharding import PartitionSpec as P

GRID_H = 8
GRID_W = 12
PATCH = GRID_H * GRID_W
HD = 128
LAT = 64
LAT_C = 16
CH = 384
TEXT_W = 768
KEY_CHUNK = 512
GATES = (2, 4)


highest = lax.Precision.HIGHEST
VM = pl.BlockSpec(memory_space=pltpu.VMEM)
SM = pl.BlockSpec(memory_space=pltpu.SMEM)
ANY = pl.BlockSpec(memory_space=pl.ANY)


def rotate(value, axis, steps):
    count = lax.axis_size(axis)
    return lax.ppermute(value, axis, [(i, (i + 2 * steps) % count) for i in range(count)])


def swap_core(value, axis):
    count = lax.axis_size(axis)
    return lax.ppermute(value, axis, [(i, i ^ 1) for i in range(count)])


def pack_kernel(blocks, at_ref, k_hbm, v_hbm, q_hbm, *refs):
    out_refs, (buf, in_sem, out_sem) = refs[:blocks], refs[blocks:]
    width = buf.shape[3]
    gets = []
    for n in range(blocks):
        at = pl.multiple_of(at_ref[n], HD)
        gets.append(
            [
                pltpu.make_async_copy(src.at[:, pl.ds(at, width)], buf.at[n, i], in_sem.at[n, i])
                for i, src in enumerate((k_hbm, v_hbm, q_hbm))
            ]
        )
        for get in gets[-1]:
            get.start()
    puts = [
        pltpu.make_async_copy(buf.at[n], out_refs[n], out_sem.at[n]) for n in range(blocks)
    ]
    for n in range(blocks):
        for get in gets[n]:
            get.wait()
        puts[n].start()
    for put in puts:
        put.wait()


def pack(keys, values, queries, starts, width):
    rows, blocks = keys.shape[0], starts.shape[0]
    return pl.pallas_call(
        functools.partial(pack_kernel, blocks),
        out_shape=[jax.ShapeDtypeStruct((3, rows, width), jnp.bfloat16)] * blocks,
        in_specs=[SM, ANY, ANY, ANY],
        out_specs=[ANY] * blocks,
        scratch_shapes=[
            pltpu.VMEM((blocks, 3, rows, width), jnp.bfloat16),
            pltpu.SemaphoreType.DMA((blocks, 3)),
            pltpu.SemaphoreType.DMA((blocks,)),
        ],
        name="pack",
    )(starts, keys, values, queries)


def attend_kernel(blocks, heads, frames, earlier, last, t_ref, sc_ref, w_ref, *refs):
    prev_refs, refs = refs[:earlier], refs[earlier:]
    near_refs, far_refs, refs = refs[:blocks], refs[blocks : 2 * blocks], refs[2 * blocks :]
    if last:
        out_refs, refs = refs[:blocks], refs[blocks:]
    else:
        sum_ref, refs = refs[0], refs[1:]
    q_s, k_s, v_s, s_a, s_b, m_a, m_b, acc_s, tot_s, sem, q_sem = refs[:11]
    if last:
        sum_ref, prev_s, prev_sem = refs[11:]
    sources = near_refs + far_refs
    rows = near_refs[0].shape[1]
    keys = len(sources) * rows
    scale = np.float32(HD**-0.5 * np.log2(np.e))

    def fetch(h, which):
        dst = (k_s, v_s)[which]
        for j, src in enumerate(sources):
            pltpu.make_async_copy(
                src.at[which, :, pl.ds(h * HD, HD)],
                dst.at[h, pl.ds(j * rows, rows), :],
                sem.at[h, which],
            ).start()

    fetch(0, 0)
    for b in range(blocks):
        pltpu.make_async_copy(near_refs[b].at[2], q_s.at[b], q_sem).start()
    fetch(0, 1)
    for h in range(1, heads):
        fetch(h, 0)
        fetch(h, 1)
    gets = []
    for n, prev in enumerate(prev_refs):
        gets.append(pltpu.make_async_copy(prev, prev_s.at[n], prev_sem.at[n]))
        gets[-1].start()
    sum_ref[...] = jnp.zeros(sum_ref.shape, jnp.float32)

    def arrived(h, which):
        whole = (k_s, v_s)[which].at[h]
        pltpu.make_async_copy(whole, whole, sem.at[h, which]).wait()

    def logits(h, b, at, s_ref, peak):
        q = q_s[b, :, pl.ds(pl.multiple_of(h * HD, HD), HD)]
        s = lax.dot_general(
            q,
            k_s[h, at : at + KEY_CHUNK, :],
            (((1,), (1,)), ((), ())),
            preferred_element_type=jnp.float32,
        )
        s_ref[:, at : at + KEY_CHUNK] = s
        folded = functools.reduce(
            jnp.maximum, [s[:, i : i + 128] for i in range(0, KEY_CHUNK, 128)]
        )
        return folded if peak is None else jnp.maximum(peak, folded)

    def keep_peak(peak, m_ref):
        m_ref[...] = jnp.broadcast_to(jnp.max(peak, axis=-1, keepdims=True) * scale, m_ref.shape)

    def finish(h, b, acc, total):
        o = acc / jnp.sum(total, axis=-1, keepdims=True)
        o = o.astype(jnp.bfloat16).astype(jnp.float32)
        square = jnp.sum(o * o, axis=-1, keepdims=True)
        per = rows // frames
        scaled = jnp.concatenate(
            [
                o[f * per : (f + 1) * per] * (1.0 + sc_ref[t_ref[b * frames + f], h])
                for f in range(frames)
            ],
            axis=0,
        )
        part = jnp.dot(scaled, w_ref[h], precision=highest, preferred_element_type=jnp.float32)
        lane = lax.broadcasted_iota(jnp.int32, part.shape, 1)
        return part + jnp.where(lane >= LAT, square, 0.0)

    def one_unit(h, now, top_ref, next_h, next_b, later, later_top_ref):
        top = top_ref[:, :1]
        peak, total = None, None
        acc = jnp.zeros((rows, HD), jnp.float32)
        for at in chunks:
            peak = logits(next_h, next_b, at, later, peak)
            e = jnp.exp2(now[:, at : at + KEY_CHUNK] * scale - top)
            folded = functools.reduce(jnp.add, [e[:, i : i + 128] for i in range(0, KEY_CHUNK, 128)])
            total = folded if total is None else total + folded
            acc = acc + jnp.dot(
                e.astype(jnp.bfloat16),
                v_s[h, at : at + KEY_CHUNK, :],
                preferred_element_type=jnp.float32,
            )
        keep_peak(peak, later_top_ref)
        return acc, total

    chunks = range(0, keys, KEY_CHUNK)
    pltpu.make_async_copy(q_s, q_s, q_sem).wait()
    arrived(0, 0)
    peak = None
    for at in chunks:
        peak = logits(0, 0, at, s_a, peak)
    keep_peak(peak, m_a)
    pairs = blocks // 2
    acc_s[...] = jnp.zeros(acc_s.shape, jnp.float32)
    tot_s[...] = jnp.ones(tot_s.shape, jnp.float32)

    def one_pair(n, carry):
        h, p = n // pairs, n % pairs
        after = jnp.minimum(n + 1, heads * pairs - 1)
        after_h, after_p = after // pairs, after % pairs
        before = jnp.maximum(n - 1, 0)
        before_h, before_p = before // pairs, before % pairs

        @pl.when(p == 0)
        def _():
            arrived(h, 1)

        @pl.when(after_h > h)
        def _():
            arrived(after_h, 0)

        late = finish(before_h, 2 * before_p + 1, acc_s[...], tot_s[...])
        sum_ref[2 * before_p + 1] = sum_ref[2 * before_p + 1] + late
        even = one_unit(h, s_a, m_a, h, 2 * p + 1, s_b, m_b)
        sum_ref[2 * p] = sum_ref[2 * p] + finish(h, 2 * p, *even)
        acc, total = one_unit(h, s_b, m_b, after_h, 2 * after_p, s_a, m_a)
        acc_s[...] = acc
        tot_s[...] = total
        return carry

    lax.fori_loop(0, heads * pairs, one_pair, 0)
    sum_ref[blocks - 1] = sum_ref[blocks - 1] + finish(
        heads - 1, blocks - 1, acc_s[...], tot_s[...]
    )
    if last:
        for get in gets:
            get.wait()
        row, lane = grid_iota(8, 128)
        pick = jnp.where(lane == LAT, 1.0, 0.0)
        for b in range(blocks):
            share = sum_ref[b]
            for n in range(earlier):
                share = share + prev_s[n, b]
            half = PATCH + 8 * frames
            spots = ((out_refs[b], 0), (out_refs[(b - 1) % blocks], half))
            beside = jnp.concatenate(
                [share[f * PATCH : (f + 1) * PATCH, :LAT] for f in range(frames)], axis=1
            ).astype(jnp.bfloat16)
            for ref, at in spots:
                ref[at : at + PATCH] = beside
            for f in range(frames):
                square = lax.dot_general(
                    pick,
                    share[f * PATCH : (f + 1) * PATCH],
                    (((1,), (1,)), ((), ())),
                    precision=highest,
                    preferred_element_type=jnp.float32,
                )
                square = jnp.concatenate(
                    [square, jnp.zeros((8, 128 - PATCH), jnp.float32)], axis=1
                )
                high = square.astype(jnp.bfloat16).astype(jnp.float32)
                both = jnp.where(row == 0, high, jnp.where(row == 1, square - high, 0.0))
                for ref, at in spots:
                    at = at + PATCH + 8 * f
                    ref[at : at + 8] = both.astype(jnp.bfloat16)


def attend(near, far, steps, scale, weight, earlier, last):
    blocks = len(near)
    _, rows, cols = near[0].shape
    heads, keys = cols // HD, 2 * blocks * rows
    frames = rows // PATCH
    sums = (blocks, rows, 128)
    if last:
        share = (2 * (PATCH + 8 * frames), frames * LAT)
        out_shape = [jax.ShapeDtypeStruct(share, jnp.bfloat16)] * blocks
        out_specs = [VM] * blocks
    else:
        out_shape, out_specs = jax.ShapeDtypeStruct(sums, jnp.float32), VM
    return pl.pallas_call(
        functools.partial(attend_kernel, blocks, heads, frames, len(earlier), last),
        out_shape=out_shape,
        in_specs=[SM, VM, VM] + [ANY] * (len(earlier) + 2 * blocks),
        out_specs=out_specs,
        scratch_shapes=[
            pltpu.VMEM((blocks, rows, cols), jnp.bfloat16),
            pltpu.VMEM((heads, keys, HD), jnp.bfloat16),
            pltpu.VMEM((heads, keys, HD), jnp.bfloat16),
            pltpu.VMEM((rows, keys), jnp.float32),
            pltpu.VMEM((rows, keys), jnp.float32),
            pltpu.VMEM((rows, 128), jnp.float32),
            pltpu.VMEM((rows, 128), jnp.float32),
            pltpu.VMEM((rows, HD), jnp.float32),
            pltpu.VMEM((rows, 128), jnp.float32),
            pltpu.SemaphoreType.DMA((heads, 2)),
            pltpu.SemaphoreType.DMA,
        ]
        + [
            pltpu.VMEM(sums, jnp.float32),
            pltpu.VMEM((max(1, len(earlier)),) + sums, jnp.float32),
            pltpu.SemaphoreType.DMA((max(1, len(earlier)),)),
        ]
        * last,
        cost_estimate=pl.CostEstimate(
            flops=4 * blocks * rows * keys * cols,
            bytes_accessed=4 * keys * cols,
            transcendentals=blocks * rows * keys * heads,
        ),
        name="attend",
    )(steps, scale, weight, *earlier, *near, *far)


WINDOW = ((-1, 1), (0, 0), (0, 1), (1, 0))


OFFSETS = [(di, dj) for di in (-1, 0, 1) for dj in (-1, 0, 1)]


def grid_iota(rows, cols):
    shape = (rows, cols)
    return lax.broadcasted_iota(jnp.int32, shape, 0), lax.broadcasted_iota(jnp.int32, shape, 1)


def over(value, count):
    return jnp.floor((value.astype(jnp.float32) + 0.5) * np.float32(1.0 / count)).astype(jnp.int32)


def as_matrix(hit):
    return jnp.where(hit, 1.0, 0.0).astype(jnp.bfloat16)


def move_matrix(di, dj, cols=PATCH):
    row, col = grid_iota(PATCH, cols)
    j = row - GRID_W * over(row, GRID_W)
    inside = (j + dj >= 0) & (j + dj < GRID_W) & (col < PATCH)
    return as_matrix((col - row == GRID_W * di + dj) & inside)


def place_matrix(di, dj):
    row, col = grid_iota(LAT, 16 * LAT_C)
    u, w, c = col >> 6, (col >> 4) & 3, col & 15
    source = 2 * LAT_C * (1 - (u & 1)) + LAT_C * (1 - (w & 1)) + c

    def seen(at, step):
        return {-1: at == 0, 0: (at == 1) | (at == 2), 1: at == 3}[step]

    return as_matrix((row == source) & seen(u, di) & seen(w, dj))


def order_matrix():
    row, col = grid_iota(4 * PATCH, 4 * PATCH)
    y = over(row, 2 * GRID_W)
    z = row - 2 * GRID_W * y
    source = (2 * (y & 1) + (z & 1)) * PATCH + (y >> 1) * GRID_W + (z >> 1)
    return as_matrix(col == source)


def latent_kernel(parts, width, frames, flag_ref, dt_ref, *refs):
    part_refs, refs = refs[:parts], refs[parts:]
    own_ref, far_ref, base_ref, next_ref, win_ref, before_ref, pass_ref = refs
    total = part_refs[0][...].astype(jnp.float32)
    for r in part_refs[1:]:
        total = total + r[...].astype(jnp.float32)
    row, _ = grid_iota(8, 128)
    pick = jnp.where(row < 2, 1.0, 0.0)
    cols = 16 * LAT_C
    moves = jnp.concatenate([move_matrix(di, dj, 128) for di, dj in OFFSETS], axis=1)
    places = jnp.concatenate([place_matrix(di, dj) for di, dj in OFFSETS], axis=1)
    none = jnp.zeros((128 - PATCH, cols), jnp.bfloat16)
    first_chip, core = flag_ref[0], flag_ref[1]
    for side, latent in enumerate((jnp.transpose(own_ref[...]), jnp.transpose(far_ref[...]))):
        skip = side * (PATCH + 8 * frames)
        for f in range(frames):
            at = slice(f * PATCH, (f + 1) * PATCH)
            squares = total[skip + PATCH + 8 * f : skip + PATCH + 8 * (f + 1)]
            square = lax.dot_general(
                squares,
                pick,
                (((0,), (0,)), ((), ())),
                precision=highest,
                preferred_element_type=jnp.float32,
            )[:PATCH, :LAT]
            inverse = lax.rsqrt(square * np.float32(1.0 / width) + 1e-06)
            scaled = total[skip : skip + PATCH, f * LAT : (f + 1) * LAT] * inverse
            g = side * frames + f
            value = latent[at] + dt_ref[g] * (scaled + base_ref[g : g + 1])
            spread = jnp.dot(
                value.astype(jnp.bfloat16), places, preferred_element_type=jnp.float32
            ).astype(jnp.bfloat16)
            stacked = jnp.concatenate(
                [x for o in range(len(OFFSETS)) for x in (spread[:, o * cols : (o + 1) * cols], none)],
                axis=0,
            )
            window = jnp.dot(moves, stacked, preferred_element_type=jnp.float32)
            if side:
                window = jnp.where(first_chip == 1, 0.0, window)
                before_ref[at] = window.astype(jnp.bfloat16)
                pass_ref[at] = jnp.where(core == 0, win_ref[at], before_ref[at])
            else:
                next_ref[at] = value
                win_ref[at] = window.astype(jnp.bfloat16)


def step_latent(flags, parts, own, far, base, step_dt, width):
    rows = own.shape[1]
    window = jax.ShapeDtypeStruct((rows, 16 * LAT_C), jnp.bfloat16)
    return pl.pallas_call(
        functools.partial(latent_kernel, len(parts), width, rows // PATCH),
        out_shape=[jax.ShapeDtypeStruct((rows, LAT), jnp.float32), window, window, window],
        in_specs=[SM, SM] + [VM] * (len(parts) + 3),
        out_specs=[VM] * 4,
        name="latent",
    )(flags, step_dt, *parts, own, far, base)


def text_kernel(at_ref, id_ref, table_hbm, out_ref, buf, sem):
    count = id_ref.shape[0]

    def block(n):
        start = pl.multiple_of((id_ref[n] // 128) * 128, 128)
        return pltpu.make_async_copy(table_hbm.at[:, pl.ds(start, 128)], buf.at[n], sem)

    def fetch(n, carry):
        block(n).start()
        return carry

    lax.fori_loop(0, count, fetch, 0)
    pltpu.make_async_copy(buf, buf, sem).wait()
    width = buf.shape[1]
    _, lane = grid_iota(width, 128)

    def add(n, acc):
        return acc + jnp.where(lane == id_ref[n] % 128, buf[n].astype(jnp.float32), 0.0)

    acc = lax.fori_loop(0, count, add, jnp.zeros((width, 128), jnp.float32))
    own = lax.dot_general(
        jnp.ones((8, 128), jnp.float32),
        acc,
        (((1,), (1,)), ((), ())),
        precision=highest,
        preferred_element_type=jnp.float32,
    )
    row, col = grid_iota(width, out_ref.shape[1])
    spot = jnp.where(col == row + at_ref[0], 1.0, 0.0)
    placed = jnp.dot(own, spot, precision=highest, preferred_element_type=jnp.float32)
    out_ref[...] = placed[:1] * np.float32(1.0 / count)


def text_mean(at, ids, table):
    width = table.shape[0]
    return pl.pallas_call(
        text_kernel,
        out_shape=jax.ShapeDtypeStruct((1, TEXT_W), jnp.float32),
        in_specs=[SM, SM, ANY],
        out_specs=VM,
        scratch_shapes=[
            pltpu.VMEM((ids.shape[0], width, 128), jnp.bfloat16),
            pltpu.SemaphoreType.DMA,
        ],
        name="text",
    )(at, ids, table)


def decode_kernel(
    frames,
    lead_ref,
    far_ref,
    near_ref,
    own_ref,
    w1_ref,
    b1_ref,
    gain_ref,
    b2_ref,
    pg_ref,
    post_ref,
    w2_hbm,
    pw_hbm,
    proj_hbm,
    out_ref,
    sent_ref,
    w2_s,
    pw_s,
    proj_s,
    win_s,
    x_s,
    sem,
):
    taps = 9 * CH
    w2_copy = pltpu.make_async_copy(w2_hbm, w2_s, sem.at[0])
    pw_copy = pltpu.make_async_copy(pw_hbm, pw_s, sem.at[1])
    w2_copy.start()
    pw_copy.start()
    proj_copy = pltpu.make_async_copy(proj_hbm, proj_s, sem.at[2])
    proj_copy.start()
    rows = frames * PATCH
    for n, r in enumerate((far_ref, near_ref, own_ref)):
        win_s[n * rows : (n + 1) * rows] = r[...]
    wide = frames + 2
    skip = 3 * frames - wide - 2
    cols = 16 * LAT_C
    firsts = []
    for q in range(4):
        acc = jnp.zeros((wide * PATCH, CH), jnp.float32)
        for t in range(3):
            acc = acc + jnp.dot(
                win_s[(skip + t) * PATCH : (skip + t + wide) * PATCH],
                w1_ref[t * cols : (t + 1) * cols, q * CH : (q + 1) * CH],
                preferred_element_type=jnp.float32,
            )
        first = (acc + b1_ref[...]).astype(jnp.bfloat16).astype(jnp.float32)
        firsts.append(first[2 * PATCH :])
        mean = jnp.mean(first * first, axis=-1, keepdims=True)
        v = first * lax.rsqrt(mean + 1e-06) * gain_ref[...]
        act = v / (1.0 + jnp.exp(-v))
        row = lax.broadcasted_iota(jnp.int32, (wide * PATCH, 1), 0)
        act = jnp.where((row >= 2 * PATCH) | (lead_ref[0] == 0), act, 0.0).astype(jnp.bfloat16)
        a, b = q // 2, q % 2
        da, db = (1, -1)[a], (1, -1)[b]
        moves = jnp.concatenate(
            [move_matrix(da, 0), move_matrix(0, db), move_matrix(da, db)], axis=0
        )
        for f in range(wide):
            plane = act[f * PATCH : (f + 1) * PATCH]
            moved = jnp.dot(
                moves, plane, preferred_element_type=jnp.float32
            ).astype(jnp.bfloat16)
            pieces = {
                (0, 0): plane,
                (1, 0): moved[:PATCH],
                (0, 1): moved[PATCH : 2 * PATCH],
                (1, 1): moved[2 * PATCH :],
            }
            for (ma, mb), piece in pieces.items():
                u = WINDOW.index(((1, -1)[a] if ma else 0, a))
                w = WINDOW.index(((1, -1)[b] if mb else 0, b))
                for oa in (0, 1):
                    for ob in (0, 1):
                        dy, dz = u - oa, w - ob
                        if 0 <= dy < 3 and 0 <= dz < 3:
                            at = (f * 4 + 2 * oa + ob) * PATCH
                            tap = (3 * dy + dz) * CH
                            x_s[at : at + PATCH, tap : tap + CH] = piece
    w2_copy.wait()
    block = 4 * PATCH
    out = jnp.zeros((frames * block, CH), jnp.float32)
    for t in range(3):
        out = out + jnp.dot(
            x_s[t * block : (t + frames) * block],
            w2_s[t * taps : (t + 1) * taps],
            preferred_element_type=jnp.float32,
        )
    first = jnp.concatenate(
        [firsts[q][f * PATCH : (f + 1) * PATCH] for f in range(frames) for q in range(4)], axis=0
    )
    dec = (out + b2_ref[...] + first).astype(jnp.bfloat16)
    order = order_matrix()
    for f in range(frames):
        out_ref[f * block : (f + 1) * block] = jnp.dot(
            order, dec[f * block : (f + 1) * block], preferred_element_type=jnp.float32
        ).astype(jnp.bfloat16)
    pw_copy.wait()
    emb = jnp.zeros((rows, pw_s.shape[1]), jnp.float32)
    for q in range(4):
        lhs = jnp.concatenate(
            [dec[(f * 4 + q) * PATCH : (f * 4 + q + 1) * PATCH] for f in range(frames)], axis=0
        )
        emb = emb + jnp.dot(
            lhs, pw_s[q * CH : (q + 1) * CH], preferred_element_type=jnp.float32
        )
    emb = emb.astype(jnp.bfloat16).astype(jnp.float32)
    centered = emb - jnp.mean(emb, axis=-1, keepdims=True)
    variance = jnp.mean(centered * centered, axis=-1, keepdims=True)
    normed = centered * lax.rsqrt(variance + 1e-05) * pg_ref[...]
    pooled = jnp.concatenate(
        [
            jnp.mean(normed[f * PATCH : (f + 1) * PATCH], axis=0, keepdims=True)
            for f in range(frames)
        ],
        axis=0,
    )
    centered = pooled - jnp.mean(pooled, axis=-1, keepdims=True)
    variance = jnp.mean(centered * centered, axis=-1, keepdims=True)
    vec = centered * lax.rsqrt(variance + 1e-05) * post_ref[...]
    columns = jnp.transpose(
        jnp.concatenate([vec, jnp.zeros((8 - frames, vec.shape[1]), jnp.float32)], axis=0)
    )
    proj_copy.wait()
    for f in range(frames):
        row = jnp.sum(columns[:, f : f + 1] * proj_s[...], axis=0, keepdims=True)
        for n in range(sent_ref.shape[0]):
            sent_ref[n, f : f + 1, :] = row


def window_weight(weight):
    taps = weight.reshape(3, 3, 3, LAT_C, CH)
    grown = [
        jnp.pad(taps, ((0, 0), (a, 1 - a), (b, 1 - b), (0, 0), (0, 0))).reshape(-1, CH)
        for a in (0, 1)
        for b in (0, 1)
    ]
    return jnp.concatenate(grown, axis=1)


def decode(
    lead, far, near, own, w1, b1, gain, w2, b2, pw, patch_gain, post_gain, proj, devices
):
    rows = own.shape[0]
    frames = rows // PATCH
    wide = frames + 2
    return pl.pallas_call(
        functools.partial(decode_kernel, frames),
        out_shape=[
            jax.ShapeDtypeStruct((frames * 4 * PATCH, CH), jnp.bfloat16),
            jax.ShapeDtypeStruct((devices, frames, proj.shape[1]), jnp.float32),
        ],
        in_specs=[SM] + [VM] * 9 + [ANY, ANY, ANY],
        out_specs=[VM, VM],
        scratch_shapes=[
            pltpu.VMEM(w2.shape, jnp.bfloat16),
            pltpu.VMEM(pw.shape, jnp.bfloat16),
            pltpu.VMEM(proj.shape, jnp.float32),
            pltpu.VMEM((3 * rows, 16 * LAT_C), jnp.bfloat16),
            pltpu.VMEM((wide * 4 * PATCH, 9 * CH), jnp.bfloat16),
            pltpu.SemaphoreType.DMA((3,)),
        ],
        name="decode",
    )(
        lead,
        far,
        near,
        own,
        w1,
        b1,
        gain,
        b2,
        patch_gain,
        post_gain,
        w2,
        pw,
        proj,
    )


def rate_kernel(frames, slot_ref, text_ref, got_ref, vec_ref, score_ref):
    text = text_ref[...]
    text_rms = jnp.sqrt(jnp.mean(text * text) + 1e-06)
    for f in range(frames):
        slot = slot_ref[f]
        block = got_ref[slot // frames]
        row = block[:1]
        for n in range(1, frames):
            row = jnp.where(slot % frames == n, block[n : n + 1], row)
        vec_ref[f : f + 1] = row
        inner = jnp.sum(row * text)
        image_rms = jnp.sqrt(jnp.mean(row * row) + 1e-06)
        score_ref[f] = 100.0 * inner / (TEXT_W * image_rms * text_rms)


def rate(slots, text, got):
    frames = slots.shape[0]
    return pl.pallas_call(
        functools.partial(rate_kernel, frames),
        out_shape=[
            jax.ShapeDtypeStruct((frames, got.shape[2]), jnp.float32),
            jax.ShapeDtypeStruct((frames,), jnp.float32),
        ],
        in_specs=[SM, VM, VM],
        out_specs=[VM, SM],
        name="rate",
    )(slots, text, got)


def local(
    queries,
    keys,
    values,
    latent_in,
    mod_table,
    step_size,
    timestep,
    head_weight,
    conv_in_weight,
    conv_in_bias,
    norm_gain,
    conv_weight,
    conv_bias,
    patch_weight,
    patch_gain,
    post_gain,
    proj_weight,
    text_table,
    prompt_ids,
    frame_order,
):
    rows, width = queries.shape
    devices = lax.axis_size("seq")
    chips = devices // 2
    cols = width // chips
    heads = cols // HD
    frames = rows // PATCH
    me = lax.axis_index("seq")
    chip, core = me // 2, me % 2

    tail = max(1, heads // 4)
    phases = tuple(n for n in (heads - 2 * tail, tail, tail) if n > 0) if heads > tail else (tail,)
    firsts = [sum(phases[:n]) for n in range(len(phases))]

    order = sorted(range(1, chips), key=lambda t: abs(2 * t - chips))

    def packed(first, count):
        at = ((chip + jnp.arange(chips)) % chips) * cols + first * HD
        return pack(keys, values, queries, at.astype(jnp.int32), count * HD)

    blocks = packed(firsts[0], phases[0])
    got = [blocks[0]] * chips
    for turn in order:
        got[turn] = rotate(blocks[turn], "seq", turn)
    scale = lax.dynamic_slice_in_dim(mod_table[:, 1, :], chip * cols, cols, 1)
    scale = scale.reshape(-1, heads, 1, HD)
    weight = lax.dynamic_slice_in_dim(head_weight, chip * cols, cols, 0).reshape(heads, HD, LAT)
    weight = jnp.pad(weight, ((0, 0), (0, 0), (0, 128 - LAT)))
    origin = 2 * ((chip - jnp.arange(chips)) % chips) + core
    steps = jnp.take(timestep.reshape(devices, frames), origin, axis=0).reshape(-1)
    near_steps = jnp.stack(
        [
            lax.dynamic_slice_in_dim(timestep, at * frames, frames, 0)
            for at in (me, jnp.maximum(me - 2, 0))
        ]
    ).reshape(-1)
    base = jnp.dot(jnp.take(mod_table[:, 0, :], near_steps, axis=0), head_weight, precision=highest)
    step_dt = jnp.take(step_size, near_steps)
    text_row = text_mean(
        (me * text_table.shape[1]).astype(jnp.int32).reshape(1), prompt_ids, text_table.T
    )
    slots = lax.dynamic_slice_in_dim(frame_order, me * frames, frames, 0)
    prepared = dict(
        scales=[scale[:, f : f + n] for f, n in zip(firsts, phases)],
        weights=[weight[f : f + n] for f, n in zip(firsts, phases)],
        steps=steps,
        base=base,
        step_dt=step_dt,
        text=text_row,
        slots=slots,
        w1=window_weight(conv_in_weight),
        b1=conv_in_bias.reshape(1, -1),
        gain=norm_gain.reshape(1, -1),
        b2=conv_bias.reshape(1, -1),
        patch_gain=patch_gain.reshape(1, -1),
        post_gain=post_gain.reshape(1, -1),
        lead=(me == 0).astype(jnp.int32).reshape(1),
        flags=jnp.stack([chip == 0, core]).astype(jnp.int32),
        later=[packed(f, n) for f, n in zip(firsts[1:], phases[1:])],
    )
    words = jnp.broadcast_to(prepared["text"][None], (devices, 1, TEXT_W))
    words = lax.all_to_all(words, "seq", split_axis=0, concat_axis=0, tiled=True)
    words = jnp.sum(words, axis=0)
    far_latent = rotate(latent_in.T, "seq", 1)
    steps, words, far_latent = lax.optimization_barrier((prepared["steps"], words, far_latent))
    phase_blocks = [got]
    for gate, blocks in zip(GATES, prepared["later"]):
        before = phase_blocks[0][order[min(gate, len(order) - 1)]]
        blocks, _ = lax.optimization_barrier((blocks, before))
        got = [blocks[0]] * chips
        for turn in order:
            got[turn] = rotate(blocks[turn], "seq", turn)
        phase_blocks.append(got)
    sums = []
    for n, got in enumerate(phase_blocks):
        if n:
            sums[-1], *got = lax.optimization_barrier((sums[-1], *got))
        other = [swap_core(block, "seq") for block in got]
        last = n + 1 == len(phase_blocks)
        shares = attend(
            got,
            other,
            steps,
            prepared["scales"][n],
            prepared["weights"][n],
            sums if last else [],
            last,
        )
        if not last:
            sums.append(shares)
    parts = [shares[0]] + [rotate(shares[t], "seq", chips - t) for t in order]

    latent_next, window, far, passed = step_latent(
        prepared["flags"],
        parts,
        latent_in.T,
        far_latent,
        prepared["base"],
        prepared["step_dt"],
        width,
    )
    near = swap_core(passed, "seq")
    decoded, sent = decode(
        prepared["lead"],
        far,
        near,
        window,
        prepared["w1"],
        prepared["b1"],
        prepared["gain"],
        conv_weight.reshape(-1, CH),
        prepared["b2"],
        patch_weight,
        prepared["patch_gain"],
        prepared["post_gain"],
        proj_weight,
        devices,
    )
    decoded = decoded.reshape(frames, 2 * GRID_H, 2 * GRID_W, CH)
    spread = lax.all_to_all(sent, "seq", split_axis=0, concat_axis=0, tiled=True)
    image_vec, scores = rate(prepared["slots"], words, spread)
    return (latent_next, decoded, image_vec, scores)


def solution(mesh):
    in_specs = (
        P(("grp", "seq"), None),
        P(("grp", "seq"), None),
        P(("grp", "seq"), None),
        P(("grp", "seq"), None),
        P(),
        P(),
        P("grp"),
        P(),
        P(),
        P(),
        P(),
        P(),
        P(),
        P(),
        P(),
        P(),
        P(),
        P(None, "seq"),
        P("grp"),
        P("grp"),
    )
    out_specs = (
        P(("grp", "seq"), None),
        P(("grp", "seq"), None, None, None),
        P(("grp", "seq"), None),
        P(("grp", "seq")),
    )

    return jax.shard_map(local, mesh=mesh, in_specs=in_specs, out_specs=out_specs, check_vma=False)
```

```python
import functools

import jax
import jax.numpy as jnp
import numpy as np
from jax import lax
from jax.experimental import pallas as pl
from jax.experimental.pallas import tpu as pltpu
from jax.sharding import PartitionSpec as P

GRID_H = 8
GRID_W = 12
PATCH = GRID_H * GRID_W
HD = 128
LAT = 64
LAT_C = 16
CH = 384
TEXT_W = 768
KEY_CHUNK = 512
GATES = (2,)


highest = lax.Precision.HIGHEST
VM = pl.BlockSpec(memory_space=pltpu.VMEM)
SM = pl.BlockSpec(memory_space=pltpu.SMEM)
ANY = pl.BlockSpec(memory_space=pl.ANY)


def rotate(value, axis, steps):
    count = lax.axis_size(axis)
    return lax.ppermute(value, axis, [(i, (i + 2 * steps) % count) for i in range(count)])


def swap_core(value, axis):
    count = lax.axis_size(axis)
    return lax.ppermute(value, axis, [(i, i ^ 1) for i in range(count)])


def pack_kernel(blocks, at_ref, k_hbm, v_hbm, q_hbm, *refs):
    out_refs, (buf, in_sem, out_sem) = refs[:blocks], refs[blocks:]
    width = buf.shape[3]
    gets = []
    for n in range(blocks):
        at = pl.multiple_of(at_ref[n], HD)
        gets.append(
            [
                pltpu.make_async_copy(src.at[:, pl.ds(at, width)], buf.at[n, i], in_sem.at[n, i])
                for i, src in enumerate((k_hbm, v_hbm, q_hbm))
            ]
        )
        for get in gets[-1]:
            get.start()
    puts = [
        pltpu.make_async_copy(buf.at[n], out_refs[n], out_sem.at[n]) for n in range(blocks)
    ]
    for n in range(blocks):
        for get in gets[n]:
            get.wait()
        puts[n].start()
    for put in puts:
        put.wait()


def pack(keys, values, queries, starts, width):
    rows, blocks = keys.shape[0], starts.shape[0]
    return pl.pallas_call(
        functools.partial(pack_kernel, blocks),
        out_shape=[jax.ShapeDtypeStruct((3, rows, width), jnp.bfloat16)] * blocks,
        in_specs=[SM, ANY, ANY, ANY],
        out_specs=[ANY] * blocks,
        scratch_shapes=[
            pltpu.VMEM((blocks, 3, rows, width), jnp.bfloat16),
            pltpu.SemaphoreType.DMA((blocks, 3)),
            pltpu.SemaphoreType.DMA((blocks,)),
        ],
        name="pack",
    )(starts, keys, values, queries)


def attend_kernel(blocks, heads, frames, earlier, last, t_ref, sc_ref, w_ref, *refs):
    prev_refs, refs = refs[:earlier], refs[earlier:]
    near_refs, far_refs, refs = refs[:blocks], refs[blocks : 2 * blocks], refs[2 * blocks :]
    if last:
        out_refs, refs = refs[:blocks], refs[blocks:]
    else:
        sum_ref, refs = refs[0], refs[1:]
    q_s, k_s, v_s, s_a, s_b, m_a, m_b, acc_s, tot_s, sem, q_sem = refs[:11]
    if last:
        sum_ref, prev_s, prev_sem = refs[11:]
    sources = near_refs + far_refs
    rows = near_refs[0].shape[1]
    keys = len(sources) * rows
    scale = np.float32(HD**-0.5 * np.log2(np.e))

    def fetch(h, which):
        dst = (k_s, v_s)[which]
        for j, src in enumerate(sources):
            pltpu.make_async_copy(
                src.at[which, :, pl.ds(h * HD, HD)],
                dst.at[h, pl.ds(j * rows, rows), :],
                sem.at[h, which],
            ).start()

    fetch(0, 0)
    for b in range(blocks):
        pltpu.make_async_copy(near_refs[b].at[2], q_s.at[b], q_sem).start()
    fetch(0, 1)
    for h in range(1, heads):
        fetch(h, 0)
        fetch(h, 1)
    gets = []
    for n, prev in enumerate(prev_refs):
        gets.append(pltpu.make_async_copy(prev, prev_s.at[n], prev_sem.at[n]))
        gets[-1].start()
    sum_ref[...] = jnp.zeros(sum_ref.shape, jnp.float32)

    def arrived(h, which):
        whole = (k_s, v_s)[which].at[h]
        pltpu.make_async_copy(whole, whole, sem.at[h, which]).wait()

    def logits(h, b, at, s_ref, peak):
        q = q_s[b, :, pl.ds(pl.multiple_of(h * HD, HD), HD)]
        s = lax.dot_general(
            q,
            k_s[h, at : at + KEY_CHUNK, :],
            (((1,), (1,)), ((), ())),
            preferred_element_type=jnp.float32,
        )
        s_ref[:, at : at + KEY_CHUNK] = s
        folded = functools.reduce(
            jnp.maximum, [s[:, i : i + 128] for i in range(0, KEY_CHUNK, 128)]
        )
        return folded if peak is None else jnp.maximum(peak, folded)

    def keep_peak(peak, m_ref):
        m_ref[...] = jnp.broadcast_to(jnp.max(peak, axis=-1, keepdims=True) * scale, m_ref.shape)

    def finish(h, b, acc, total):
        o = acc / jnp.sum(total, axis=-1, keepdims=True)
        o = o.astype(jnp.bfloat16).astype(jnp.float32)
        square = jnp.sum(o * o, axis=-1, keepdims=True)
        per = rows // frames
        scaled = jnp.concatenate(
            [
                o[f * per : (f + 1) * per] * (1.0 + sc_ref[t_ref[b * frames + f], h])
                for f in range(frames)
            ],
            axis=0,
        )
        part = jnp.dot(scaled, w_ref[h], precision=highest, preferred_element_type=jnp.float32)
        lane = lax.broadcasted_iota(jnp.int32, part.shape, 1)
        return part + jnp.where(lane >= LAT, square, 0.0)

    def one_unit(h, now, top_ref, next_h, next_b, later, later_top_ref):
        top = top_ref[:, :1]
        peak, total = None, None
        acc = jnp.zeros((rows, HD), jnp.float32)
        for at in chunks:
            peak = logits(next_h, next_b, at, later, peak)
            e = jnp.exp2(now[:, at : at + KEY_CHUNK] * scale - top)
            folded = functools.reduce(jnp.add, [e[:, i : i + 128] for i in range(0, KEY_CHUNK, 128)])
            total = folded if total is None else total + folded
            acc = acc + jnp.dot(
                e.astype(jnp.bfloat16),
                v_s[h, at : at + KEY_CHUNK, :],
                preferred_element_type=jnp.float32,
            )
        keep_peak(peak, later_top_ref)
        return acc, total

    chunks = range(0, keys, KEY_CHUNK)
    pltpu.make_async_copy(q_s, q_s, q_sem).wait()
    arrived(0, 0)
    peak = None
    for at in chunks:
        peak = logits(0, 0, at, s_a, peak)
    keep_peak(peak, m_a)
    pairs = blocks // 2
    acc_s[...] = jnp.zeros(acc_s.shape, jnp.float32)
    tot_s[...] = jnp.ones(tot_s.shape, jnp.float32)

    def one_pair(n, carry):
        h, p = n // pairs, n % pairs
        after = jnp.minimum(n + 1, heads * pairs - 1)
        after_h, after_p = after // pairs, after % pairs
        before = jnp.maximum(n - 1, 0)
        before_h, before_p = before // pairs, before % pairs

        @pl.when(p == 0)
        def _():
            arrived(h, 1)

        @pl.when(after_h > h)
        def _():
            arrived(after_h, 0)

        late = finish(before_h, 2 * before_p + 1, acc_s[...], tot_s[...])
        sum_ref[2 * before_p + 1] = sum_ref[2 * before_p + 1] + late
        even = one_unit(h, s_a, m_a, h, 2 * p + 1, s_b, m_b)
        sum_ref[2 * p] = sum_ref[2 * p] + finish(h, 2 * p, *even)
        acc, total = one_unit(h, s_b, m_b, after_h, 2 * after_p, s_a, m_a)
        acc_s[...] = acc
        tot_s[...] = total
        return carry

    lax.fori_loop(0, heads * pairs, one_pair, 0)
    sum_ref[blocks - 1] = sum_ref[blocks - 1] + finish(
        heads - 1, blocks - 1, acc_s[...], tot_s[...]
    )
    if last:
        for get in gets:
            get.wait()
        row, lane = grid_iota(8, 128)
        pick = jnp.where(lane == LAT, 1.0, 0.0)
        for b in range(blocks):
            share = sum_ref[b]
            for n in range(earlier):
                share = share + prev_s[n, b]
            half = PATCH + 8 * frames
            spots = ((out_refs[b], 0), (out_refs[(b - 1) % blocks], half))
            beside = jnp.concatenate(
                [share[f * PATCH : (f + 1) * PATCH, :LAT] for f in range(frames)], axis=1
            ).astype(jnp.bfloat16)
            for ref, at in spots:
                ref[at : at + PATCH] = beside
            for f in range(frames):
                square = lax.dot_general(
                    pick,
                    share[f * PATCH : (f + 1) * PATCH],
                    (((1,), (1,)), ((), ())),
                    precision=highest,
                    preferred_element_type=jnp.float32,
                )
                square = jnp.concatenate(
                    [square, jnp.zeros((8, 128 - PATCH), jnp.float32)], axis=1
                )
                high = square.astype(jnp.bfloat16).astype(jnp.float32)
                both = jnp.where(row == 0, high, jnp.where(row == 1, square - high, 0.0))
                for ref, at in spots:
                    at = at + PATCH + 8 * f
                    ref[at : at + 8] = both.astype(jnp.bfloat16)


def attend(near, far, steps, scale, weight, earlier, last):
    blocks = len(near)
    _, rows, cols = near[0].shape
    heads, keys = cols // HD, 2 * blocks * rows
    frames = rows // PATCH
    sums = (blocks, rows, 128)
    if last:
        share = (2 * (PATCH + 8 * frames), frames * LAT)
        out_shape = [jax.ShapeDtypeStruct(share, jnp.bfloat16)] * blocks
        out_specs = [VM] * blocks
    else:
        out_shape, out_specs = jax.ShapeDtypeStruct(sums, jnp.float32), VM
    return pl.pallas_call(
        functools.partial(attend_kernel, blocks, heads, frames, len(earlier), last),
        out_shape=out_shape,
        in_specs=[SM, VM, VM] + [ANY] * (len(earlier) + 2 * blocks),
        out_specs=out_specs,
        scratch_shapes=[
            pltpu.VMEM((blocks, rows, cols), jnp.bfloat16),
            pltpu.VMEM((heads, keys, HD), jnp.bfloat16),
            pltpu.VMEM((heads, keys, HD), jnp.bfloat16),
            pltpu.VMEM((rows, keys), jnp.float32),
            pltpu.VMEM((rows, keys), jnp.float32),
            pltpu.VMEM((rows, 128), jnp.float32),
            pltpu.VMEM((rows, 128), jnp.float32),
            pltpu.VMEM((rows, HD), jnp.float32),
            pltpu.VMEM((rows, 128), jnp.float32),
            pltpu.SemaphoreType.DMA((heads, 2)),
            pltpu.SemaphoreType.DMA,
        ]
        + [
            pltpu.VMEM(sums, jnp.float32),
            pltpu.VMEM((max(1, len(earlier)),) + sums, jnp.float32),
            pltpu.SemaphoreType.DMA((max(1, len(earlier)),)),
        ]
        * last,
        cost_estimate=pl.CostEstimate(
            flops=4 * blocks * rows * keys * cols,
            bytes_accessed=4 * keys * cols,
            transcendentals=blocks * rows * keys * heads,
        ),
        name="attend",
    )(steps, scale, weight, *earlier, *near, *far)


WINDOW = ((-1, 1), (0, 0), (0, 1), (1, 0))


OFFSETS = [(di, dj) for di in (-1, 0, 1) for dj in (-1, 0, 1)]


def grid_iota(rows, cols):
    shape = (rows, cols)
    return lax.broadcasted_iota(jnp.int32, shape, 0), lax.broadcasted_iota(jnp.int32, shape, 1)


def over(value, count):
    return jnp.floor((value.astype(jnp.float32) + 0.5) * np.float32(1.0 / count)).astype(jnp.int32)


def as_matrix(hit):
    return jnp.where(hit, 1.0, 0.0).astype(jnp.bfloat16)


def move_matrix(di, dj, cols=PATCH):
    row, col = grid_iota(PATCH, cols)
    j = row - GRID_W * over(row, GRID_W)
    inside = (j + dj >= 0) & (j + dj < GRID_W) & (col < PATCH)
    return as_matrix((col - row == GRID_W * di + dj) & inside)


def place_matrix(di, dj):
    row, col = grid_iota(LAT, 16 * LAT_C)
    u, w, c = col >> 6, (col >> 4) & 3, col & 15
    source = 2 * LAT_C * (1 - (u & 1)) + LAT_C * (1 - (w & 1)) + c

    def seen(at, step):
        return {-1: at == 0, 0: (at == 1) | (at == 2), 1: at == 3}[step]

    return as_matrix((row == source) & seen(u, di) & seen(w, dj))


def order_matrix():
    row, col = grid_iota(4 * PATCH, 4 * PATCH)
    y = over(row, 2 * GRID_W)
    z = row - 2 * GRID_W * y
    source = (2 * (y & 1) + (z & 1)) * PATCH + (y >> 1) * GRID_W + (z >> 1)
    return as_matrix(col == source)


def latent_kernel(parts, width, frames, flag_ref, dt_ref, *refs):
    part_refs, refs = refs[:parts], refs[parts:]
    own_ref, far_ref, base_ref, next_ref, win_ref, before_ref, pass_ref = refs
    total = part_refs[0][...].astype(jnp.float32)
    for r in part_refs[1:]:
        total = total + r[...].astype(jnp.float32)
    row, _ = grid_iota(8, 128)
    pick = jnp.where(row < 2, 1.0, 0.0)
    cols = 16 * LAT_C
    moves = jnp.concatenate([move_matrix(di, dj, 128) for di, dj in OFFSETS], axis=1)
    places = jnp.concatenate([place_matrix(di, dj) for di, dj in OFFSETS], axis=1)
    none = jnp.zeros((128 - PATCH, cols), jnp.bfloat16)
    first_chip, core = flag_ref[0], flag_ref[1]
    for side, latent in enumerate((jnp.transpose(own_ref[...]), jnp.transpose(far_ref[...]))):
        skip = side * (PATCH + 8 * frames)
        for f in range(frames):
            at = slice(f * PATCH, (f + 1) * PATCH)
            squares = total[skip + PATCH + 8 * f : skip + PATCH + 8 * (f + 1)]
            square = lax.dot_general(
                squares,
                pick,
                (((0,), (0,)), ((), ())),
                precision=highest,
                preferred_element_type=jnp.float32,
            )[:PATCH, :LAT]
            inverse = lax.rsqrt(square * np.float32(1.0 / width) + 1e-06)
            scaled = total[skip : skip + PATCH, f * LAT : (f + 1) * LAT] * inverse
            g = side * frames + f
            value = latent[at] + dt_ref[g] * (scaled + base_ref[g : g + 1])
            spread = jnp.dot(
                value.astype(jnp.bfloat16), places, preferred_element_type=jnp.float32
            ).astype(jnp.bfloat16)
            stacked = jnp.concatenate(
                [x for o in range(len(OFFSETS)) for x in (spread[:, o * cols : (o + 1) * cols], none)],
                axis=0,
            )
            window = jnp.dot(moves, stacked, preferred_element_type=jnp.float32)
            if side:
                window = jnp.where(first_chip == 1, 0.0, window)
                before_ref[at] = window.astype(jnp.bfloat16)
                pass_ref[at] = jnp.where(core == 0, win_ref[at], before_ref[at])
            else:
                next_ref[at] = value
                win_ref[at] = window.astype(jnp.bfloat16)


def step_latent(flags, parts, own, far, base, step_dt, width):
    rows = own.shape[1]
    window = jax.ShapeDtypeStruct((rows, 16 * LAT_C), jnp.bfloat16)
    return pl.pallas_call(
        functools.partial(latent_kernel, len(parts), width, rows // PATCH),
        out_shape=[jax.ShapeDtypeStruct((rows, LAT), jnp.float32), window, window, window],
        in_specs=[SM, SM] + [VM] * (len(parts) + 3),
        out_specs=[VM] * 4,
        name="latent",
    )(flags, step_dt, *parts, own, far, base)


def text_kernel(at_ref, id_ref, table_hbm, out_ref, buf, sem):
    count = id_ref.shape[0]

    def block(n):
        start = pl.multiple_of((id_ref[n] // 128) * 128, 128)
        return pltpu.make_async_copy(table_hbm.at[:, pl.ds(start, 128)], buf.at[n], sem)

    def fetch(n, carry):
        block(n).start()
        return carry

    lax.fori_loop(0, count, fetch, 0)
    pltpu.make_async_copy(buf, buf, sem).wait()
    width = buf.shape[1]
    _, lane = grid_iota(width, 128)

    def add(n, acc):
        return acc + jnp.where(lane == id_ref[n] % 128, buf[n].astype(jnp.float32), 0.0)

    acc = lax.fori_loop(0, count, add, jnp.zeros((width, 128), jnp.float32))
    own = lax.dot_general(
        jnp.ones((8, 128), jnp.float32),
        acc,
        (((1,), (1,)), ((), ())),
        precision=highest,
        preferred_element_type=jnp.float32,
    )
    row, col = grid_iota(width, out_ref.shape[1])
    spot = jnp.where(col == row + at_ref[0], 1.0, 0.0)
    placed = jnp.dot(own, spot, precision=highest, preferred_element_type=jnp.float32)
    out_ref[...] = placed[:1] * np.float32(1.0 / count)


def text_mean(at, ids, table):
    width = table.shape[0]
    return pl.pallas_call(
        text_kernel,
        out_shape=jax.ShapeDtypeStruct((1, TEXT_W), jnp.float32),
        in_specs=[SM, SM, ANY],
        out_specs=VM,
        scratch_shapes=[
            pltpu.VMEM((ids.shape[0], width, 128), jnp.bfloat16),
            pltpu.SemaphoreType.DMA,
        ],
        name="text",
    )(at, ids, table)


def decode_kernel(
    frames,
    lead_ref,
    far_ref,
    near_ref,
    own_ref,
    w1_ref,
    b1_ref,
    gain_ref,
    b2_ref,
    pg_ref,
    post_ref,
    w2_hbm,
    pw_hbm,
    proj_hbm,
    out_ref,
    sent_ref,
    w2_s,
    pw_s,
    proj_s,
    win_s,
    x_s,
    sem,
):
    taps = 9 * CH
    w2_copy = pltpu.make_async_copy(w2_hbm, w2_s, sem.at[0])
    pw_copy = pltpu.make_async_copy(pw_hbm, pw_s, sem.at[1])
    w2_copy.start()
    pw_copy.start()
    proj_copy = pltpu.make_async_copy(proj_hbm, proj_s, sem.at[2])
    proj_copy.start()
    rows = frames * PATCH
    for n, r in enumerate((far_ref, near_ref, own_ref)):
        win_s[n * rows : (n + 1) * rows] = r[...]
    wide = frames + 2
    skip = 3 * frames - wide - 2
    cols = 16 * LAT_C
    firsts = []
    for q in range(4):
        acc = jnp.zeros((wide * PATCH, CH), jnp.float32)
        for t in range(3):
            acc = acc + jnp.dot(
                win_s[(skip + t) * PATCH : (skip + t + wide) * PATCH],
                w1_ref[t * cols : (t + 1) * cols, q * CH : (q + 1) * CH],
                preferred_element_type=jnp.float32,
            )
        first = (acc + b1_ref[...]).astype(jnp.bfloat16).astype(jnp.float32)
        firsts.append(first[2 * PATCH :])
        mean = jnp.mean(first * first, axis=-1, keepdims=True)
        v = first * lax.rsqrt(mean + 1e-06) * gain_ref[...]
        act = v / (1.0 + jnp.exp(-v))
        row = lax.broadcasted_iota(jnp.int32, (wide * PATCH, 1), 0)
        act = jnp.where((row >= 2 * PATCH) | (lead_ref[0] == 0), act, 0.0).astype(jnp.bfloat16)
        a, b = q // 2, q % 2
        da, db = (1, -1)[a], (1, -1)[b]
        moves = jnp.concatenate(
            [move_matrix(da, 0), move_matrix(0, db), move_matrix(da, db)], axis=0
        )
        for f in range(wide):
            plane = act[f * PATCH : (f + 1) * PATCH]
            moved = jnp.dot(
                moves, plane, preferred_element_type=jnp.float32
            ).astype(jnp.bfloat16)
            pieces = {
                (0, 0): plane,
                (1, 0): moved[:PATCH],
                (0, 1): moved[PATCH : 2 * PATCH],
                (1, 1): moved[2 * PATCH :],
            }
            for (ma, mb), piece in pieces.items():
                u = WINDOW.index(((1, -1)[a] if ma else 0, a))
                w = WINDOW.index(((1, -1)[b] if mb else 0, b))
                for oa in (0, 1):
                    for ob in (0, 1):
                        dy, dz = u - oa, w - ob
                        if 0 <= dy < 3 and 0 <= dz < 3:
                            at = (f * 4 + 2 * oa + ob) * PATCH
                            tap = (3 * dy + dz) * CH
                            x_s[at : at + PATCH, tap : tap + CH] = piece
    w2_copy.wait()
    block = 4 * PATCH
    out = jnp.zeros((frames * block, CH), jnp.float32)
    for t in range(3):
        out = out + jnp.dot(
            x_s[t * block : (t + frames) * block],
            w2_s[t * taps : (t + 1) * taps],
            preferred_element_type=jnp.float32,
        )
    first = jnp.concatenate(
        [firsts[q][f * PATCH : (f + 1) * PATCH] for f in range(frames) for q in range(4)], axis=0
    )
    dec = (out + b2_ref[...] + first).astype(jnp.bfloat16)
    order = order_matrix()
    for f in range(frames):
        out_ref[f * block : (f + 1) * block] = jnp.dot(
            order, dec[f * block : (f + 1) * block], preferred_element_type=jnp.float32
        ).astype(jnp.bfloat16)
    pw_copy.wait()
    emb = jnp.zeros((rows, pw_s.shape[1]), jnp.float32)
    for q in range(4):
        lhs = jnp.concatenate(
            [dec[(f * 4 + q) * PATCH : (f * 4 + q + 1) * PATCH] for f in range(frames)], axis=0
        )
        emb = emb + jnp.dot(
            lhs, pw_s[q * CH : (q + 1) * CH], preferred_element_type=jnp.float32
        )
    emb = emb.astype(jnp.bfloat16).astype(jnp.float32)
    centered = emb - jnp.mean(emb, axis=-1, keepdims=True)
    variance = jnp.mean(centered * centered, axis=-1, keepdims=True)
    normed = centered * lax.rsqrt(variance + 1e-05) * pg_ref[...]
    pooled = jnp.concatenate(
        [
            jnp.mean(normed[f * PATCH : (f + 1) * PATCH], axis=0, keepdims=True)
            for f in range(frames)
        ],
        axis=0,
    )
    centered = pooled - jnp.mean(pooled, axis=-1, keepdims=True)
    variance = jnp.mean(centered * centered, axis=-1, keepdims=True)
    vec = centered * lax.rsqrt(variance + 1e-05) * post_ref[...]
    columns = jnp.transpose(
        jnp.concatenate([vec, jnp.zeros((8 - frames, vec.shape[1]), jnp.float32)], axis=0)
    )
    proj_copy.wait()
    for f in range(frames):
        row = jnp.sum(columns[:, f : f + 1] * proj_s[...], axis=0, keepdims=True)
        for n in range(sent_ref.shape[0]):
            sent_ref[n, f : f + 1, :] = row


def window_weight(weight):
    taps = weight.reshape(3, 3, 3, LAT_C, CH)
    grown = [
        jnp.pad(taps, ((0, 0), (a, 1 - a), (b, 1 - b), (0, 0), (0, 0))).reshape(-1, CH)
        for a in (0, 1)
        for b in (0, 1)
    ]
    return jnp.concatenate(grown, axis=1)


def decode(
    lead, far, near, own, w1, b1, gain, w2, b2, pw, patch_gain, post_gain, proj, devices
):
    rows = own.shape[0]
    frames = rows // PATCH
    wide = frames + 2
    return pl.pallas_call(
        functools.partial(decode_kernel, frames),
        out_shape=[
            jax.ShapeDtypeStruct((frames * 4 * PATCH, CH), jnp.bfloat16),
            jax.ShapeDtypeStruct((devices, frames, proj.shape[1]), jnp.float32),
        ],
        in_specs=[SM] + [VM] * 9 + [ANY, ANY, ANY],
        out_specs=[VM, VM],
        scratch_shapes=[
            pltpu.VMEM(w2.shape, jnp.bfloat16),
            pltpu.VMEM(pw.shape, jnp.bfloat16),
            pltpu.VMEM(proj.shape, jnp.float32),
            pltpu.VMEM((3 * rows, 16 * LAT_C), jnp.bfloat16),
            pltpu.VMEM((wide * 4 * PATCH, 9 * CH), jnp.bfloat16),
            pltpu.SemaphoreType.DMA((3,)),
        ],
        name="decode",
    )(
        lead,
        far,
        near,
        own,
        w1,
        b1,
        gain,
        b2,
        patch_gain,
        post_gain,
        w2,
        pw,
        proj,
    )


def rate_kernel(frames, slot_ref, text_ref, got_ref, vec_ref, score_ref):
    text = text_ref[...]
    text_rms = jnp.sqrt(jnp.mean(text * text) + 1e-06)
    for f in range(frames):
        slot = slot_ref[f]
        block = got_ref[slot // frames]
        row = block[:1]
        for n in range(1, frames):
            row = jnp.where(slot % frames == n, block[n : n + 1], row)
        vec_ref[f : f + 1] = row
        inner = jnp.sum(row * text)
        image_rms = jnp.sqrt(jnp.mean(row * row) + 1e-06)
        score_ref[f] = 100.0 * inner / (TEXT_W * image_rms * text_rms)


def rate(slots, text, got):
    frames = slots.shape[0]
    return pl.pallas_call(
        functools.partial(rate_kernel, frames),
        out_shape=[
            jax.ShapeDtypeStruct((frames, got.shape[2]), jnp.float32),
            jax.ShapeDtypeStruct((frames,), jnp.float32),
        ],
        in_specs=[SM, VM, VM],
        out_specs=[VM, SM],
        name="rate",
    )(slots, text, got)


def local(
    queries,
    keys,
    values,
    latent_in,
    mod_table,
    step_size,
    timestep,
    head_weight,
    conv_in_weight,
    conv_in_bias,
    norm_gain,
    conv_weight,
    conv_bias,
    patch_weight,
    patch_gain,
    post_gain,
    proj_weight,
    text_table,
    prompt_ids,
    frame_order,
):
    rows, width = queries.shape
    devices = lax.axis_size("seq")
    chips = devices // 2
    cols = width // chips
    heads = cols // HD
    frames = rows // PATCH
    me = lax.axis_index("seq")
    chip, core = me // 2, me % 2

    tail = max(1, heads // 2)
    phases = (heads - tail, tail) if heads > tail else (tail,)
    firsts = [sum(phases[:n]) for n in range(len(phases))]

    order = sorted(range(1, chips), key=lambda t: abs(2 * t - chips))

    def packed(first, count):
        at = ((chip + jnp.arange(chips)) % chips) * cols + first * HD
        return pack(keys, values, queries, at.astype(jnp.int32), count * HD)

    blocks = packed(firsts[0], phases[0])
    got = [blocks[0]] * chips
    for turn in order:
        got[turn] = rotate(blocks[turn], "seq", turn)
    scale = lax.dynamic_slice_in_dim(mod_table[:, 1, :], chip * cols, cols, 1)
    scale = scale.reshape(-1, heads, 1, HD)
    weight = lax.dynamic_slice_in_dim(head_weight, chip * cols, cols, 0).reshape(heads, HD, LAT)
    weight = jnp.pad(weight, ((0, 0), (0, 0), (0, 128 - LAT)))
    origin = 2 * ((chip - jnp.arange(chips)) % chips) + core
    steps = jnp.take(timestep.reshape(devices, frames), origin, axis=0).reshape(-1)
    near_steps = jnp.stack(
        [
            lax.dynamic_slice_in_dim(timestep, at * frames, frames, 0)
            for at in (me, jnp.maximum(me - 2, 0))
        ]
    ).reshape(-1)
    base = jnp.dot(jnp.take(mod_table[:, 0, :], near_steps, axis=0), head_weight, precision=highest)
    step_dt = jnp.take(step_size, near_steps)
    text_row = text_mean(
        (me * text_table.shape[1]).astype(jnp.int32).reshape(1), prompt_ids, text_table.T
    )
    slots = lax.dynamic_slice_in_dim(frame_order, me * frames, frames, 0)
    prepared = dict(
        scales=[scale[:, f : f + n] for f, n in zip(firsts, phases)],
        weights=[weight[f : f + n] for f, n in zip(firsts, phases)],
        steps=steps,
        base=base,
        step_dt=step_dt,
        text=text_row,
        slots=slots,
        w1=window_weight(conv_in_weight),
        b1=conv_in_bias.reshape(1, -1),
        gain=norm_gain.reshape(1, -1),
        b2=conv_bias.reshape(1, -1),
        patch_gain=patch_gain.reshape(1, -1),
        post_gain=post_gain.reshape(1, -1),
        lead=(me == 0).astype(jnp.int32).reshape(1),
        flags=jnp.stack([chip == 0, core]).astype(jnp.int32),
        later=[packed(f, n) for f, n in zip(firsts[1:], phases[1:])],
    )
    words = jnp.broadcast_to(prepared["text"][None], (devices, 1, TEXT_W))
    words = lax.all_to_all(words, "seq", split_axis=0, concat_axis=0, tiled=True)
    words = jnp.sum(words, axis=0)
    far_latent = rotate(latent_in.T, "seq", 1)
    steps, words, far_latent = lax.optimization_barrier((prepared["steps"], words, far_latent))
    phase_blocks = [got]
    for gate, blocks in zip(GATES, prepared["later"]):
        before = phase_blocks[0][order[min(gate, len(order) - 1)]]
        blocks, _ = lax.optimization_barrier((blocks, before))
        got = [blocks[0]] * chips
        for turn in order:
            got[turn] = rotate(blocks[turn], "seq", turn)
        phase_blocks.append(got)
    sums = []
    for n, got in enumerate(phase_blocks):
        if n:
            sums[-1], *got = lax.optimization_barrier((sums[-1], *got))
        other = [swap_core(block, "seq") for block in got]
        last = n + 1 == len(phase_blocks)
        shares = attend(
            got,
            other,
            steps,
            prepared["scales"][n],
            prepared["weights"][n],
            sums if last else [],
            last,
        )
        if not last:
            sums.append(shares)
    parts = [shares[0]] + [rotate(shares[t], "seq", chips - t) for t in order]

    latent_next, window, far, passed = step_latent(
        prepared["flags"],
        parts,
        latent_in.T,
        far_latent,
        prepared["base"],
        prepared["step_dt"],
        width,
    )
    near = swap_core(passed, "seq")
    decoded, sent = decode(
        prepared["lead"],
        far,
        near,
        window,
        prepared["w1"],
        prepared["b1"],
        prepared["gain"],
        conv_weight.reshape(-1, CH),
        prepared["b2"],
        patch_weight,
        prepared["patch_gain"],
        prepared["post_gain"],
        proj_weight,
        devices,
    )
    decoded = decoded.reshape(frames, 2 * GRID_H, 2 * GRID_W, CH)
    spread = lax.all_to_all(sent, "seq", split_axis=0, concat_axis=0, tiled=True)
    image_vec, scores = rate(prepared["slots"], words, spread)
    return (latent_next, decoded, image_vec, scores)


def solution(mesh):
    in_specs = (
        P(("grp", "seq"), None),
        P(("grp", "seq"), None),
        P(("grp", "seq"), None),
        P(("grp", "seq"), None),
        P(),
        P(),
        P("grp"),
        P(),
        P(),
        P(),
        P(),
        P(),
        P(),
        P(),
        P(),
        P(),
        P(),
        P(None, "seq"),
        P("grp"),
        P("grp"),
    )
    out_specs = (
        P(("grp", "seq"), None),
        P(("grp", "seq"), None, None, None),
        P(("grp", "seq"), None),
        P(("grp", "seq")),
    )

    return jax.shard_map(local, mesh=mesh, in_specs=in_specs, out_specs=out_specs, check_vma=False)
```

```python
import functools

import jax
import jax.numpy as jnp
import numpy as np
from jax import lax
from jax.experimental import pallas as pl
from jax.experimental.pallas import tpu as pltpu
from jax.sharding import PartitionSpec as P

GRID_H = 8
GRID_W = 12
PATCH = GRID_H * GRID_W
HD = 128
LAT = 64
LAT_C = 16
CH = 384
TEXT_W = 768
KEY_CHUNK = 256
GATES = (1,)


highest = lax.Precision.HIGHEST
VM = pl.BlockSpec(memory_space=pltpu.VMEM)
SM = pl.BlockSpec(memory_space=pltpu.SMEM)
ANY = pl.BlockSpec(memory_space=pl.ANY)


def rotate(value, axis, steps):
    count = lax.axis_size(axis)
    return lax.ppermute(value, axis, [(i, (i + 2 * steps) % count) for i in range(count)])


def swap_core(value, axis):
    count = lax.axis_size(axis)
    return lax.ppermute(value, axis, [(i, i ^ 1) for i in range(count)])


def pack_kernel(blocks, at_ref, k_hbm, v_hbm, q_hbm, *refs):
    out_refs, (buf, in_sem, out_sem) = refs[:blocks], refs[blocks:]
    width = buf.shape[3]
    gets = []
    for n in range(blocks):
        at = pl.multiple_of(at_ref[n], HD)
        gets.append(
            [
                pltpu.make_async_copy(src.at[:, pl.ds(at, width)], buf.at[n, i], in_sem.at[n, i])
                for i, src in enumerate((k_hbm, v_hbm, q_hbm))
            ]
        )
        for get in gets[-1]:
            get.start()
    puts = [
        pltpu.make_async_copy(buf.at[n], out_refs[n], out_sem.at[n]) for n in range(blocks)
    ]
    for n in range(blocks):
        for get in gets[n]:
            get.wait()
        puts[n].start()
    for put in puts:
        put.wait()


def pack(keys, values, queries, starts, width):
    rows, blocks = keys.shape[0], starts.shape[0]
    return pl.pallas_call(
        functools.partial(pack_kernel, blocks),
        out_shape=[jax.ShapeDtypeStruct((3, rows, width), jnp.bfloat16)] * blocks,
        in_specs=[SM, ANY, ANY, ANY],
        out_specs=[ANY] * blocks,
        scratch_shapes=[
            pltpu.VMEM((blocks, 3, rows, width), jnp.bfloat16),
            pltpu.SemaphoreType.DMA((blocks, 3)),
            pltpu.SemaphoreType.DMA((blocks,)),
        ],
        name="pack",
    )(starts, keys, values, queries)


def attend_kernel(blocks, heads, frames, earlier, last, t_ref, sc_ref, w_ref, *refs):
    prev_refs, refs = refs[:earlier], refs[earlier:]
    near_refs, far_refs, refs = refs[:blocks], refs[blocks : 2 * blocks], refs[2 * blocks :]
    if last:
        out_refs, refs = refs[:blocks], refs[blocks:]
    else:
        sum_ref, refs = refs[0], refs[1:]
    q_s, k_s, v_s, s_a, s_b, m_a, m_b, acc_s, tot_s, sem, q_sem = refs[:11]
    if last:
        sum_ref, prev_s, prev_sem = refs[11:]
    sources = near_refs + far_refs
    rows = near_refs[0].shape[1]
    keys = len(sources) * rows
    scale = np.float32(HD**-0.5 * np.log2(np.e))

    def fetch(h, which):
        dst = (k_s, v_s)[which]
        for j, src in enumerate(sources):
            pltpu.make_async_copy(
                src.at[which, :, pl.ds(h * HD, HD)],
                dst.at[h, pl.ds(j * rows, rows), :],
                sem.at[h, which],
            ).start()

    fetch(0, 0)
    for b in range(blocks):
        pltpu.make_async_copy(near_refs[b].at[2], q_s.at[b], q_sem).start()
    fetch(0, 1)
    for h in range(1, heads):
        fetch(h, 0)
        fetch(h, 1)
    gets = []
    for n, prev in enumerate(prev_refs):
        gets.append(pltpu.make_async_copy(prev, prev_s.at[n], prev_sem.at[n]))
        gets[-1].start()
    sum_ref[...] = jnp.zeros(sum_ref.shape, jnp.float32)

    def arrived(h, which):
        whole = (k_s, v_s)[which].at[h]
        pltpu.make_async_copy(whole, whole, sem.at[h, which]).wait()

    def logits(h, b, at, s_ref, peak):
        q = q_s[b, :, pl.ds(pl.multiple_of(h * HD, HD), HD)]
        s = lax.dot_general(
            q,
            k_s[h, at : at + KEY_CHUNK, :],
            (((1,), (1,)), ((), ())),
            preferred_element_type=jnp.float32,
        )
        s_ref[:, at : at + KEY_CHUNK] = s
        folded = functools.reduce(
            jnp.maximum, [s[:, i : i + 128] for i in range(0, KEY_CHUNK, 128)]
        )
        return folded if peak is None else jnp.maximum(peak, folded)

    def keep_peak(peak, m_ref):
        m_ref[...] = jnp.broadcast_to(jnp.max(peak, axis=-1, keepdims=True) * scale, m_ref.shape)

    def finish(h, b, acc, total):
        o = acc / jnp.sum(total, axis=-1, keepdims=True)
        o = o.astype(jnp.bfloat16).astype(jnp.float32)
        square = jnp.sum(o * o, axis=-1, keepdims=True)
        per = rows // frames
        scaled = jnp.concatenate(
            [
                o[f * per : (f + 1) * per] * (1.0 + sc_ref[t_ref[b * frames + f], h])
                for f in range(frames)
            ],
            axis=0,
        )
        part = jnp.dot(scaled, w_ref[h], precision=highest, preferred_element_type=jnp.float32)
        lane = lax.broadcasted_iota(jnp.int32, part.shape, 1)
        return part + jnp.where(lane >= LAT, square, 0.0)

    def one_unit(h, now, top_ref, next_h, next_b, later, later_top_ref):
        top = top_ref[...]
        peak, total = None, None
        acc = jnp.zeros((rows, HD), jnp.float32)
        for at in chunks:
            peak = logits(next_h, next_b, at, later, peak)
            weights = []
            for i in range(at, at + KEY_CHUNK, 128):
                e = jnp.exp2(now[:, i : i + 128] * scale - top)
                total = e if total is None else total + e
                weights.append(e.astype(jnp.bfloat16))
            acc = acc + jnp.dot(
                jnp.concatenate(weights, axis=1),
                v_s[h, at : at + KEY_CHUNK, :],
                preferred_element_type=jnp.float32,
            )
        keep_peak(peak, later_top_ref)
        return acc, total

    chunks = range(0, keys, KEY_CHUNK)
    pltpu.make_async_copy(q_s, q_s, q_sem).wait()
    arrived(0, 0)
    peak = None
    for at in chunks:
        peak = logits(0, 0, at, s_a, peak)
    keep_peak(peak, m_a)
    pairs = blocks // 2
    acc_s[...] = jnp.zeros(acc_s.shape, jnp.float32)
    tot_s[...] = jnp.ones(tot_s.shape, jnp.float32)

    def one_pair(n, carry):
        h, p = n // pairs, n % pairs
        after = jnp.minimum(n + 1, heads * pairs - 1)
        after_h, after_p = after // pairs, after % pairs
        before = jnp.maximum(n - 1, 0)
        before_h, before_p = before // pairs, before % pairs

        @pl.when(p == 0)
        def _():
            arrived(h, 1)

        @pl.when(after_h > h)
        def _():
            arrived(after_h, 0)

        late = finish(before_h, 2 * before_p + 1, acc_s[...], tot_s[...])
        sum_ref[2 * before_p + 1] = sum_ref[2 * before_p + 1] + late
        even = one_unit(h, s_a, m_a, h, 2 * p + 1, s_b, m_b)
        sum_ref[2 * p] = sum_ref[2 * p] + finish(h, 2 * p, *even)
        acc, total = one_unit(h, s_b, m_b, after_h, 2 * after_p, s_a, m_a)
        acc_s[...] = acc
        tot_s[...] = total
        return carry

    lax.fori_loop(0, heads * pairs, one_pair, 0)
    sum_ref[blocks - 1] = sum_ref[blocks - 1] + finish(
        heads - 1, blocks - 1, acc_s[...], tot_s[...]
    )
    if last:
        for get in gets:
            get.wait()
        row, lane = grid_iota(8, 128)
        pick = jnp.where(lane == LAT, 1.0, 0.0)
        for b in range(blocks):
            share = sum_ref[b]
            for n in range(earlier):
                share = share + prev_s[n, b]
            half = PATCH + 8 * frames
            spots = ((out_refs[b], 0), (out_refs[(b - 1) % blocks], half))
            beside = jnp.concatenate(
                [share[f * PATCH : (f + 1) * PATCH, :LAT] for f in range(frames)], axis=1
            ).astype(jnp.bfloat16)
            for ref, at in spots:
                ref[at : at + PATCH] = beside
            for f in range(frames):
                square = lax.dot_general(
                    pick,
                    share[f * PATCH : (f + 1) * PATCH],
                    (((1,), (1,)), ((), ())),
                    precision=highest,
                    preferred_element_type=jnp.float32,
                )
                square = jnp.concatenate(
                    [square, jnp.zeros((8, 128 - PATCH), jnp.float32)], axis=1
                )
                high = square.astype(jnp.bfloat16).astype(jnp.float32)
                both = jnp.where(row == 0, high, jnp.where(row == 1, square - high, 0.0))
                for ref, at in spots:
                    at = at + PATCH + 8 * f
                    ref[at : at + 8] = both.astype(jnp.bfloat16)


def attend(near, far, steps, scale, weight, earlier, last):
    blocks = len(near)
    _, rows, cols = near[0].shape
    heads, keys = cols // HD, 2 * blocks * rows
    frames = rows // PATCH
    sums = (blocks, rows, 128)
    if last:
        share = (2 * (PATCH + 8 * frames), frames * LAT)
        out_shape = [jax.ShapeDtypeStruct(share, jnp.bfloat16)] * blocks
        out_specs = [VM] * blocks
    else:
        out_shape, out_specs = jax.ShapeDtypeStruct(sums, jnp.float32), VM
    return pl.pallas_call(
        functools.partial(attend_kernel, blocks, heads, frames, len(earlier), last),
        out_shape=out_shape,
        in_specs=[SM, VM, VM] + [ANY] * (len(earlier) + 2 * blocks),
        out_specs=out_specs,
        scratch_shapes=[
            pltpu.VMEM((blocks, rows, cols), jnp.bfloat16),
            pltpu.VMEM((heads, keys, HD), jnp.bfloat16),
            pltpu.VMEM((heads, keys, HD), jnp.bfloat16),
            pltpu.VMEM((rows, keys), jnp.float32),
            pltpu.VMEM((rows, keys), jnp.float32),
            pltpu.VMEM((rows, 128), jnp.float32),
            pltpu.VMEM((rows, 128), jnp.float32),
            pltpu.VMEM((rows, HD), jnp.float32),
            pltpu.VMEM((rows, 128), jnp.float32),
            pltpu.SemaphoreType.DMA((heads, 2)),
            pltpu.SemaphoreType.DMA,
        ]
        + [
            pltpu.VMEM(sums, jnp.float32),
            pltpu.VMEM((max(1, len(earlier)),) + sums, jnp.float32),
            pltpu.SemaphoreType.DMA((max(1, len(earlier)),)),
        ]
        * last,
        cost_estimate=pl.CostEstimate(
            flops=4 * blocks * rows * keys * cols,
            bytes_accessed=4 * keys * cols,
            transcendentals=blocks * rows * keys * heads,
        ),
        name="attend",
    )(steps, scale, weight, *earlier, *near, *far)


WINDOW = ((-1, 1), (0, 0), (0, 1), (1, 0))


OFFSETS = [(di, dj) for di in (-1, 0, 1) for dj in (-1, 0, 1)]


def grid_iota(rows, cols):
    shape = (rows, cols)
    return lax.broadcasted_iota(jnp.int32, shape, 0), lax.broadcasted_iota(jnp.int32, shape, 1)


def over(value, count):
    return jnp.floor((value.astype(jnp.float32) + 0.5) * np.float32(1.0 / count)).astype(jnp.int32)


def as_matrix(hit):
    return jnp.where(hit, 1.0, 0.0).astype(jnp.bfloat16)


def move_matrix(di, dj, cols=PATCH):
    row, col = grid_iota(PATCH, cols)
    j = row - GRID_W * over(row, GRID_W)
    inside = (j + dj >= 0) & (j + dj < GRID_W) & (col < PATCH)
    return as_matrix((col - row == GRID_W * di + dj) & inside)


def place_matrix(di, dj):
    row, col = grid_iota(LAT, 16 * LAT_C)
    u, w, c = col >> 6, (col >> 4) & 3, col & 15
    source = 2 * LAT_C * (1 - (u & 1)) + LAT_C * (1 - (w & 1)) + c

    def seen(at, step):
        return {-1: at == 0, 0: (at == 1) | (at == 2), 1: at == 3}[step]

    return as_matrix((row == source) & seen(u, di) & seen(w, dj))


def order_matrix():
    row, col = grid_iota(4 * PATCH, 4 * PATCH)
    y = over(row, 2 * GRID_W)
    z = row - 2 * GRID_W * y
    source = (2 * (y & 1) + (z & 1)) * PATCH + (y >> 1) * GRID_W + (z >> 1)
    return as_matrix(col == source)


def latent_kernel(parts, width, frames, flag_ref, dt_ref, *refs):
    part_refs, refs = refs[:parts], refs[parts:]
    own_ref, far_ref, base_ref, next_ref, win_ref, before_ref, pass_ref = refs
    total = part_refs[0][...].astype(jnp.float32)
    for r in part_refs[1:]:
        total = total + r[...].astype(jnp.float32)
    row, _ = grid_iota(8, 128)
    pick = jnp.where(row < 2, 1.0, 0.0)
    cols = 16 * LAT_C
    moves = jnp.concatenate([move_matrix(di, dj, 128) for di, dj in OFFSETS], axis=1)
    places = jnp.concatenate([place_matrix(di, dj) for di, dj in OFFSETS], axis=1)
    none = jnp.zeros((128 - PATCH, cols), jnp.bfloat16)
    first_chip, core = flag_ref[0], flag_ref[1]
    for side, latent in enumerate((jnp.transpose(own_ref[...]), jnp.transpose(far_ref[...]))):
        skip = side * (PATCH + 8 * frames)
        for f in range(frames):
            at = slice(f * PATCH, (f + 1) * PATCH)
            squares = total[skip + PATCH + 8 * f : skip + PATCH + 8 * (f + 1)]
            square = lax.dot_general(
                squares,
                pick,
                (((0,), (0,)), ((), ())),
                precision=highest,
                preferred_element_type=jnp.float32,
            )[:PATCH, :LAT]
            inverse = lax.rsqrt(square * np.float32(1.0 / width) + 1e-06)
            scaled = total[skip : skip + PATCH, f * LAT : (f + 1) * LAT] * inverse
            g = side * frames + f
            value = latent[at] + dt_ref[g] * (scaled + base_ref[g : g + 1])
            spread = jnp.dot(
                value.astype(jnp.bfloat16), places, preferred_element_type=jnp.float32
            ).astype(jnp.bfloat16)
            stacked = jnp.concatenate(
                [x for o in range(len(OFFSETS)) for x in (spread[:, o * cols : (o + 1) * cols], none)],
                axis=0,
            )
            window = jnp.dot(moves, stacked, preferred_element_type=jnp.float32)
            if side:
                window = jnp.where(first_chip == 1, 0.0, window)
                before_ref[at] = window.astype(jnp.bfloat16)
                pass_ref[at] = jnp.where(core == 0, win_ref[at], before_ref[at])
            else:
                next_ref[at] = value
                win_ref[at] = window.astype(jnp.bfloat16)


def step_latent(flags, parts, own, far, base, step_dt, width):
    rows = own.shape[1]
    window = jax.ShapeDtypeStruct((rows, 16 * LAT_C), jnp.bfloat16)
    return pl.pallas_call(
        functools.partial(latent_kernel, len(parts), width, rows // PATCH),
        out_shape=[jax.ShapeDtypeStruct((rows, LAT), jnp.float32), window, window, window],
        in_specs=[SM, SM] + [VM] * (len(parts) + 3),
        out_specs=[VM] * 4,
        name="latent",
    )(flags, step_dt, *parts, own, far, base)


def text_kernel(at_ref, id_ref, table_hbm, out_ref, buf, sem):
    count = id_ref.shape[0]

    def block(n):
        start = pl.multiple_of((id_ref[n] // 128) * 128, 128)
        return pltpu.make_async_copy(table_hbm.at[:, pl.ds(start, 128)], buf.at[n], sem)

    def fetch(n, carry):
        block(n).start()
        return carry

    lax.fori_loop(0, count, fetch, 0)
    pltpu.make_async_copy(buf, buf, sem).wait()
    width = buf.shape[1]
    _, lane = grid_iota(width, 128)

    def add(n, acc):
        return acc + jnp.where(lane == id_ref[n] % 128, buf[n].astype(jnp.float32), 0.0)

    acc = lax.fori_loop(0, count, add, jnp.zeros((width, 128), jnp.float32))
    own = lax.dot_general(
        jnp.ones((8, 128), jnp.float32),
        acc,
        (((1,), (1,)), ((), ())),
        precision=highest,
        preferred_element_type=jnp.float32,
    )
    row, col = grid_iota(width, out_ref.shape[1])
    spot = jnp.where(col == row + at_ref[0], 1.0, 0.0)
    placed = jnp.dot(own, spot, precision=highest, preferred_element_type=jnp.float32)
    out_ref[...] = placed[:1] * np.float32(1.0 / count)


def text_mean(at, ids, table):
    width = table.shape[0]
    return pl.pallas_call(
        text_kernel,
        out_shape=jax.ShapeDtypeStruct((1, TEXT_W), jnp.float32),
        in_specs=[SM, SM, ANY],
        out_specs=VM,
        scratch_shapes=[
            pltpu.VMEM((ids.shape[0], width, 128), jnp.bfloat16),
            pltpu.SemaphoreType.DMA,
        ],
        name="text",
    )(at, ids, table)


def decode_kernel(
    frames,
    lead_ref,
    far_ref,
    near_ref,
    own_ref,
    w1_ref,
    b1_ref,
    gain_ref,
    b2_ref,
    pg_ref,
    post_ref,
    w2_hbm,
    pw_hbm,
    proj_hbm,
    out_ref,
    sent_ref,
    w2_s,
    pw_s,
    proj_s,
    win_s,
    x_s,
    sem,
):
    taps = 9 * CH
    w2_copy = pltpu.make_async_copy(w2_hbm, w2_s, sem.at[0])
    pw_copy = pltpu.make_async_copy(pw_hbm, pw_s, sem.at[1])
    w2_copy.start()
    pw_copy.start()
    proj_copy = pltpu.make_async_copy(proj_hbm, proj_s, sem.at[2])
    proj_copy.start()
    rows = frames * PATCH
    for n, r in enumerate((far_ref, near_ref, own_ref)):
        win_s[n * rows : (n + 1) * rows] = r[...]
    wide = frames + 2
    skip = 3 * frames - wide - 2
    cols = 16 * LAT_C
    firsts = []
    for q in range(4):
        acc = jnp.zeros((wide * PATCH, CH), jnp.float32)
        for t in range(3):
            acc = acc + jnp.dot(
                win_s[(skip + t) * PATCH : (skip + t + wide) * PATCH],
                w1_ref[t * cols : (t + 1) * cols, q * CH : (q + 1) * CH],
                preferred_element_type=jnp.float32,
            )
        first = (acc + b1_ref[...]).astype(jnp.bfloat16).astype(jnp.float32)
        firsts.append(first[2 * PATCH :])
        mean = jnp.mean(first * first, axis=-1, keepdims=True)
        v = first * lax.rsqrt(mean + 1e-06) * gain_ref[...]
        act = v / (1.0 + jnp.exp(-v))
        row = lax.broadcasted_iota(jnp.int32, (wide * PATCH, 1), 0)
        act = jnp.where((row >= 2 * PATCH) | (lead_ref[0] == 0), act, 0.0).astype(jnp.bfloat16)
        a, b = q // 2, q % 2
        da, db = (1, -1)[a], (1, -1)[b]
        moves = jnp.concatenate(
            [move_matrix(da, 0), move_matrix(0, db), move_matrix(da, db)], axis=0
        )
        for f in range(wide):
            plane = act[f * PATCH : (f + 1) * PATCH]
            moved = jnp.dot(
                moves, plane, preferred_element_type=jnp.float32
            ).astype(jnp.bfloat16)
            pieces = {
                (0, 0): plane,
                (1, 0): moved[:PATCH],
                (0, 1): moved[PATCH : 2 * PATCH],
                (1, 1): moved[2 * PATCH :],
            }
            for (ma, mb), piece in pieces.items():
                u = WINDOW.index(((1, -1)[a] if ma else 0, a))
                w = WINDOW.index(((1, -1)[b] if mb else 0, b))
                for oa in (0, 1):
                    for ob in (0, 1):
                        dy, dz = u - oa, w - ob
                        if 0 <= dy < 3 and 0 <= dz < 3:
                            at = (f * 4 + 2 * oa + ob) * PATCH
                            tap = (3 * dy + dz) * CH
                            x_s[at : at + PATCH, tap : tap + CH] = piece
    w2_copy.wait()
    block = 4 * PATCH
    out = jnp.zeros((frames * block, CH), jnp.float32)
    for t in range(3):
        out = out + jnp.dot(
            x_s[t * block : (t + frames) * block],
            w2_s[t * taps : (t + 1) * taps],
            preferred_element_type=jnp.float32,
        )
    first = jnp.concatenate(
        [firsts[q][f * PATCH : (f + 1) * PATCH] for f in range(frames) for q in range(4)], axis=0
    )
    dec = (out + b2_ref[...] + first).astype(jnp.bfloat16)
    order = order_matrix()
    for f in range(frames):
        out_ref[f * block : (f + 1) * block] = jnp.dot(
            order, dec[f * block : (f + 1) * block], preferred_element_type=jnp.float32
        ).astype(jnp.bfloat16)
    pw_copy.wait()
    emb = jnp.zeros((rows, pw_s.shape[1]), jnp.float32)
    for q in range(4):
        lhs = jnp.concatenate(
            [dec[(f * 4 + q) * PATCH : (f * 4 + q + 1) * PATCH] for f in range(frames)], axis=0
        )
        emb = emb + jnp.dot(
            lhs, pw_s[q * CH : (q + 1) * CH], preferred_element_type=jnp.float32
        )
    emb = emb.astype(jnp.bfloat16).astype(jnp.float32)
    centered = emb - jnp.mean(emb, axis=-1, keepdims=True)
    variance = jnp.mean(centered * centered, axis=-1, keepdims=True)
    normed = centered * lax.rsqrt(variance + 1e-05) * pg_ref[...]
    pooled = jnp.concatenate(
        [
            jnp.mean(normed[f * PATCH : (f + 1) * PATCH], axis=0, keepdims=True)
            for f in range(frames)
        ],
        axis=0,
    )
    centered = pooled - jnp.mean(pooled, axis=-1, keepdims=True)
    variance = jnp.mean(centered * centered, axis=-1, keepdims=True)
    vec = centered * lax.rsqrt(variance + 1e-05) * post_ref[...]
    columns = jnp.transpose(
        jnp.concatenate([vec, jnp.zeros((8 - frames, vec.shape[1]), jnp.float32)], axis=0)
    )
    proj_copy.wait()
    for f in range(frames):
        row = jnp.sum(columns[:, f : f + 1] * proj_s[...], axis=0, keepdims=True)
        for n in range(sent_ref.shape[0]):
            sent_ref[n, f : f + 1, :] = row


def window_weight(weight):
    taps = weight.reshape(3, 3, 3, LAT_C, CH)
    grown = [
        jnp.pad(taps, ((0, 0), (a, 1 - a), (b, 1 - b), (0, 0), (0, 0))).reshape(-1, CH)
        for a in (0, 1)
        for b in (0, 1)
    ]
    return jnp.concatenate(grown, axis=1)


def decode(
    lead, far, near, own, w1, b1, gain, w2, b2, pw, patch_gain, post_gain, proj, devices
):
    rows = own.shape[0]
    frames = rows // PATCH
    wide = frames + 2
    return pl.pallas_call(
        functools.partial(decode_kernel, frames),
        out_shape=[
            jax.ShapeDtypeStruct((frames * 4 * PATCH, CH), jnp.bfloat16),
            jax.ShapeDtypeStruct((devices, frames, proj.shape[1]), jnp.float32),
        ],
        in_specs=[SM] + [VM] * 9 + [ANY, ANY, ANY],
        out_specs=[VM, VM],
        scratch_shapes=[
            pltpu.VMEM(w2.shape, jnp.bfloat16),
            pltpu.VMEM(pw.shape, jnp.bfloat16),
            pltpu.VMEM(proj.shape, jnp.float32),
            pltpu.VMEM((3 * rows, 16 * LAT_C), jnp.bfloat16),
            pltpu.VMEM((wide * 4 * PATCH, 9 * CH), jnp.bfloat16),
            pltpu.SemaphoreType.DMA((3,)),
        ],
        name="decode",
    )(
        lead,
        far,
        near,
        own,
        w1,
        b1,
        gain,
        b2,
        patch_gain,
        post_gain,
        w2,
        pw,
        proj,
    )


def rate_kernel(frames, slot_ref, text_ref, got_ref, vec_ref, score_ref):
    text = text_ref[...]
    text_rms = jnp.sqrt(jnp.mean(text * text) + 1e-06)
    for f in range(frames):
        slot = slot_ref[f]
        block = got_ref[slot // frames]
        row = block[:1]
        for n in range(1, frames):
            row = jnp.where(slot % frames == n, block[n : n + 1], row)
        vec_ref[f : f + 1] = row
        inner = jnp.sum(row * text)
        image_rms = jnp.sqrt(jnp.mean(row * row) + 1e-06)
        score_ref[f] = 100.0 * inner / (TEXT_W * image_rms * text_rms)


def rate(slots, text, got):
    frames = slots.shape[0]
    return pl.pallas_call(
        functools.partial(rate_kernel, frames),
        out_shape=[
            jax.ShapeDtypeStruct((frames, got.shape[2]), jnp.float32),
            jax.ShapeDtypeStruct((frames,), jnp.float32),
        ],
        in_specs=[SM, VM, VM],
        out_specs=[VM, SM],
        name="rate",
    )(slots, text, got)


def local(
    queries,
    keys,
    values,
    latent_in,
    mod_table,
    step_size,
    timestep,
    head_weight,
    conv_in_weight,
    conv_in_bias,
    norm_gain,
    conv_weight,
    conv_bias,
    patch_weight,
    patch_gain,
    post_gain,
    proj_weight,
    text_table,
    prompt_ids,
    frame_order,
):
    rows, width = queries.shape
    devices = lax.axis_size("seq")
    chips = devices // 2
    cols = width // chips
    heads = cols // HD
    frames = rows // PATCH
    me = lax.axis_index("seq")
    chip, core = me // 2, me % 2

    tail = max(1, heads // 2)
    phases = (heads - tail, tail) if heads > tail else (tail,)
    firsts = [sum(phases[:n]) for n in range(len(phases))]

    order = sorted(range(1, chips), key=lambda t: abs(2 * t - chips))

    def packed(first, count):
        at = ((chip + jnp.arange(chips)) % chips) * cols + first * HD
        return pack(keys, values, queries, at.astype(jnp.int32), count * HD)

    blocks = packed(firsts[0], phases[0])
    got = [blocks[0]] * chips
    for turn in order:
        got[turn] = rotate(blocks[turn], "seq", turn)
    scale = lax.dynamic_slice_in_dim(mod_table[:, 1, :], chip * cols, cols, 1)
    scale = scale.reshape(-1, heads, 1, HD)
    weight = lax.dynamic_slice_in_dim(head_weight, chip * cols, cols, 0).reshape(heads, HD, LAT)
    weight = jnp.pad(weight, ((0, 0), (0, 0), (0, 128 - LAT)))
    origin = 2 * ((chip - jnp.arange(chips)) % chips) + core
    steps = jnp.take(timestep.reshape(devices, frames), origin, axis=0).reshape(-1)
    near_steps = jnp.stack(
        [
            lax.dynamic_slice_in_dim(timestep, at * frames, frames, 0)
            for at in (me, jnp.maximum(me - 2, 0))
        ]
    ).reshape(-1)
    base = jnp.dot(jnp.take(mod_table[:, 0, :], near_steps, axis=0), head_weight, precision=highest)
    step_dt = jnp.take(step_size, near_steps)
    text_row = text_mean(
        (me * text_table.shape[1]).astype(jnp.int32).reshape(1), prompt_ids, text_table.T
    )
    slots = lax.dynamic_slice_in_dim(frame_order, me * frames, frames, 0)
    prepared = dict(
        scales=[scale[:, f : f + n] for f, n in zip(firsts, phases)],
        weights=[weight[f : f + n] for f, n in zip(firsts, phases)],
        steps=steps,
        base=base,
        step_dt=step_dt,
        text=text_row,
        slots=slots,
        w1=window_weight(conv_in_weight),
        b1=conv_in_bias.reshape(1, -1),
        gain=norm_gain.reshape(1, -1),
        b2=conv_bias.reshape(1, -1),
        patch_gain=patch_gain.reshape(1, -1),
        post_gain=post_gain.reshape(1, -1),
        lead=(me == 0).astype(jnp.int32).reshape(1),
        flags=jnp.stack([chip == 0, core]).astype(jnp.int32),
        later=[packed(f, n) for f, n in zip(firsts[1:], phases[1:])],
    )
    words = jnp.broadcast_to(prepared["text"][None], (devices, 1, TEXT_W))
    words = lax.all_to_all(words, "seq", split_axis=0, concat_axis=0, tiled=True)
    words = jnp.sum(words, axis=0)
    far_latent = rotate(latent_in.T, "seq", 1)
    steps, words, far_latent = lax.optimization_barrier((prepared["steps"], words, far_latent))
    phase_blocks = [got]
    for gate, blocks in zip(GATES, prepared["later"]):
        before = phase_blocks[0][order[min(gate, len(order) - 1)]]
        blocks, _ = lax.optimization_barrier((blocks, before))
        got = [blocks[0]] * chips
        for turn in order:
            got[turn] = rotate(blocks[turn], "seq", turn)
        phase_blocks.append(got)
    sums = []
    for n, got in enumerate(phase_blocks):
        if n:
            sums[-1], *got = lax.optimization_barrier((sums[-1], *got))
        other = [swap_core(block, "seq") for block in got]
        last = n + 1 == len(phase_blocks)
        shares = attend(
            got,
            other,
            steps,
            prepared["scales"][n],
            prepared["weights"][n],
            sums if last else [],
            last,
        )
        if not last:
            sums.append(shares)
    parts = [shares[0]] + [rotate(shares[t], "seq", chips - t) for t in order]

    latent_next, window, far, passed = step_latent(
        prepared["flags"],
        parts,
        latent_in.T,
        far_latent,
        prepared["base"],
        prepared["step_dt"],
        width,
    )
    near = swap_core(passed, "seq")
    decoded, sent = decode(
        prepared["lead"],
        far,
        near,
        window,
        prepared["w1"],
        prepared["b1"],
        prepared["gain"],
        conv_weight.reshape(-1, CH),
        prepared["b2"],
        patch_weight,
        prepared["patch_gain"],
        prepared["post_gain"],
        proj_weight,
        devices,
    )
    decoded = decoded.reshape(frames, 2 * GRID_H, 2 * GRID_W, CH)
    spread = lax.all_to_all(sent, "seq", split_axis=0, concat_axis=0, tiled=True)
    image_vec, scores = rate(prepared["slots"], words, spread)
    return (latent_next, decoded, image_vec, scores)


def solution(mesh):
    in_specs = (
        P(("grp", "seq"), None),
        P(("grp", "seq"), None),
        P(("grp", "seq"), None),
        P(("grp", "seq"), None),
        P(),
        P(),
        P("grp"),
        P(),
        P(),
        P(),
        P(),
        P(),
        P(),
        P(),
        P(),
        P(),
        P(),
        P(None, "seq"),
        P("grp"),
        P("grp"),
    )
    out_specs = (
        P(("grp", "seq"), None),
        P(("grp", "seq"), None, None, None),
        P(("grp", "seq"), None),
        P(("grp", "seq")),
    )

    return jax.shard_map(local, mesh=mesh, in_specs=in_specs, out_specs=out_specs, check_vma=False)
```

```python
import functools

import jax
import jax.numpy as jnp
import numpy as np
from jax import lax
from jax.experimental import pallas as pl
from jax.experimental.pallas import tpu as pltpu
from jax.sharding import PartitionSpec as P

GRID_H = 8
GRID_W = 12
PATCH = GRID_H * GRID_W
HD = 128
LAT = 64
LAT_C = 16
CH = 384
TEXT_W = 768
KEY_CHUNK = 256
GATES = (1,)


highest = lax.Precision.HIGHEST
VM = pl.BlockSpec(memory_space=pltpu.VMEM)
SM = pl.BlockSpec(memory_space=pltpu.SMEM)
ANY = pl.BlockSpec(memory_space=pl.ANY)


def rotate(value, axis, steps):
    count = lax.axis_size(axis)
    return lax.ppermute(value, axis, [(i, (i + 2 * steps) % count) for i in range(count)])


def swap_core(value, axis):
    count = lax.axis_size(axis)
    return lax.ppermute(value, axis, [(i, i ^ 1) for i in range(count)])


def pack_kernel(blocks, at_ref, k_hbm, v_hbm, q_hbm, *refs):
    out_refs, (buf, in_sem, out_sem) = refs[:blocks], refs[blocks:]
    width = buf.shape[3]
    gets = []
    for n in range(blocks):
        at = pl.multiple_of(at_ref[n], HD)
        gets.append(
            [
                pltpu.make_async_copy(src.at[:, pl.ds(at, width)], buf.at[n, i], in_sem.at[n, i])
                for i, src in enumerate((k_hbm, v_hbm, q_hbm))
            ]
        )
        for get in gets[-1]:
            get.start()
    puts = [
        pltpu.make_async_copy(buf.at[n], out_refs[n], out_sem.at[n]) for n in range(blocks)
    ]
    for n in range(blocks):
        for get in gets[n]:
            get.wait()
        puts[n].start()
    for put in puts:
        put.wait()


def pack(keys, values, queries, starts, width):
    rows, blocks = keys.shape[0], starts.shape[0]
    return pl.pallas_call(
        functools.partial(pack_kernel, blocks),
        out_shape=[jax.ShapeDtypeStruct((3, rows, width), jnp.bfloat16)] * blocks,
        in_specs=[SM, ANY, ANY, ANY],
        out_specs=[ANY] * blocks,
        scratch_shapes=[
            pltpu.VMEM((blocks, 3, rows, width), jnp.bfloat16),
            pltpu.SemaphoreType.DMA((blocks, 3)),
            pltpu.SemaphoreType.DMA((blocks,)),
        ],
        name="pack",
    )(starts, keys, values, queries)


def attend_kernel(blocks, heads, frames, earlier, last, chip_ref, t_ref, sc_ref, w_ref, *refs):
    prev_refs, refs = refs[:earlier], refs[earlier:]
    near_refs, far_refs, refs = refs[:blocks], refs[blocks : 2 * blocks], refs[2 * blocks :]
    if last:
        out_ref, refs = refs[0], refs[1:]
    else:
        sum_ref, refs = refs[0], refs[1:]
    q_s, k_s, v_s, s_a, s_b, m_a, m_b, acc_s, tot_s, sem, q_sem = refs[:11]
    if last:
        sum_ref, prev_s, prev_sem = refs[11:]
    sources = near_refs + far_refs
    rows = near_refs[0].shape[1]
    keys = len(sources) * rows
    scale = np.float32(HD**-0.5 * np.log2(np.e))

    def fetch(h, which):
        dst = (k_s, v_s)[which]
        for j, src in enumerate(sources):
            pltpu.make_async_copy(
                src.at[which, :, pl.ds(h * HD, HD)],
                dst.at[h, pl.ds(j * rows, rows), :],
                sem.at[h, which],
            ).start()

    fetch(0, 0)
    for b in range(blocks):
        pltpu.make_async_copy(near_refs[b].at[2], q_s.at[b], q_sem).start()
    fetch(0, 1)
    for h in range(1, heads):
        fetch(h, 0)
        fetch(h, 1)
    gets = []
    for n, prev in enumerate(prev_refs):
        gets.append(pltpu.make_async_copy(prev, prev_s.at[n], prev_sem.at[n]))
        gets[-1].start()
    sum_ref[...] = jnp.zeros(sum_ref.shape, jnp.float32)

    def arrived(h, which):
        whole = (k_s, v_s)[which].at[h]
        pltpu.make_async_copy(whole, whole, sem.at[h, which]).wait()

    def logits(h, b, at, s_ref, peak):
        q = q_s[b, :, pl.ds(pl.multiple_of(h * HD, HD), HD)]
        s = lax.dot_general(
            q,
            k_s[h, at : at + KEY_CHUNK, :],
            (((1,), (1,)), ((), ())),
            preferred_element_type=jnp.float32,
        )
        s_ref[:, at : at + KEY_CHUNK] = s
        folded = functools.reduce(
            jnp.maximum, [s[:, i : i + 128] for i in range(0, KEY_CHUNK, 128)]
        )
        return folded if peak is None else jnp.maximum(peak, folded)

    def keep_peak(peak, m_ref):
        m_ref[...] = jnp.broadcast_to(jnp.max(peak, axis=-1, keepdims=True) * scale, m_ref.shape)

    def finish(h, b, acc, total):
        o = acc / jnp.sum(total, axis=-1, keepdims=True)
        o = o.astype(jnp.bfloat16).astype(jnp.float32)
        square = jnp.sum(o * o, axis=-1, keepdims=True)
        per = rows // frames
        scaled = jnp.concatenate(
            [
                o[f * per : (f + 1) * per] * (1.0 + sc_ref[t_ref[b * frames + f], h])
                for f in range(frames)
            ],
            axis=0,
        )
        part = jnp.dot(scaled, w_ref[h], precision=highest, preferred_element_type=jnp.float32)
        lane = lax.broadcasted_iota(jnp.int32, part.shape, 1)
        return part + jnp.where(lane >= LAT, square, 0.0)

    def one_unit(h, now, top_ref, next_h, next_b, later, later_top_ref):
        top = top_ref[...]
        peak, total = None, None
        acc = jnp.zeros((rows, HD), jnp.float32)
        for at in chunks:
            peak = logits(next_h, next_b, at, later, peak)
            weights = []
            for i in range(at, at + KEY_CHUNK, 128):
                e = jnp.exp2(now[:, i : i + 128] * scale - top)
                total = e if total is None else total + e
                weights.append(e.astype(jnp.bfloat16))
            acc = acc + jnp.dot(
                jnp.concatenate(weights, axis=1),
                v_s[h, at : at + KEY_CHUNK, :],
                preferred_element_type=jnp.float32,
            )
        keep_peak(peak, later_top_ref)
        return acc, total

    chunks = range(0, keys, KEY_CHUNK)
    pltpu.make_async_copy(q_s, q_s, q_sem).wait()
    arrived(0, 0)
    peak = None
    for at in chunks:
        peak = logits(0, 0, at, s_a, peak)
    keep_peak(peak, m_a)
    pairs = blocks // 2
    acc_s[...] = jnp.zeros(acc_s.shape, jnp.float32)
    tot_s[...] = jnp.ones(tot_s.shape, jnp.float32)

    def one_pair(n, carry):
        h, p = n // pairs, n % pairs
        after = jnp.minimum(n + 1, heads * pairs - 1)
        after_h, after_p = after // pairs, after % pairs
        before = jnp.maximum(n - 1, 0)
        before_h, before_p = before // pairs, before % pairs

        @pl.when(p == 0)
        def _():
            arrived(h, 1)

        @pl.when(after_h > h)
        def _():
            arrived(after_h, 0)

        late = finish(before_h, 2 * before_p + 1, acc_s[...], tot_s[...])
        sum_ref[2 * before_p + 1] = sum_ref[2 * before_p + 1] + late
        even = one_unit(h, s_a, m_a, h, 2 * p + 1, s_b, m_b)
        sum_ref[2 * p] = sum_ref[2 * p] + finish(h, 2 * p, *even)
        acc, total = one_unit(h, s_b, m_b, after_h, 2 * after_p, s_a, m_a)
        acc_s[...] = acc
        tot_s[...] = total
        return carry

    lax.fori_loop(0, heads * pairs, one_pair, 0)
    sum_ref[blocks - 1] = sum_ref[blocks - 1] + finish(
        heads - 1, blocks - 1, acc_s[...], tot_s[...]
    )
    if last:
        for get in gets:
            get.wait()
        row, lane = grid_iota(8, 128)
        pick = jnp.where(lane == LAT, 1.0, 0.0)
        for b in range(blocks):
            share = sum_ref[b]
            for n in range(earlier):
                share = share + prev_s[n, b]
            half = PATCH + 8 * frames
            owner = lax.rem(chip_ref[0] - b + blocks, blocks)
            spots = ((owner, 0), (lax.rem(owner + 1, blocks), half))
            beside = jnp.concatenate(
                [share[f * PATCH : (f + 1) * PATCH, :LAT] for f in range(frames)], axis=1
            ).astype(jnp.bfloat16)
            for to, at in spots:
                out_ref[to, at : at + PATCH] = beside
            for f in range(frames):
                square = lax.dot_general(
                    pick,
                    share[f * PATCH : (f + 1) * PATCH],
                    (((1,), (1,)), ((), ())),
                    precision=highest,
                    preferred_element_type=jnp.float32,
                )
                square = jnp.concatenate(
                    [square, jnp.zeros((8, 128 - PATCH), jnp.float32)], axis=1
                )
                high = square.astype(jnp.bfloat16).astype(jnp.float32)
                both = jnp.where(row == 0, high, jnp.where(row == 1, square - high, 0.0))
                for to, at in spots:
                    at = at + PATCH + 8 * f
                    out_ref[to, at : at + 8] = both.astype(jnp.bfloat16)


def attend(near, far, chip, steps, scale, weight, earlier, last):
    blocks = len(near)
    _, rows, cols = near[0].shape
    heads, keys = cols // HD, 2 * blocks * rows
    frames = rows // PATCH
    sums = (blocks, rows, 128)
    if last:
        share = (blocks, 2 * (PATCH + 8 * frames), frames * LAT)
        out_shape = jax.ShapeDtypeStruct(share, jnp.bfloat16)
    else:
        out_shape = jax.ShapeDtypeStruct(sums, jnp.float32)
    return pl.pallas_call(
        functools.partial(attend_kernel, blocks, heads, frames, len(earlier), last),
        out_shape=out_shape,
        in_specs=[SM, SM, VM, VM] + [ANY] * (len(earlier) + 2 * blocks),
        out_specs=VM,
        scratch_shapes=[
            pltpu.VMEM((blocks, rows, cols), jnp.bfloat16),
            pltpu.VMEM((heads, keys, HD), jnp.bfloat16),
            pltpu.VMEM((heads, keys, HD), jnp.bfloat16),
            pltpu.VMEM((rows, keys), jnp.float32),
            pltpu.VMEM((rows, keys), jnp.float32),
            pltpu.VMEM((rows, 128), jnp.float32),
            pltpu.VMEM((rows, 128), jnp.float32),
            pltpu.VMEM((rows, HD), jnp.float32),
            pltpu.VMEM((rows, 128), jnp.float32),
            pltpu.SemaphoreType.DMA((heads, 2)),
            pltpu.SemaphoreType.DMA,
        ]
        + [
            pltpu.VMEM(sums, jnp.float32),
            pltpu.VMEM((max(1, len(earlier)),) + sums, jnp.float32),
            pltpu.SemaphoreType.DMA((max(1, len(earlier)),)),
        ]
        * last,
        cost_estimate=pl.CostEstimate(
            flops=4 * blocks * rows * keys * cols,
            bytes_accessed=4 * keys * cols,
            transcendentals=blocks * rows * keys * heads,
        ),
        name="attend",
    )(chip, steps, scale, weight, *earlier, *near, *far)


WINDOW = ((-1, 1), (0, 0), (0, 1), (1, 0))


OFFSETS = [(di, dj) for di in (-1, 0, 1) for dj in (-1, 0, 1)]


def grid_iota(rows, cols):
    shape = (rows, cols)
    return lax.broadcasted_iota(jnp.int32, shape, 0), lax.broadcasted_iota(jnp.int32, shape, 1)


def over(value, count):
    return jnp.floor((value.astype(jnp.float32) + 0.5) * np.float32(1.0 / count)).astype(jnp.int32)


def as_matrix(hit):
    return jnp.where(hit, 1.0, 0.0).astype(jnp.bfloat16)


def move_matrix(di, dj, cols=PATCH):
    row, col = grid_iota(PATCH, cols)
    j = row - GRID_W * over(row, GRID_W)
    inside = (j + dj >= 0) & (j + dj < GRID_W) & (col < PATCH)
    return as_matrix((col - row == GRID_W * di + dj) & inside)


def place_matrix(di, dj):
    row, col = grid_iota(LAT, 16 * LAT_C)
    u, w, c = col >> 6, (col >> 4) & 3, col & 15
    source = 2 * LAT_C * (1 - (u & 1)) + LAT_C * (1 - (w & 1)) + c

    def seen(at, step):
        return {-1: at == 0, 0: (at == 1) | (at == 2), 1: at == 3}[step]

    return as_matrix((row == source) & seen(u, di) & seen(w, dj))


def order_matrix():
    row, col = grid_iota(4 * PATCH, 4 * PATCH)
    y = over(row, 2 * GRID_W)
    z = row - 2 * GRID_W * y
    source = (2 * (y & 1) + (z & 1)) * PATCH + (y >> 1) * GRID_W + (z >> 1)
    return as_matrix(col == source)


def latent_kernel(width, frames, flag_ref, dt_ref, part_ref, *refs):
    own_ref, far_ref, base_ref, next_ref, win_ref, before_ref, pass_ref = refs
    total = part_ref[0].astype(jnp.float32)
    for n in range(1, part_ref.shape[0]):
        total = total + part_ref[n].astype(jnp.float32)
    row, _ = grid_iota(8, 128)
    pick = jnp.where(row < 2, 1.0, 0.0)
    cols = 16 * LAT_C
    moves = jnp.concatenate([move_matrix(di, dj, 128) for di, dj in OFFSETS], axis=1)
    places = jnp.concatenate([place_matrix(di, dj) for di, dj in OFFSETS], axis=1)
    none = jnp.zeros((128 - PATCH, cols), jnp.bfloat16)
    first_chip, core = flag_ref[0], flag_ref[1]
    for side, latent in enumerate((jnp.transpose(own_ref[...]), jnp.transpose(far_ref[...]))):
        skip = side * (PATCH + 8 * frames)
        for f in range(frames):
            at = slice(f * PATCH, (f + 1) * PATCH)
            squares = total[skip + PATCH + 8 * f : skip + PATCH + 8 * (f + 1)]
            square = lax.dot_general(
                squares,
                pick,
                (((0,), (0,)), ((), ())),
                precision=highest,
                preferred_element_type=jnp.float32,
            )[:PATCH, :LAT]
            inverse = lax.rsqrt(square * np.float32(1.0 / width) + 1e-06)
            scaled = total[skip : skip + PATCH, f * LAT : (f + 1) * LAT] * inverse
            g = side * frames + f
            value = latent[at] + dt_ref[g] * (scaled + base_ref[g : g + 1])
            spread = jnp.dot(
                value.astype(jnp.bfloat16), places, preferred_element_type=jnp.float32
            ).astype(jnp.bfloat16)
            stacked = jnp.concatenate(
                [x for o in range(len(OFFSETS)) for x in (spread[:, o * cols : (o + 1) * cols], none)],
                axis=0,
            )
            window = jnp.dot(moves, stacked, preferred_element_type=jnp.float32)
            if side:
                window = jnp.where(first_chip == 1, 0.0, window)
                before_ref[at] = window.astype(jnp.bfloat16)
                pass_ref[at] = jnp.where(core == 0, win_ref[at], before_ref[at])
            else:
                next_ref[at] = value
                win_ref[at] = window.astype(jnp.bfloat16)


def step_latent(flags, parts, own, far, base, step_dt, width):
    rows = own.shape[1]
    window = jax.ShapeDtypeStruct((rows, 16 * LAT_C), jnp.bfloat16)
    return pl.pallas_call(
        functools.partial(latent_kernel, width, rows // PATCH),
        out_shape=[jax.ShapeDtypeStruct((rows, LAT), jnp.float32), window, window, window],
        in_specs=[SM, SM] + [VM] * 4,
        out_specs=[VM] * 4,
        name="latent",
    )(flags, step_dt, parts, own, far, base)


def text_kernel(at_ref, id_ref, table_hbm, out_ref, buf, sem):
    count = id_ref.shape[0]

    def block(n):
        start = pl.multiple_of((id_ref[n] // 128) * 128, 128)
        return pltpu.make_async_copy(table_hbm.at[:, pl.ds(start, 128)], buf.at[n], sem)

    def fetch(n, carry):
        block(n).start()
        return carry

    lax.fori_loop(0, count, fetch, 0)
    pltpu.make_async_copy(buf, buf, sem).wait()
    width = buf.shape[1]
    _, lane = grid_iota(width, 128)

    def add(n, acc):
        return acc + jnp.where(lane == id_ref[n] % 128, buf[n].astype(jnp.float32), 0.0)

    acc = lax.fori_loop(0, count, add, jnp.zeros((width, 128), jnp.float32))
    own = lax.dot_general(
        jnp.ones((8, 128), jnp.float32),
        acc,
        (((1,), (1,)), ((), ())),
        precision=highest,
        preferred_element_type=jnp.float32,
    )
    row, col = grid_iota(width, out_ref.shape[1])
    spot = jnp.where(col == row + at_ref[0], 1.0, 0.0)
    placed = jnp.dot(own, spot, precision=highest, preferred_element_type=jnp.float32)
    out_ref[...] = placed[:1] * np.float32(1.0 / count)


def text_mean(at, ids, table):
    width = table.shape[0]
    return pl.pallas_call(
        text_kernel,
        out_shape=jax.ShapeDtypeStruct((1, TEXT_W), jnp.float32),
        in_specs=[SM, SM, ANY],
        out_specs=VM,
        scratch_shapes=[
            pltpu.VMEM((ids.shape[0], width, 128), jnp.bfloat16),
            pltpu.SemaphoreType.DMA,
        ],
        name="text",
    )(at, ids, table)


def decode_kernel(
    frames,
    lead_ref,
    far_ref,
    near_ref,
    own_ref,
    w1_ref,
    b1_ref,
    gain_ref,
    b2_ref,
    pg_ref,
    post_ref,
    w2_hbm,
    pw_hbm,
    proj_hbm,
    out_ref,
    sent_ref,
    w2_s,
    pw_s,
    proj_s,
    win_s,
    x_s,
    sem,
):
    taps = 9 * CH
    w2_copy = pltpu.make_async_copy(w2_hbm, w2_s, sem.at[0])
    pw_copy = pltpu.make_async_copy(pw_hbm, pw_s, sem.at[1])
    w2_copy.start()
    pw_copy.start()
    proj_copy = pltpu.make_async_copy(proj_hbm, proj_s, sem.at[2])
    proj_copy.start()
    rows = frames * PATCH
    for n, r in enumerate((far_ref, near_ref, own_ref)):
        win_s[n * rows : (n + 1) * rows] = r[...]
    wide = frames + 2
    skip = 3 * frames - wide - 2
    cols = 16 * LAT_C
    firsts = []
    for q in range(4):
        acc = jnp.zeros((wide * PATCH, CH), jnp.float32)
        for t in range(3):
            acc = acc + jnp.dot(
                win_s[(skip + t) * PATCH : (skip + t + wide) * PATCH],
                w1_ref[t * cols : (t + 1) * cols, q * CH : (q + 1) * CH],
                preferred_element_type=jnp.float32,
            )
        first = (acc + b1_ref[...]).astype(jnp.bfloat16).astype(jnp.float32)
        firsts.append(first[2 * PATCH :])
        mean = jnp.mean(first * first, axis=-1, keepdims=True)
        v = first * lax.rsqrt(mean + 1e-06) * gain_ref[...]
        act = v / (1.0 + jnp.exp(-v))
        row = lax.broadcasted_iota(jnp.int32, (wide * PATCH, 1), 0)
        act = jnp.where((row >= 2 * PATCH) | (lead_ref[0] == 0), act, 0.0).astype(jnp.bfloat16)
        a, b = q // 2, q % 2
        da, db = (1, -1)[a], (1, -1)[b]
        moves = jnp.concatenate(
            [move_matrix(da, 0), move_matrix(0, db), move_matrix(da, db)], axis=0
        )
        for f in range(wide):
            plane = act[f * PATCH : (f + 1) * PATCH]
            moved = jnp.dot(
                moves, plane, preferred_element_type=jnp.float32
            ).astype(jnp.bfloat16)
            pieces = {
                (0, 0): plane,
                (1, 0): moved[:PATCH],
                (0, 1): moved[PATCH : 2 * PATCH],
                (1, 1): moved[2 * PATCH :],
            }
            for (ma, mb), piece in pieces.items():
                u = WINDOW.index(((1, -1)[a] if ma else 0, a))
                w = WINDOW.index(((1, -1)[b] if mb else 0, b))
                for oa in (0, 1):
                    for ob in (0, 1):
                        dy, dz = u - oa, w - ob
                        if 0 <= dy < 3 and 0 <= dz < 3:
                            at = (f * 4 + 2 * oa + ob) * PATCH
                            tap = (3 * dy + dz) * CH
                            x_s[at : at + PATCH, tap : tap + CH] = piece
    w2_copy.wait()
    block = 4 * PATCH
    out = jnp.zeros((frames * block, CH), jnp.float32)
    for t in range(3):
        out = out + jnp.dot(
            x_s[t * block : (t + frames) * block],
            w2_s[t * taps : (t + 1) * taps],
            preferred_element_type=jnp.float32,
        )
    first = jnp.concatenate(
        [firsts[q][f * PATCH : (f + 1) * PATCH] for f in range(frames) for q in range(4)], axis=0
    )
    dec = (out + b2_ref[...] + first).astype(jnp.bfloat16)
    order = order_matrix()
    for f in range(frames):
        out_ref[f * block : (f + 1) * block] = jnp.dot(
            order, dec[f * block : (f + 1) * block], preferred_element_type=jnp.float32
        ).astype(jnp.bfloat16)
    pw_copy.wait()
    emb = jnp.zeros((rows, pw_s.shape[1]), jnp.float32)
    for q in range(4):
        lhs = jnp.concatenate(
            [dec[(f * 4 + q) * PATCH : (f * 4 + q + 1) * PATCH] for f in range(frames)], axis=0
        )
        emb = emb + jnp.dot(
            lhs, pw_s[q * CH : (q + 1) * CH], preferred_element_type=jnp.float32
        )
    emb = emb.astype(jnp.bfloat16).astype(jnp.float32)
    centered = emb - jnp.mean(emb, axis=-1, keepdims=True)
    variance = jnp.mean(centered * centered, axis=-1, keepdims=True)
    normed = centered * lax.rsqrt(variance + 1e-05) * pg_ref[...]
    pooled = jnp.concatenate(
        [
            jnp.mean(normed[f * PATCH : (f + 1) * PATCH], axis=0, keepdims=True)
            for f in range(frames)
        ],
        axis=0,
    )
    centered = pooled - jnp.mean(pooled, axis=-1, keepdims=True)
    variance = jnp.mean(centered * centered, axis=-1, keepdims=True)
    vec = centered * lax.rsqrt(variance + 1e-05) * post_ref[...]
    columns = jnp.transpose(
        jnp.concatenate([vec, jnp.zeros((8 - frames, vec.shape[1]), jnp.float32)], axis=0)
    )
    proj_copy.wait()
    for f in range(frames):
        row = jnp.sum(columns[:, f : f + 1] * proj_s[...], axis=0, keepdims=True)
        for n in range(sent_ref.shape[0]):
            sent_ref[n, f : f + 1, :] = row


def window_weight(weight):
    taps = weight.reshape(3, 3, 3, LAT_C, CH)
    grown = [
        jnp.pad(taps, ((0, 0), (a, 1 - a), (b, 1 - b), (0, 0), (0, 0))).reshape(-1, CH)
        for a in (0, 1)
        for b in (0, 1)
    ]
    return jnp.concatenate(grown, axis=1)


def decode(
    lead, far, near, own, w1, b1, gain, w2, b2, pw, patch_gain, post_gain, proj, devices
):
    rows = own.shape[0]
    frames = rows // PATCH
    wide = frames + 2
    return pl.pallas_call(
        functools.partial(decode_kernel, frames),
        out_shape=[
            jax.ShapeDtypeStruct((frames * 4 * PATCH, CH), jnp.bfloat16),
            jax.ShapeDtypeStruct((devices, frames, proj.shape[1]), jnp.float32),
        ],
        in_specs=[SM] + [VM] * 9 + [ANY, ANY, ANY],
        out_specs=[VM, VM],
        scratch_shapes=[
            pltpu.VMEM(w2.shape, jnp.bfloat16),
            pltpu.VMEM(pw.shape, jnp.bfloat16),
            pltpu.VMEM(proj.shape, jnp.float32),
            pltpu.VMEM((3 * rows, 16 * LAT_C), jnp.bfloat16),
            pltpu.VMEM((wide * 4 * PATCH, 9 * CH), jnp.bfloat16),
            pltpu.SemaphoreType.DMA((3,)),
        ],
        name="decode",
    )(
        lead,
        far,
        near,
        own,
        w1,
        b1,
        gain,
        b2,
        patch_gain,
        post_gain,
        w2,
        pw,
        proj,
    )


def rate_kernel(frames, slot_ref, text_ref, got_ref, vec_ref, score_ref):
    text = text_ref[...]
    text_rms = jnp.sqrt(jnp.mean(text * text) + 1e-06)
    for f in range(frames):
        slot = slot_ref[f]
        block = got_ref[slot // frames]
        row = block[:1]
        for n in range(1, frames):
            row = jnp.where(slot % frames == n, block[n : n + 1], row)
        vec_ref[f : f + 1] = row
        inner = jnp.sum(row * text)
        image_rms = jnp.sqrt(jnp.mean(row * row) + 1e-06)
        score_ref[f] = 100.0 * inner / (TEXT_W * image_rms * text_rms)


def rate(slots, text, got):
    frames = slots.shape[0]
    return pl.pallas_call(
        functools.partial(rate_kernel, frames),
        out_shape=[
            jax.ShapeDtypeStruct((frames, got.shape[2]), jnp.float32),
            jax.ShapeDtypeStruct((frames,), jnp.float32),
        ],
        in_specs=[SM, VM, VM],
        out_specs=[VM, SM],
        name="rate",
    )(slots, text, got)


def local(
    queries,
    keys,
    values,
    latent_in,
    mod_table,
    step_size,
    timestep,
    head_weight,
    conv_in_weight,
    conv_in_bias,
    norm_gain,
    conv_weight,
    conv_bias,
    patch_weight,
    patch_gain,
    post_gain,
    proj_weight,
    text_table,
    prompt_ids,
    frame_order,
):
    rows, width = queries.shape
    devices = lax.axis_size("seq")
    chips = devices // 2
    cols = width // chips
    heads = cols // HD
    frames = rows // PATCH
    me = lax.axis_index("seq")
    chip, core = me // 2, me % 2

    tail = max(1, heads // 2)
    phases = (heads - tail, tail) if heads > tail else (tail,)
    firsts = [sum(phases[:n]) for n in range(len(phases))]

    order = sorted(range(1, chips), key=lambda t: abs(2 * t - chips))

    def packed(first, count):
        at = ((chip + jnp.arange(chips)) % chips) * cols + first * HD
        return pack(keys, values, queries, at.astype(jnp.int32), count * HD)

    blocks = packed(firsts[0], phases[0])
    got = [blocks[0]] * chips
    for turn in order:
        got[turn] = rotate(blocks[turn], "seq", turn)
    scale = lax.dynamic_slice_in_dim(mod_table[:, 1, :], chip * cols, cols, 1)
    scale = scale.reshape(-1, heads, 1, HD)
    weight = lax.dynamic_slice_in_dim(head_weight, chip * cols, cols, 0).reshape(heads, HD, LAT)
    weight = jnp.pad(weight, ((0, 0), (0, 0), (0, 128 - LAT)))
    origin = 2 * ((chip - jnp.arange(chips)) % chips) + core
    steps = jnp.take(timestep.reshape(devices, frames), origin, axis=0).reshape(-1)
    near_steps = jnp.stack(
        [
            lax.dynamic_slice_in_dim(timestep, at * frames, frames, 0)
            for at in (me, jnp.maximum(me - 2, 0))
        ]
    ).reshape(-1)
    base = jnp.dot(jnp.take(mod_table[:, 0, :], near_steps, axis=0), head_weight, precision=highest)
    step_dt = jnp.take(step_size, near_steps)
    text_row = text_mean(
        (me * text_table.shape[1]).astype(jnp.int32).reshape(1), prompt_ids, text_table.T
    )
    slots = lax.dynamic_slice_in_dim(frame_order, me * frames, frames, 0)
    prepared = dict(
        scales=[scale[:, f : f + n] for f, n in zip(firsts, phases)],
        weights=[weight[f : f + n] for f, n in zip(firsts, phases)],
        steps=steps,
        base=base,
        step_dt=step_dt,
        text=text_row,
        slots=slots,
        w1=window_weight(conv_in_weight),
        b1=conv_in_bias.reshape(1, -1),
        gain=norm_gain.reshape(1, -1),
        b2=conv_bias.reshape(1, -1),
        patch_gain=patch_gain.reshape(1, -1),
        post_gain=post_gain.reshape(1, -1),
        lead=(me == 0).astype(jnp.int32).reshape(1),
        chip=chip.astype(jnp.int32).reshape(1),
        flags=jnp.stack([chip == 0, core]).astype(jnp.int32),
        later=[packed(f, n) for f, n in zip(firsts[1:], phases[1:])],
    )
    words = jnp.broadcast_to(prepared["text"][None], (devices, 1, TEXT_W))
    words = lax.all_to_all(words, "seq", split_axis=0, concat_axis=0, tiled=True)
    words = jnp.sum(words, axis=0)
    far_latent = rotate(latent_in.T, "seq", 1)
    steps = prepared["steps"]
    phase_blocks = [got]
    for gate, blocks in zip(GATES, prepared["later"]):
        before = phase_blocks[0][order[min(gate, len(order) - 1)]]
        blocks, _ = lax.optimization_barrier((blocks, before))
        got = [blocks[0]] * chips
        for turn in order:
            got[turn] = rotate(blocks[turn], "seq", turn)
        phase_blocks.append(got)
    sums = []
    for n, got in enumerate(phase_blocks):
        if n:
            sums[-1], words, far_latent, *got = lax.optimization_barrier(
                (sums[-1], words, far_latent, *got)
            )
        other = [swap_core(block, "seq") for block in got]
        last = n + 1 == len(phase_blocks)
        shares = attend(
            got,
            other,
            prepared["chip"],
            steps,
            prepared["scales"][n],
            prepared["weights"][n],
            sums if last else [],
            last,
        )
        if not last:
            sums.append(shares)
    same_core = [list(range(k, devices, 2)) for k in (0, 1)]
    parts = lax.all_to_all(
        shares, "seq", split_axis=0, concat_axis=0, axis_index_groups=same_core, tiled=True
    )

    latent_next, window, far, passed = step_latent(
        prepared["flags"],
        parts,
        latent_in.T,
        far_latent,
        prepared["base"],
        prepared["step_dt"],
        width,
    )
    near = swap_core(passed, "seq")
    decoded, sent = decode(
        prepared["lead"],
        far,
        near,
        window,
        prepared["w1"],
        prepared["b1"],
        prepared["gain"],
        conv_weight.reshape(-1, CH),
        prepared["b2"],
        patch_weight,
        prepared["patch_gain"],
        prepared["post_gain"],
        proj_weight,
        devices,
    )
    decoded = decoded.reshape(frames, 2 * GRID_H, 2 * GRID_W, CH)
    spread = lax.all_to_all(sent, "seq", split_axis=0, concat_axis=0, tiled=True)
    image_vec, scores = rate(prepared["slots"], words, spread)
    return (latent_next, decoded, image_vec, scores)


def solution(mesh):
    in_specs = (
        P(("grp", "seq"), None),
        P(("grp", "seq"), None),
        P(("grp", "seq"), None),
        P(("grp", "seq"), None),
        P(),
        P(),
        P("grp"),
        P(),
        P(),
        P(),
        P(),
        P(),
        P(),
        P(),
        P(),
        P(),
        P(),
        P(None, "seq"),
        P("grp"),
        P("grp"),
    )
    out_specs = (
        P(("grp", "seq"), None),
        P(("grp", "seq"), None, None, None),
        P(("grp", "seq"), None),
        P(("grp", "seq")),
    )

    return jax.shard_map(local, mesh=mesh, in_specs=in_specs, out_specs=out_specs, check_vma=False)
```

```python
import functools

import jax
import jax.numpy as jnp
import numpy as np
from jax import lax
from jax.experimental import pallas as pl
from jax.experimental.pallas import tpu as pltpu
from jax.sharding import PartitionSpec as P

GRID_H = 8
GRID_W = 12
PATCH = GRID_H * GRID_W
HD = 128
LAT = 64
LAT_C = 16
CH = 384
TEXT_W = 768
KEY_CHUNK = 256
GATES = (1,)


highest = lax.Precision.HIGHEST
VM = pl.BlockSpec(memory_space=pltpu.VMEM)
SM = pl.BlockSpec(memory_space=pltpu.SMEM)
ANY = pl.BlockSpec(memory_space=pl.ANY)


def rotate(value, axis, steps):
    count = lax.axis_size(axis)
    return lax.ppermute(value, axis, [(i, (i + 2 * steps) % count) for i in range(count)])


def swap_core(value, axis):
    count = lax.axis_size(axis)
    return lax.ppermute(value, axis, [(i, i ^ 1) for i in range(count)])


def pack_kernel(blocks, at_ref, k_hbm, v_hbm, q_hbm, *refs):
    out_refs, (buf, in_sem, out_sem) = refs[:blocks], refs[blocks:]
    width = buf.shape[3]
    gets = []
    for n in range(blocks):
        at = pl.multiple_of(at_ref[n], HD)
        gets.append(
            [
                pltpu.make_async_copy(src.at[:, pl.ds(at, width)], buf.at[n, i], in_sem.at[n, i])
                for i, src in enumerate((k_hbm, v_hbm, q_hbm))
            ]
        )
        for get in gets[-1]:
            get.start()
    puts = [
        pltpu.make_async_copy(buf.at[n], out_refs[n], out_sem.at[n]) for n in range(blocks)
    ]
    for n in range(blocks):
        for get in gets[n]:
            get.wait()
        puts[n].start()
    for put in puts:
        put.wait()


def pack(keys, values, queries, starts, width):
    rows, blocks = keys.shape[0], starts.shape[0]
    return pl.pallas_call(
        functools.partial(pack_kernel, blocks),
        out_shape=[jax.ShapeDtypeStruct((3, rows, width), jnp.bfloat16)] * blocks,
        in_specs=[SM, ANY, ANY, ANY],
        out_specs=[ANY] * blocks,
        scratch_shapes=[
            pltpu.VMEM((blocks, 3, rows, width), jnp.bfloat16),
            pltpu.SemaphoreType.DMA((blocks, 3)),
            pltpu.SemaphoreType.DMA((blocks,)),
        ],
        name="pack",
    )(starts, keys, values, queries)


def attend_kernel(blocks, heads, frames, earlier, last, chip_ref, t_ref, sc_ref, w_ref, *refs):
    prev_refs, refs = refs[:earlier], refs[earlier:]
    near_refs, far_refs, refs = refs[:blocks], refs[blocks : 2 * blocks], refs[2 * blocks :]
    if last:
        out_ref, refs = refs[0], refs[1:]
    else:
        sum_ref, refs = refs[0], refs[1:]
    q_s, k_s, v_s, s_a, s_b, m_a, m_b, acc_s, tot_s, sem, q_sem = refs[:11]
    if last:
        sum_ref, prev_s, prev_sem = refs[11:]
    sources = near_refs + far_refs
    rows = near_refs[0].shape[1]
    keys = len(sources) * rows
    scale = np.float32(HD**-0.5 * np.log2(np.e))

    def fetch(h, which):
        dst = (k_s, v_s)[which]
        for j, src in enumerate(sources):
            pltpu.make_async_copy(
                src.at[which, :, pl.ds(h * HD, HD)],
                dst.at[h, pl.ds(j * rows, rows), :],
                sem.at[h, which],
            ).start()

    fetch(0, 0)
    for b in range(blocks):
        pltpu.make_async_copy(near_refs[b].at[2], q_s.at[b], q_sem).start()
    fetch(0, 1)
    for h in range(1, heads):
        fetch(h, 0)
        fetch(h, 1)
    gets = []
    for n, prev in enumerate(prev_refs):
        gets.append(pltpu.make_async_copy(prev, prev_s.at[n], prev_sem.at[n]))
        gets[-1].start()
    sum_ref[...] = jnp.zeros(sum_ref.shape, jnp.float32)

    def arrived(h, which):
        whole = (k_s, v_s)[which].at[h]
        pltpu.make_async_copy(whole, whole, sem.at[h, which]).wait()

    def logits(h, b, at, s_ref, peak):
        q = q_s[b, :, pl.ds(pl.multiple_of(h * HD, HD), HD)]
        s = lax.dot_general(
            q,
            k_s[h, at : at + KEY_CHUNK, :],
            (((1,), (1,)), ((), ())),
            preferred_element_type=jnp.float32,
        )
        s_ref[:, at : at + KEY_CHUNK] = s
        folded = functools.reduce(
            jnp.maximum, [s[:, i : i + 128] for i in range(0, KEY_CHUNK, 128)]
        )
        return folded if peak is None else jnp.maximum(peak, folded)

    def keep_peak(peak, m_ref):
        m_ref[...] = jnp.broadcast_to(jnp.max(peak, axis=-1, keepdims=True) * scale, m_ref.shape)

    def finish(h, b, acc, total):
        o = acc / jnp.sum(total, axis=-1, keepdims=True)
        o = o.astype(jnp.bfloat16).astype(jnp.float32)
        square = jnp.sum(o * o, axis=-1, keepdims=True)
        per = rows // frames
        scaled = jnp.concatenate(
            [
                o[f * per : (f + 1) * per] * (1.0 + sc_ref[t_ref[b * frames + f], h])
                for f in range(frames)
            ],
            axis=0,
        )
        part = jnp.dot(scaled, w_ref[h], precision=highest, preferred_element_type=jnp.float32)
        lane = lax.broadcasted_iota(jnp.int32, part.shape, 1)
        return part + jnp.where(lane >= LAT, square, 0.0)

    def one_unit(h, now, top_ref, next_h, next_b, later, later_top_ref):
        top = top_ref[...]
        peak, total = None, None
        acc = jnp.zeros((rows, HD), jnp.float32)
        for at in chunks:
            peak = logits(next_h, next_b, at, later, peak)
            weights = []
            for i in range(at, at + KEY_CHUNK, 128):
                e = jnp.exp2(now[:, i : i + 128] * scale - top)
                total = e if total is None else total + e
                weights.append(e.astype(jnp.bfloat16))
            acc = acc + jnp.dot(
                jnp.concatenate(weights, axis=1),
                v_s[h, at : at + KEY_CHUNK, :],
                preferred_element_type=jnp.float32,
            )
        keep_peak(peak, later_top_ref)
        return acc, total

    chunks = range(0, keys, KEY_CHUNK)
    pltpu.make_async_copy(q_s, q_s, q_sem).wait()
    arrived(0, 0)
    peak = None
    for at in chunks:
        peak = logits(0, 0, at, s_a, peak)
    keep_peak(peak, m_a)
    pairs = blocks // 2
    acc_s[...] = jnp.zeros(acc_s.shape, jnp.float32)
    tot_s[...] = jnp.ones(tot_s.shape, jnp.float32)

    def one_pair(n, carry):
        h, p = n // pairs, n % pairs
        after = jnp.minimum(n + 1, heads * pairs - 1)
        after_h, after_p = after // pairs, after % pairs
        before = jnp.maximum(n - 1, 0)
        before_h, before_p = before // pairs, before % pairs

        @pl.when(p == 0)
        def _():
            arrived(h, 1)

        @pl.when(after_h > h)
        def _():
            arrived(after_h, 0)

        late = finish(before_h, 2 * before_p + 1, acc_s[...], tot_s[...])
        sum_ref[2 * before_p + 1] = sum_ref[2 * before_p + 1] + late
        even = one_unit(h, s_a, m_a, h, 2 * p + 1, s_b, m_b)
        sum_ref[2 * p] = sum_ref[2 * p] + finish(h, 2 * p, *even)
        acc, total = one_unit(h, s_b, m_b, after_h, 2 * after_p, s_a, m_a)
        acc_s[...] = acc
        tot_s[...] = total
        return carry

    lax.fori_loop(0, heads * pairs, one_pair, 0)
    sum_ref[blocks - 1] = sum_ref[blocks - 1] + finish(
        heads - 1, blocks - 1, acc_s[...], tot_s[...]
    )
    if last:
        for get in gets:
            get.wait()
        row, lane = grid_iota(8, 128)
        pick = jnp.where(lane == LAT, 1.0, 0.0)
        for b in range(blocks):
            share = sum_ref[b]
            for n in range(earlier):
                share = share + prev_s[n, b]
            half = PATCH + 8 * frames
            owner = lax.rem(chip_ref[0] - b + blocks, blocks)
            spots = ((owner, 0), (lax.rem(owner + 1, blocks), half))
            beside = jnp.concatenate(
                [share[f * PATCH : (f + 1) * PATCH, :LAT] for f in range(frames)], axis=1
            ).astype(jnp.bfloat16)
            for to, at in spots:
                out_ref[to, at : at + PATCH] = beside
            for f in range(frames):
                square = lax.dot_general(
                    pick,
                    share[f * PATCH : (f + 1) * PATCH],
                    (((1,), (1,)), ((), ())),
                    precision=highest,
                    preferred_element_type=jnp.float32,
                )
                square = jnp.concatenate(
                    [square, jnp.zeros((8, 128 - PATCH), jnp.float32)], axis=1
                )
                high = square.astype(jnp.bfloat16).astype(jnp.float32)
                both = jnp.where(row == 0, high, jnp.where(row == 1, square - high, 0.0))
                for to, at in spots:
                    at = at + PATCH + 8 * f
                    out_ref[to, at : at + 8] = both.astype(jnp.bfloat16)


def attend(near, far, chip, steps, scale, weight, earlier, last):
    blocks = len(near)
    _, rows, cols = near[0].shape
    heads, keys = cols // HD, 2 * blocks * rows
    frames = rows // PATCH
    sums = (blocks, rows, 128)
    if last:
        share = (blocks, 2 * (PATCH + 8 * frames), frames * LAT)
        out_shape = jax.ShapeDtypeStruct(share, jnp.bfloat16)
    else:
        out_shape = jax.ShapeDtypeStruct(sums, jnp.float32)
    return pl.pallas_call(
        functools.partial(attend_kernel, blocks, heads, frames, len(earlier), last),
        out_shape=out_shape,
        in_specs=[SM, SM, VM, VM] + [ANY] * (len(earlier) + 2 * blocks),
        out_specs=VM,
        scratch_shapes=[
            pltpu.VMEM((blocks, rows, cols), jnp.bfloat16),
            pltpu.VMEM((heads, keys, HD), jnp.bfloat16),
            pltpu.VMEM((heads, keys, HD), jnp.bfloat16),
            pltpu.VMEM((rows, keys), jnp.float32),
            pltpu.VMEM((rows, keys), jnp.float32),
            pltpu.VMEM((rows, 128), jnp.float32),
            pltpu.VMEM((rows, 128), jnp.float32),
            pltpu.VMEM((rows, HD), jnp.float32),
            pltpu.VMEM((rows, 128), jnp.float32),
            pltpu.SemaphoreType.DMA((heads, 2)),
            pltpu.SemaphoreType.DMA,
        ]
        + [
            pltpu.VMEM(sums, jnp.float32),
            pltpu.VMEM((max(1, len(earlier)),) + sums, jnp.float32),
            pltpu.SemaphoreType.DMA((max(1, len(earlier)),)),
        ]
        * last,
        cost_estimate=pl.CostEstimate(
            flops=4 * blocks * rows * keys * cols,
            bytes_accessed=4 * keys * cols,
            transcendentals=blocks * rows * keys * heads,
        ),
        compiler_params=pltpu.CompilerParams(vmem_limit_bytes=40 << 20),
        name="attend",
    )(chip, steps, scale, weight, *earlier, *near, *far)


WINDOW = ((-1, 1), (0, 0), (0, 1), (1, 0))


OFFSETS = [(di, dj) for di in (-1, 0, 1) for dj in (-1, 0, 1)]


def grid_iota(rows, cols):
    shape = (rows, cols)
    return lax.broadcasted_iota(jnp.int32, shape, 0), lax.broadcasted_iota(jnp.int32, shape, 1)


def over(value, count):
    return jnp.floor((value.astype(jnp.float32) + 0.5) * np.float32(1.0 / count)).astype(jnp.int32)


def as_matrix(hit):
    return jnp.where(hit, 1.0, 0.0).astype(jnp.bfloat16)


def move_matrix(di, dj, cols=PATCH):
    row, col = grid_iota(PATCH, cols)
    j = row - GRID_W * over(row, GRID_W)
    inside = (j + dj >= 0) & (j + dj < GRID_W) & (col < PATCH)
    return as_matrix((col - row == GRID_W * di + dj) & inside)


def place_matrix(di, dj):
    row, col = grid_iota(LAT, 16 * LAT_C)
    u, w, c = col >> 6, (col >> 4) & 3, col & 15
    source = 2 * LAT_C * (1 - (u & 1)) + LAT_C * (1 - (w & 1)) + c

    def seen(at, step):
        return {-1: at == 0, 0: (at == 1) | (at == 2), 1: at == 3}[step]

    return as_matrix((row == source) & seen(u, di) & seen(w, dj))


def order_matrix():
    row, col = grid_iota(4 * PATCH, 4 * PATCH)
    y = over(row, 2 * GRID_W)
    z = row - 2 * GRID_W * y
    source = (2 * (y & 1) + (z & 1)) * PATCH + (y >> 1) * GRID_W + (z >> 1)
    return as_matrix(col == source)


def latent_kernel(width, frames, flag_ref, dt_ref, part_ref, *refs):
    own_ref, far_ref, base_ref, next_ref, win_ref, before_ref, pass_ref = refs
    total = part_ref[0].astype(jnp.float32)
    for n in range(1, part_ref.shape[0]):
        total = total + part_ref[n].astype(jnp.float32)
    row, _ = grid_iota(8, 128)
    pick = jnp.where(row < 2, 1.0, 0.0)
    cols = 16 * LAT_C
    moves = jnp.concatenate([move_matrix(di, dj, 128) for di, dj in OFFSETS], axis=1)
    places = jnp.concatenate([place_matrix(di, dj) for di, dj in OFFSETS], axis=1)
    none = jnp.zeros((128 - PATCH, cols), jnp.bfloat16)
    first_chip, core = flag_ref[0], flag_ref[1]
    for side, latent in enumerate((jnp.transpose(own_ref[...]), jnp.transpose(far_ref[...]))):
        skip = side * (PATCH + 8 * frames)
        for f in range(frames):
            at = slice(f * PATCH, (f + 1) * PATCH)
            squares = total[skip + PATCH + 8 * f : skip + PATCH + 8 * (f + 1)]
            square = lax.dot_general(
                squares,
                pick,
                (((0,), (0,)), ((), ())),
                precision=highest,
                preferred_element_type=jnp.float32,
            )[:PATCH, :LAT]
            inverse = lax.rsqrt(square * np.float32(1.0 / width) + 1e-06)
            scaled = total[skip : skip + PATCH, f * LAT : (f + 1) * LAT] * inverse
            g = side * frames + f
            value = latent[at] + dt_ref[g] * (scaled + base_ref[g : g + 1])
            spread = jnp.dot(
                value.astype(jnp.bfloat16), places, preferred_element_type=jnp.float32
            ).astype(jnp.bfloat16)
            stacked = jnp.concatenate(
                [x for o in range(len(OFFSETS)) for x in (spread[:, o * cols : (o + 1) * cols], none)],
                axis=0,
            )
            window = jnp.dot(moves, stacked, preferred_element_type=jnp.float32)
            if side:
                window = jnp.where(first_chip == 1, 0.0, window)
                before_ref[at] = window.astype(jnp.bfloat16)
                pass_ref[at] = jnp.where(core == 0, win_ref[at], before_ref[at])
            else:
                next_ref[at] = value
                win_ref[at] = window.astype(jnp.bfloat16)


def step_latent(flags, parts, own, far, base, step_dt, width):
    rows = own.shape[1]
    window = jax.ShapeDtypeStruct((rows, 16 * LAT_C), jnp.bfloat16)
    return pl.pallas_call(
        functools.partial(latent_kernel, width, rows // PATCH),
        out_shape=[jax.ShapeDtypeStruct((rows, LAT), jnp.float32), window, window, window],
        in_specs=[SM, SM] + [VM] * 4,
        out_specs=[VM] * 4,
        compiler_params=pltpu.CompilerParams(vmem_limit_bytes=16 << 20),
        name="latent",
    )(flags, step_dt, parts, own, far, base)


def text_kernel(at_ref, id_ref, table_hbm, out_ref, buf, sem):
    count = id_ref.shape[0]

    def block(n):
        start = pl.multiple_of((id_ref[n] // 128) * 128, 128)
        return pltpu.make_async_copy(table_hbm.at[:, pl.ds(start, 128)], buf.at[n], sem)

    def fetch(n, carry):
        block(n).start()
        return carry

    lax.fori_loop(0, count, fetch, 0)
    pltpu.make_async_copy(buf, buf, sem).wait()
    width = buf.shape[1]
    _, lane = grid_iota(width, 128)

    def add(n, acc):
        return acc + jnp.where(lane == id_ref[n] % 128, buf[n].astype(jnp.float32), 0.0)

    acc = lax.fori_loop(0, count, add, jnp.zeros((width, 128), jnp.float32))
    own = lax.dot_general(
        jnp.ones((8, 128), jnp.float32),
        acc,
        (((1,), (1,)), ((), ())),
        precision=highest,
        preferred_element_type=jnp.float32,
    )
    row, col = grid_iota(width, out_ref.shape[1])
    spot = jnp.where(col == row + at_ref[0], 1.0, 0.0)
    placed = jnp.dot(own, spot, precision=highest, preferred_element_type=jnp.float32)
    out_ref[...] = placed[:1] * np.float32(1.0 / count)


def text_mean(at, ids, table):
    width = table.shape[0]
    return pl.pallas_call(
        text_kernel,
        out_shape=jax.ShapeDtypeStruct((1, TEXT_W), jnp.float32),
        in_specs=[SM, SM, ANY],
        out_specs=VM,
        scratch_shapes=[
            pltpu.VMEM((ids.shape[0], width, 128), jnp.bfloat16),
            pltpu.SemaphoreType.DMA,
        ],
        name="text",
    )(at, ids, table)


def decode_kernel(
    frames,
    lead_ref,
    far_ref,
    near_ref,
    own_ref,
    w1_ref,
    b1_ref,
    gain_ref,
    b2_ref,
    pg_ref,
    post_ref,
    w2_hbm,
    pw_hbm,
    proj_hbm,
    out_ref,
    sent_ref,
    w2_s,
    pw_s,
    proj_s,
    win_s,
    x_s,
    sem,
):
    taps = 9 * CH
    w2_copy = pltpu.make_async_copy(w2_hbm, w2_s, sem.at[0])
    pw_copy = pltpu.make_async_copy(pw_hbm, pw_s, sem.at[1])
    w2_copy.start()
    pw_copy.start()
    proj_copy = pltpu.make_async_copy(proj_hbm, proj_s, sem.at[2])
    proj_copy.start()
    rows = frames * PATCH
    for n, r in enumerate((far_ref, near_ref, own_ref)):
        win_s[n * rows : (n + 1) * rows] = r[...]
    wide = frames + 2
    skip = 3 * frames - wide - 2
    cols = 16 * LAT_C
    firsts = []
    for q in range(4):
        acc = jnp.zeros((wide * PATCH, CH), jnp.float32)
        for t in range(3):
            acc = acc + jnp.dot(
                win_s[(skip + t) * PATCH : (skip + t + wide) * PATCH],
                w1_ref[t * cols : (t + 1) * cols, q * CH : (q + 1) * CH],
                preferred_element_type=jnp.float32,
            )
        first = (acc + b1_ref[...]).astype(jnp.bfloat16).astype(jnp.float32)
        firsts.append(first[2 * PATCH :])
        mean = jnp.mean(first * first, axis=-1, keepdims=True)
        v = first * lax.rsqrt(mean + 1e-06) * gain_ref[...]
        act = v / (1.0 + jnp.exp(-v))
        row = lax.broadcasted_iota(jnp.int32, (wide * PATCH, 1), 0)
        act = jnp.where((row >= 2 * PATCH) | (lead_ref[0] == 0), act, 0.0).astype(jnp.bfloat16)
        a, b = q // 2, q % 2
        da, db = (1, -1)[a], (1, -1)[b]
        moves = jnp.concatenate(
            [move_matrix(da, 0), move_matrix(0, db), move_matrix(da, db)], axis=0
        )
        for f in range(wide):
            plane = act[f * PATCH : (f + 1) * PATCH]
            moved = jnp.dot(
                moves, plane, preferred_element_type=jnp.float32
            ).astype(jnp.bfloat16)
            pieces = {
                (0, 0): plane,
                (1, 0): moved[:PATCH],
                (0, 1): moved[PATCH : 2 * PATCH],
                (1, 1): moved[2 * PATCH :],
            }
            for (ma, mb), piece in pieces.items():
                u = WINDOW.index(((1, -1)[a] if ma else 0, a))
                w = WINDOW.index(((1, -1)[b] if mb else 0, b))
                for oa in (0, 1):
                    for ob in (0, 1):
                        dy, dz = u - oa, w - ob
                        if 0 <= dy < 3 and 0 <= dz < 3:
                            at = (f * 4 + 2 * oa + ob) * PATCH
                            tap = (3 * dy + dz) * CH
                            x_s[at : at + PATCH, tap : tap + CH] = piece
    w2_copy.wait()
    block = 4 * PATCH
    out = jnp.zeros((frames * block, CH), jnp.float32)
    for t in range(3):
        out = out + jnp.dot(
            x_s[t * block : (t + frames) * block],
            w2_s[t * taps : (t + 1) * taps],
            preferred_element_type=jnp.float32,
        )
    first = jnp.concatenate(
        [firsts[q][f * PATCH : (f + 1) * PATCH] for f in range(frames) for q in range(4)], axis=0
    )
    dec = (out + b2_ref[...] + first).astype(jnp.bfloat16)
    order = order_matrix()
    for f in range(frames):
        out_ref[f * block : (f + 1) * block] = jnp.dot(
            order, dec[f * block : (f + 1) * block], preferred_element_type=jnp.float32
        ).astype(jnp.bfloat16)
    pw_copy.wait()
    emb = jnp.zeros((rows, pw_s.shape[1]), jnp.float32)
    for q in range(4):
        lhs = jnp.concatenate(
            [dec[(f * 4 + q) * PATCH : (f * 4 + q + 1) * PATCH] for f in range(frames)], axis=0
        )
        emb = emb + jnp.dot(
            lhs, pw_s[q * CH : (q + 1) * CH], preferred_element_type=jnp.float32
        )
    emb = emb.astype(jnp.bfloat16).astype(jnp.float32)
    centered = emb - jnp.mean(emb, axis=-1, keepdims=True)
    variance = jnp.mean(centered * centered, axis=-1, keepdims=True)
    normed = centered * lax.rsqrt(variance + 1e-05) * pg_ref[...]
    pooled = jnp.concatenate(
        [
            jnp.mean(normed[f * PATCH : (f + 1) * PATCH], axis=0, keepdims=True)
            for f in range(frames)
        ],
        axis=0,
    )
    centered = pooled - jnp.mean(pooled, axis=-1, keepdims=True)
    variance = jnp.mean(centered * centered, axis=-1, keepdims=True)
    vec = centered * lax.rsqrt(variance + 1e-05) * post_ref[...]
    columns = jnp.transpose(
        jnp.concatenate([vec, jnp.zeros((8 - frames, vec.shape[1]), jnp.float32)], axis=0)
    )
    proj_copy.wait()
    for f in range(frames):
        row = jnp.sum(columns[:, f : f + 1] * proj_s[...], axis=0, keepdims=True)
        for n in range(sent_ref.shape[0]):
            sent_ref[n, f : f + 1, :] = row


def window_weight(weight):
    taps = weight.reshape(3, 3, 3, LAT_C, CH)
    grown = [
        jnp.pad(taps, ((0, 0), (a, 1 - a), (b, 1 - b), (0, 0), (0, 0))).reshape(-1, CH)
        for a in (0, 1)
        for b in (0, 1)
    ]
    return jnp.concatenate(grown, axis=1)


def decode(
    lead, far, near, own, w1, b1, gain, w2, b2, pw, patch_gain, post_gain, proj, devices
):
    rows = own.shape[0]
    frames = rows // PATCH
    wide = frames + 2
    return pl.pallas_call(
        functools.partial(decode_kernel, frames),
        out_shape=[
            jax.ShapeDtypeStruct((frames * 4 * PATCH, CH), jnp.bfloat16),
            jax.ShapeDtypeStruct((devices, frames, proj.shape[1]), jnp.float32),
        ],
        in_specs=[SM] + [VM] * 9 + [ANY, ANY, ANY],
        out_specs=[VM, VM],
        scratch_shapes=[
            pltpu.VMEM(w2.shape, jnp.bfloat16),
            pltpu.VMEM(pw.shape, jnp.bfloat16),
            pltpu.VMEM(proj.shape, jnp.float32),
            pltpu.VMEM((3 * rows, 16 * LAT_C), jnp.bfloat16),
            pltpu.VMEM((wide * 4 * PATCH, 9 * CH), jnp.bfloat16),
            pltpu.SemaphoreType.DMA((3,)),
        ],
        compiler_params=pltpu.CompilerParams(vmem_limit_bytes=48 << 20),
        name="decode",
    )(
        lead,
        far,
        near,
        own,
        w1,
        b1,
        gain,
        b2,
        patch_gain,
        post_gain,
        w2,
        pw,
        proj,
    )


def rate_kernel(frames, slot_ref, text_ref, got_ref, vec_ref, score_ref):
    text = text_ref[...]
    text_rms = jnp.sqrt(jnp.mean(text * text) + 1e-06)
    for f in range(frames):
        slot = slot_ref[f]
        block = got_ref[slot // frames]
        row = block[:1]
        for n in range(1, frames):
            row = jnp.where(slot % frames == n, block[n : n + 1], row)
        vec_ref[f : f + 1] = row
        inner = jnp.sum(row * text)
        image_rms = jnp.sqrt(jnp.mean(row * row) + 1e-06)
        score_ref[f] = 100.0 * inner / (TEXT_W * image_rms * text_rms)


def rate(slots, text, got):
    frames = slots.shape[0]
    return pl.pallas_call(
        functools.partial(rate_kernel, frames),
        out_shape=[
            jax.ShapeDtypeStruct((frames, got.shape[2]), jnp.float32),
            jax.ShapeDtypeStruct((frames,), jnp.float32),
        ],
        in_specs=[SM, VM, VM],
        out_specs=[VM, SM],
        name="rate",
    )(slots, text, got)


def local(
    queries,
    keys,
    values,
    latent_in,
    mod_table,
    step_size,
    timestep,
    head_weight,
    conv_in_weight,
    conv_in_bias,
    norm_gain,
    conv_weight,
    conv_bias,
    patch_weight,
    patch_gain,
    post_gain,
    proj_weight,
    text_table,
    prompt_ids,
    frame_order,
):
    rows, width = queries.shape
    devices = lax.axis_size("seq")
    chips = devices // 2
    cols = width // chips
    heads = cols // HD
    frames = rows // PATCH
    me = lax.axis_index("seq")
    chip, core = me // 2, me % 2

    tail = max(1, heads // 2)
    phases = (heads - tail, tail) if heads > tail else (tail,)
    firsts = [sum(phases[:n]) for n in range(len(phases))]

    order = sorted(range(1, chips), key=lambda t: abs(2 * t - chips))

    def packed(first, count, turns):
        at = ((chip + jnp.asarray(turns, jnp.int32)) % chips) * cols + first * HD
        blocks = pack(keys, values, queries, at.astype(jnp.int32), count * HD)
        return dict(zip(turns, blocks))

    early = order[:2]
    blocks = packed(firsts[0], phases[0], early)
    blocks |= packed(firsts[0], phases[0], [t for t in range(chips) if t not in early])
    got = [blocks[0]] * chips
    for turn in order:
        got[turn] = rotate(blocks[turn], "seq", turn)
    scale = lax.dynamic_slice_in_dim(mod_table[:, 1, :], chip * cols, cols, 1)
    scale = scale.reshape(-1, heads, 1, HD)
    weight = lax.dynamic_slice_in_dim(head_weight, chip * cols, cols, 0).reshape(heads, HD, LAT)
    weight = jnp.pad(weight, ((0, 0), (0, 0), (0, 128 - LAT)))
    origin = 2 * ((chip - jnp.arange(chips)) % chips) + core
    steps = jnp.take(timestep.reshape(devices, frames), origin, axis=0).reshape(-1)
    near_steps = jnp.stack(
        [
            lax.dynamic_slice_in_dim(timestep, at * frames, frames, 0)
            for at in (me, jnp.maximum(me - 2, 0))
        ]
    ).reshape(-1)
    base = jnp.dot(jnp.take(mod_table[:, 0, :], near_steps, axis=0), head_weight, precision=highest)
    step_dt = jnp.take(step_size, near_steps)
    text_row = text_mean(
        (me * text_table.shape[1]).astype(jnp.int32).reshape(1), prompt_ids, text_table.T
    )
    slots = lax.dynamic_slice_in_dim(frame_order, me * frames, frames, 0)
    prepared = dict(
        scales=[scale[:, f : f + n] for f, n in zip(firsts, phases)],
        weights=[weight[f : f + n] for f, n in zip(firsts, phases)],
        steps=steps,
        base=base,
        step_dt=step_dt,
        text=text_row,
        slots=slots,
        w1=window_weight(conv_in_weight),
        b1=conv_in_bias.reshape(1, -1),
        gain=norm_gain.reshape(1, -1),
        b2=conv_bias.reshape(1, -1),
        patch_gain=patch_gain.reshape(1, -1),
        post_gain=post_gain.reshape(1, -1),
        lead=(me == 0).astype(jnp.int32).reshape(1),
        chip=chip.astype(jnp.int32).reshape(1),
        flags=jnp.stack([chip == 0, core]).astype(jnp.int32),
        later=[packed(f, n, list(range(chips))) for f, n in zip(firsts[1:], phases[1:])],
    )
    words = jnp.broadcast_to(prepared["text"][None], (devices, 1, TEXT_W))
    words = lax.all_to_all(words, "seq", split_axis=0, concat_axis=0, tiled=True)
    words = jnp.sum(words, axis=0)
    far_latent = rotate(latent_in.T, "seq", 1)
    steps = prepared["steps"]
    phase_blocks = [got]
    for gate, blocks in zip(GATES, prepared["later"]):
        before = phase_blocks[0][order[min(gate, len(order) - 1)]]
        blocks, _ = lax.optimization_barrier((blocks, before))
        got = [blocks[0]] * chips
        for turn in order:
            got[turn] = rotate(blocks[turn], "seq", turn)
        phase_blocks.append(got)
    sums = []
    for n, got in enumerate(phase_blocks):
        if n:
            sums[-1], words, far_latent, *got = lax.optimization_barrier(
                (sums[-1], words, far_latent, *got)
            )
        other = [swap_core(block, "seq") for block in got]
        last = n + 1 == len(phase_blocks)
        shares = attend(
            got,
            other,
            prepared["chip"],
            steps,
            prepared["scales"][n],
            prepared["weights"][n],
            sums if last else [],
            last,
        )
        if not last:
            sums.append(shares)
    same_core = [list(range(k, devices, 2)) for k in (0, 1)]
    parts = lax.all_to_all(
        shares, "seq", split_axis=0, concat_axis=0, axis_index_groups=same_core, tiled=True
    )

    latent_next, window, far, passed = step_latent(
        prepared["flags"],
        parts,
        latent_in.T,
        far_latent,
        prepared["base"],
        prepared["step_dt"],
        width,
    )
    near = swap_core(passed, "seq")
    decoded, sent = decode(
        prepared["lead"],
        far,
        near,
        window,
        prepared["w1"],
        prepared["b1"],
        prepared["gain"],
        conv_weight.reshape(-1, CH),
        prepared["b2"],
        patch_weight,
        prepared["patch_gain"],
        prepared["post_gain"],
        proj_weight,
        devices,
    )
    decoded = decoded.reshape(frames, 2 * GRID_H, 2 * GRID_W, CH)
    spread = lax.all_to_all(sent, "seq", split_axis=0, concat_axis=0, tiled=True)
    image_vec, scores = rate(prepared["slots"], words, spread)
    return (latent_next, decoded, image_vec, scores)


def solution(mesh):
    in_specs = (
        P(("grp", "seq"), None),
        P(("grp", "seq"), None),
        P(("grp", "seq"), None),
        P(("grp", "seq"), None),
        P(),
        P(),
        P("grp"),
        P(),
        P(),
        P(),
        P(),
        P(),
        P(),
        P(),
        P(),
        P(),
        P(),
        P(None, "seq"),
        P("grp"),
        P("grp"),
    )
    out_specs = (
        P(("grp", "seq"), None),
        P(("grp", "seq"), None, None, None),
        P(("grp", "seq"), None),
        P(("grp", "seq")),
    )

    return jax.shard_map(local, mesh=mesh, in_specs=in_specs, out_specs=out_specs, check_vma=False)
```

```python
import functools

import jax
import jax.numpy as jnp
import numpy as np
from jax import lax
from jax.experimental import pallas as pl
from jax.experimental.pallas import tpu as pltpu
from jax.sharding import PartitionSpec as P

GRID_H = 8
GRID_W = 12
PATCH = GRID_H * GRID_W
HD = 128
LAT = 64
LAT_C = 16
CH = 384
TEXT_W = 768
KEY_CHUNK = 256
GATES = (1,)


highest = lax.Precision.HIGHEST
VM = pl.BlockSpec(memory_space=pltpu.VMEM)
SM = pl.BlockSpec(memory_space=pltpu.SMEM)
ANY = pl.BlockSpec(memory_space=pl.ANY)


def rotate(value, axis, steps):
    count = lax.axis_size(axis)
    return lax.ppermute(value, axis, [(i, (i + 2 * steps) % count) for i in range(count)])


def swap_core(value, axis):
    count = lax.axis_size(axis)
    return lax.ppermute(value, axis, [(i, i ^ 1) for i in range(count)])


def pack_kernel(turns, chips, cols, first, chip_ref, k_hbm, v_hbm, q_hbm, *refs):
    blocks = len(turns)
    out_refs, (buf, in_sem, out_sem) = refs[:blocks], refs[blocks:]
    width = buf.shape[3]
    gets = []
    for n in range(blocks):
        owner = lax.rem(chip_ref[0] + turns[n], chips)
        at = pl.multiple_of(owner * cols + first, HD)
        gets.append(
            [
                pltpu.make_async_copy(src.at[:, pl.ds(at, width)], buf.at[n, i], in_sem.at[n, i])
                for i, src in enumerate((k_hbm, v_hbm, q_hbm))
            ]
        )
        for get in gets[-1]:
            get.start()
    puts = [
        pltpu.make_async_copy(buf.at[n], out_refs[n], out_sem.at[n]) for n in range(blocks)
    ]
    for n in range(blocks):
        for get in gets[n]:
            get.wait()
        puts[n].start()
    for put in puts:
        put.wait()


def pack(keys, values, queries, chip, turns, chips, first, width):
    rows, blocks = keys.shape[0], len(turns)
    cols = keys.shape[1] // chips
    return pl.pallas_call(
        functools.partial(pack_kernel, tuple(turns), chips, cols, first),
        out_shape=[jax.ShapeDtypeStruct((3, rows, width), jnp.bfloat16)] * blocks,
        in_specs=[SM, ANY, ANY, ANY],
        out_specs=[ANY] * blocks,
        scratch_shapes=[
            pltpu.VMEM((blocks, 3, rows, width), jnp.bfloat16),
            pltpu.SemaphoreType.DMA((blocks, 3)),
            pltpu.SemaphoreType.DMA((blocks,)),
        ],
        name="pack",
    )(chip, keys, values, queries)


def attend_kernel(blocks, heads, frames, earlier, last, chip_ref, t_ref, sc_ref, w_ref, *refs):
    prev_refs, refs = refs[:earlier], refs[earlier:]
    near_refs, far_refs, refs = refs[:blocks], refs[blocks : 2 * blocks], refs[2 * blocks :]
    if last:
        out_ref, refs = refs[0], refs[1:]
    else:
        sum_ref, refs = refs[0], refs[1:]
    q_s, k_s, v_s, s_a, s_b, m_a, m_b, acc_s, tot_s, sem, q_sem = refs[:11]
    if last:
        sum_ref, prev_s, prev_sem = refs[11:]
    sources = near_refs + far_refs
    rows = near_refs[0].shape[1]
    keys = len(sources) * rows
    scale = np.float32(HD**-0.5 * np.log2(np.e))

    def fetch(h, which):
        dst = (k_s, v_s)[which]
        for j, src in enumerate(sources):
            pltpu.make_async_copy(
                src.at[which, :, pl.ds(h * HD, HD)],
                dst.at[h, pl.ds(j * rows, rows), :],
                sem.at[h, which],
            ).start()

    fetch(0, 0)
    for b in range(blocks):
        pltpu.make_async_copy(near_refs[b].at[2], q_s.at[b], q_sem).start()
    fetch(0, 1)
    for h in range(1, heads):
        fetch(h, 0)
        fetch(h, 1)
    gets = []
    for n, prev in enumerate(prev_refs):
        gets.append(pltpu.make_async_copy(prev, prev_s.at[n], prev_sem.at[n]))
        gets[-1].start()
    sum_ref[...] = jnp.zeros(sum_ref.shape, jnp.float32)

    def arrived(h, which):
        whole = (k_s, v_s)[which].at[h]
        pltpu.make_async_copy(whole, whole, sem.at[h, which]).wait()

    def logits(h, b, at, s_ref, peak):
        q = q_s[b, :, pl.ds(pl.multiple_of(h * HD, HD), HD)]
        s = lax.dot_general(
            q,
            k_s[h, at : at + KEY_CHUNK, :],
            (((1,), (1,)), ((), ())),
            preferred_element_type=jnp.float32,
        )
        s_ref[:, at : at + KEY_CHUNK] = s
        folded = functools.reduce(
            jnp.maximum, [s[:, i : i + 128] for i in range(0, KEY_CHUNK, 128)]
        )
        return folded if peak is None else jnp.maximum(peak, folded)

    def keep_peak(peak, m_ref):
        m_ref[...] = jnp.broadcast_to(jnp.max(peak, axis=-1, keepdims=True) * scale, m_ref.shape)

    def finish(h, b, acc, total):
        o = acc / jnp.sum(total, axis=-1, keepdims=True)
        o = o.astype(jnp.bfloat16).astype(jnp.float32)
        square = jnp.sum(o * o, axis=-1, keepdims=True)
        per = rows // frames
        scaled = jnp.concatenate(
            [
                o[f * per : (f + 1) * per] * (1.0 + sc_ref[t_ref[b * frames + f], h])
                for f in range(frames)
            ],
            axis=0,
        )
        part = jnp.dot(scaled, w_ref[h], precision=highest, preferred_element_type=jnp.float32)
        lane = lax.broadcasted_iota(jnp.int32, part.shape, 1)
        return part + jnp.where(lane >= LAT, square, 0.0)

    def one_unit(h, now, top_ref, next_h, next_b, later, later_top_ref):
        top = top_ref[...]
        peak, total = None, None
        acc = jnp.zeros((rows, HD), jnp.float32)
        for at in chunks:
            peak = logits(next_h, next_b, at, later, peak)
            weights = []
            for i in range(at, at + KEY_CHUNK, 128):
                e = jnp.exp2(now[:, i : i + 128] * scale - top)
                total = e if total is None else total + e
                weights.append(e.astype(jnp.bfloat16))
            acc = acc + jnp.dot(
                jnp.concatenate(weights, axis=1),
                v_s[h, at : at + KEY_CHUNK, :],
                preferred_element_type=jnp.float32,
            )
        keep_peak(peak, later_top_ref)
        return acc, total

    chunks = range(0, keys, KEY_CHUNK)
    pltpu.make_async_copy(q_s, q_s, q_sem).wait()
    arrived(0, 0)
    peak = None
    for at in chunks:
        peak = logits(0, 0, at, s_a, peak)
    keep_peak(peak, m_a)
    pairs = blocks // 2
    acc_s[...] = jnp.zeros(acc_s.shape, jnp.float32)
    tot_s[...] = jnp.ones(tot_s.shape, jnp.float32)

    def one_pair(n, carry):
        h, p = n // pairs, n % pairs
        after = jnp.minimum(n + 1, heads * pairs - 1)
        after_h, after_p = after // pairs, after % pairs
        before = jnp.maximum(n - 1, 0)
        before_h, before_p = before // pairs, before % pairs

        @pl.when(p == 0)
        def _():
            arrived(h, 1)

        @pl.when(after_h > h)
        def _():
            arrived(after_h, 0)

        late = finish(before_h, 2 * before_p + 1, acc_s[...], tot_s[...])
        sum_ref[2 * before_p + 1] = sum_ref[2 * before_p + 1] + late
        even = one_unit(h, s_a, m_a, h, 2 * p + 1, s_b, m_b)
        sum_ref[2 * p] = sum_ref[2 * p] + finish(h, 2 * p, *even)
        acc, total = one_unit(h, s_b, m_b, after_h, 2 * after_p, s_a, m_a)
        acc_s[...] = acc
        tot_s[...] = total
        return carry

    lax.fori_loop(0, heads * pairs, one_pair, 0)
    sum_ref[blocks - 1] = sum_ref[blocks - 1] + finish(
        heads - 1, blocks - 1, acc_s[...], tot_s[...]
    )
    if last:
        for get in gets:
            get.wait()
        row, lane = grid_iota(8, 128)
        pick = jnp.where(lane == LAT, 1.0, 0.0)
        for b in range(blocks):
            share = sum_ref[b]
            for n in range(earlier):
                share = share + prev_s[n, b]
            half = PATCH + 8 * frames
            owner = lax.rem(chip_ref[0] - b + blocks, blocks)
            spots = ((owner, 0), (lax.rem(owner + 1, blocks), half))
            beside = jnp.concatenate(
                [share[f * PATCH : (f + 1) * PATCH, :LAT] for f in range(frames)], axis=1
            ).astype(jnp.bfloat16)
            for to, at in spots:
                out_ref[to, at : at + PATCH] = beside
            for f in range(frames):
                square = lax.dot_general(
                    pick,
                    share[f * PATCH : (f + 1) * PATCH],
                    (((1,), (1,)), ((), ())),
                    precision=highest,
                    preferred_element_type=jnp.float32,
                )
                square = jnp.concatenate(
                    [square, jnp.zeros((8, 128 - PATCH), jnp.float32)], axis=1
                )
                high = square.astype(jnp.bfloat16).astype(jnp.float32)
                both = jnp.where(row == 0, high, jnp.where(row == 1, square - high, 0.0))
                for to, at in spots:
                    at = at + PATCH + 8 * f
                    out_ref[to, at : at + 8] = both.astype(jnp.bfloat16)


def attend(near, far, chip, steps, scale, weight, earlier, last):
    blocks = len(near)
    _, rows, cols = near[0].shape
    heads, keys = cols // HD, 2 * blocks * rows
    frames = rows // PATCH
    sums = (blocks, rows, 128)
    if last:
        share = (blocks, 2 * (PATCH + 8 * frames), frames * LAT)
        out_shape = jax.ShapeDtypeStruct(share, jnp.bfloat16)
    else:
        out_shape = jax.ShapeDtypeStruct(sums, jnp.float32)
    return pl.pallas_call(
        functools.partial(attend_kernel, blocks, heads, frames, len(earlier), last),
        out_shape=out_shape,
        in_specs=[SM, SM, VM, VM] + [ANY] * (len(earlier) + 2 * blocks),
        out_specs=VM,
        scratch_shapes=[
            pltpu.VMEM((blocks, rows, cols), jnp.bfloat16),
            pltpu.VMEM((heads, keys, HD), jnp.bfloat16),
            pltpu.VMEM((heads, keys, HD), jnp.bfloat16),
            pltpu.VMEM((rows, keys), jnp.float32),
            pltpu.VMEM((rows, keys), jnp.float32),
            pltpu.VMEM((rows, 128), jnp.float32),
            pltpu.VMEM((rows, 128), jnp.float32),
            pltpu.VMEM((rows, HD), jnp.float32),
            pltpu.VMEM((rows, 128), jnp.float32),
            pltpu.SemaphoreType.DMA((heads, 2)),
            pltpu.SemaphoreType.DMA,
        ]
        + [
            pltpu.VMEM(sums, jnp.float32),
            pltpu.VMEM((max(1, len(earlier)),) + sums, jnp.float32),
            pltpu.SemaphoreType.DMA((max(1, len(earlier)),)),
        ]
        * last,
        cost_estimate=pl.CostEstimate(
            flops=4 * blocks * rows * keys * cols,
            bytes_accessed=4 * keys * cols,
            transcendentals=blocks * rows * keys * heads,
        ),
        compiler_params=pltpu.CompilerParams(vmem_limit_bytes=40 << 20),
        name="attend",
    )(chip, steps, scale, weight, *earlier, *near, *far)


WINDOW = ((-1, 1), (0, 0), (0, 1), (1, 0))


OFFSETS = [(di, dj) for di in (-1, 0, 1) for dj in (-1, 0, 1)]


def grid_iota(rows, cols):
    shape = (rows, cols)
    return lax.broadcasted_iota(jnp.int32, shape, 0), lax.broadcasted_iota(jnp.int32, shape, 1)


def over(value, count):
    return jnp.floor((value.astype(jnp.float32) + 0.5) * np.float32(1.0 / count)).astype(jnp.int32)


def as_matrix(hit):
    return jnp.where(hit, 1.0, 0.0).astype(jnp.bfloat16)


def move_matrix(di, dj, cols=PATCH):
    row, col = grid_iota(PATCH, cols)
    j = row - GRID_W * over(row, GRID_W)
    inside = (j + dj >= 0) & (j + dj < GRID_W) & (col < PATCH)
    return as_matrix((col - row == GRID_W * di + dj) & inside)


def place_matrix(di, dj):
    row, col = grid_iota(LAT, 16 * LAT_C)
    u, w, c = col >> 6, (col >> 4) & 3, col & 15
    source = 2 * LAT_C * (1 - (u & 1)) + LAT_C * (1 - (w & 1)) + c

    def seen(at, step):
        return {-1: at == 0, 0: (at == 1) | (at == 2), 1: at == 3}[step]

    return as_matrix((row == source) & seen(u, di) & seen(w, dj))


def order_matrix():
    row, col = grid_iota(4 * PATCH, 4 * PATCH)
    y = over(row, 2 * GRID_W)
    z = row - 2 * GRID_W * y
    source = (2 * (y & 1) + (z & 1)) * PATCH + (y >> 1) * GRID_W + (z >> 1)
    return as_matrix(col == source)


def latent_kernel(width, frames, flag_ref, dt_ref, part_ref, *refs):
    own_ref, far_ref, base_ref, next_ref, win_ref, before_ref, pass_ref = refs
    total = part_ref[0].astype(jnp.float32)
    for n in range(1, part_ref.shape[0]):
        total = total + part_ref[n].astype(jnp.float32)
    row, _ = grid_iota(8, 128)
    pick = jnp.where(row < 2, 1.0, 0.0)
    cols = 16 * LAT_C
    moves = jnp.concatenate([move_matrix(di, dj, 128) for di, dj in OFFSETS], axis=1)
    places = jnp.concatenate([place_matrix(di, dj) for di, dj in OFFSETS], axis=1)
    none = jnp.zeros((128 - PATCH, cols), jnp.bfloat16)
    first_chip, core = flag_ref[0], flag_ref[1]
    for side, latent in enumerate((jnp.transpose(own_ref[...]), jnp.transpose(far_ref[...]))):
        skip = side * (PATCH + 8 * frames)
        for f in range(frames):
            at = slice(f * PATCH, (f + 1) * PATCH)
            squares = total[skip + PATCH + 8 * f : skip + PATCH + 8 * (f + 1)]
            square = lax.dot_general(
                squares,
                pick,
                (((0,), (0,)), ((), ())),
                precision=highest,
                preferred_element_type=jnp.float32,
            )[:PATCH, :LAT]
            inverse = lax.rsqrt(square * np.float32(1.0 / width) + 1e-06)
            scaled = total[skip : skip + PATCH, f * LAT : (f + 1) * LAT] * inverse
            g = side * frames + f
            value = latent[at] + dt_ref[g] * (scaled + base_ref[g : g + 1])
            spread = jnp.dot(
                value.astype(jnp.bfloat16), places, preferred_element_type=jnp.float32
            ).astype(jnp.bfloat16)
            stacked = jnp.concatenate(
                [x for o in range(len(OFFSETS)) for x in (spread[:, o * cols : (o + 1) * cols], none)],
                axis=0,
            )
            window = jnp.dot(moves, stacked, preferred_element_type=jnp.float32)
            if side:
                window = jnp.where(first_chip == 1, 0.0, window)
                before_ref[at] = window.astype(jnp.bfloat16)
                pass_ref[at] = jnp.where(core == 0, win_ref[at], before_ref[at])
            else:
                next_ref[at] = value
                win_ref[at] = window.astype(jnp.bfloat16)


def step_latent(flags, parts, own, far, base, step_dt, width):
    rows = own.shape[1]
    window = jax.ShapeDtypeStruct((rows, 16 * LAT_C), jnp.bfloat16)
    return pl.pallas_call(
        functools.partial(latent_kernel, width, rows // PATCH),
        out_shape=[jax.ShapeDtypeStruct((rows, LAT), jnp.float32), window, window, window],
        in_specs=[SM, SM] + [VM] * 4,
        out_specs=[VM] * 4,
        compiler_params=pltpu.CompilerParams(vmem_limit_bytes=16 << 20),
        name="latent",
    )(flags, step_dt, parts, own, far, base)


def text_kernel(at_ref, id_ref, table_hbm, out_ref, buf, sem):
    count = id_ref.shape[0]

    def block(n):
        start = pl.multiple_of((id_ref[n] // 128) * 128, 128)
        return pltpu.make_async_copy(table_hbm.at[:, pl.ds(start, 128)], buf.at[n], sem)

    def fetch(n, carry):
        block(n).start()
        return carry

    lax.fori_loop(0, count, fetch, 0)
    pltpu.make_async_copy(buf, buf, sem).wait()
    width = buf.shape[1]
    _, lane = grid_iota(width, 128)

    def add(n, acc):
        return acc + jnp.where(lane == id_ref[n] % 128, buf[n].astype(jnp.float32), 0.0)

    acc = lax.fori_loop(0, count, add, jnp.zeros((width, 128), jnp.float32))
    own = lax.dot_general(
        jnp.ones((8, 128), jnp.float32),
        acc,
        (((1,), (1,)), ((), ())),
        precision=highest,
        preferred_element_type=jnp.float32,
    )
    row, col = grid_iota(width, out_ref.shape[1])
    spot = jnp.where(col == row + at_ref[0], 1.0, 0.0)
    placed = jnp.dot(own, spot, precision=highest, preferred_element_type=jnp.float32)
    out_ref[...] = placed[:1] * np.float32(1.0 / count)


def text_mean(at, ids, table):
    width = table.shape[0]
    return pl.pallas_call(
        text_kernel,
        out_shape=jax.ShapeDtypeStruct((1, TEXT_W), jnp.float32),
        in_specs=[SM, SM, ANY],
        out_specs=VM,
        scratch_shapes=[
            pltpu.VMEM((ids.shape[0], width, 128), jnp.bfloat16),
            pltpu.SemaphoreType.DMA,
        ],
        name="text",
    )(at, ids, table)


def decode_kernel(
    frames,
    lead_ref,
    far_ref,
    near_ref,
    own_ref,
    w1_ref,
    b1_ref,
    gain_ref,
    b2_ref,
    pg_ref,
    post_ref,
    w2_hbm,
    pw_hbm,
    proj_hbm,
    out_ref,
    sent_ref,
    w2_s,
    pw_s,
    proj_s,
    win_s,
    x_s,
    sem,
):
    taps = 9 * CH
    w2_copy = pltpu.make_async_copy(w2_hbm, w2_s, sem.at[0])
    pw_copy = pltpu.make_async_copy(pw_hbm, pw_s, sem.at[1])
    w2_copy.start()
    pw_copy.start()
    proj_copy = pltpu.make_async_copy(proj_hbm, proj_s, sem.at[2])
    proj_copy.start()
    rows = frames * PATCH
    for n, r in enumerate((far_ref, near_ref, own_ref)):
        win_s[n * rows : (n + 1) * rows] = r[...]
    wide = frames + 2
    skip = 3 * frames - wide - 2
    cols = 16 * LAT_C
    firsts = []
    for q in range(4):
        acc = jnp.zeros((wide * PATCH, CH), jnp.float32)
        for t in range(3):
            acc = acc + jnp.dot(
                win_s[(skip + t) * PATCH : (skip + t + wide) * PATCH],
                w1_ref[t * cols : (t + 1) * cols, q * CH : (q + 1) * CH],
                preferred_element_type=jnp.float32,
            )
        first = (acc + b1_ref[...]).astype(jnp.bfloat16).astype(jnp.float32)
        firsts.append(first[2 * PATCH :])
        mean = jnp.mean(first * first, axis=-1, keepdims=True)
        v = first * lax.rsqrt(mean + 1e-06) * gain_ref[...]
        act = v / (1.0 + jnp.exp(-v))
        row = lax.broadcasted_iota(jnp.int32, (wide * PATCH, 1), 0)
        act = jnp.where((row >= 2 * PATCH) | (lead_ref[0] == 0), act, 0.0).astype(jnp.bfloat16)
        a, b = q // 2, q % 2
        da, db = (1, -1)[a], (1, -1)[b]
        moves = jnp.concatenate(
            [move_matrix(da, 0), move_matrix(0, db), move_matrix(da, db)], axis=0
        )
        for f in range(wide):
            plane = act[f * PATCH : (f + 1) * PATCH]
            moved = jnp.dot(
                moves, plane, preferred_element_type=jnp.float32
            ).astype(jnp.bfloat16)
            pieces = {
                (0, 0): plane,
                (1, 0): moved[:PATCH],
                (0, 1): moved[PATCH : 2 * PATCH],
                (1, 1): moved[2 * PATCH :],
            }
            for (ma, mb), piece in pieces.items():
                u = WINDOW.index(((1, -1)[a] if ma else 0, a))
                w = WINDOW.index(((1, -1)[b] if mb else 0, b))
                for oa in (0, 1):
                    for ob in (0, 1):
                        dy, dz = u - oa, w - ob
                        if 0 <= dy < 3 and 0 <= dz < 3:
                            at = (f * 4 + 2 * oa + ob) * PATCH
                            tap = (3 * dy + dz) * CH
                            x_s[at : at + PATCH, tap : tap + CH] = piece
    w2_copy.wait()
    block = 4 * PATCH
    out = jnp.zeros((frames * block, CH), jnp.float32)
    for t in range(3):
        out = out + jnp.dot(
            x_s[t * block : (t + frames) * block],
            w2_s[t * taps : (t + 1) * taps],
            preferred_element_type=jnp.float32,
        )
    first = jnp.concatenate(
        [firsts[q][f * PATCH : (f + 1) * PATCH] for f in range(frames) for q in range(4)], axis=0
    )
    dec = (out + b2_ref[...] + first).astype(jnp.bfloat16)
    order = order_matrix()
    for f in range(frames):
        out_ref[f * block : (f + 1) * block] = jnp.dot(
            order, dec[f * block : (f + 1) * block], preferred_element_type=jnp.float32
        ).astype(jnp.bfloat16)
    pw_copy.wait()
    emb = jnp.zeros((rows, pw_s.shape[1]), jnp.float32)
    for q in range(4):
        lhs = jnp.concatenate(
            [dec[(f * 4 + q) * PATCH : (f * 4 + q + 1) * PATCH] for f in range(frames)], axis=0
        )
        emb = emb + jnp.dot(
            lhs, pw_s[q * CH : (q + 1) * CH], preferred_element_type=jnp.float32
        )
    emb = emb.astype(jnp.bfloat16).astype(jnp.float32)
    centered = emb - jnp.mean(emb, axis=-1, keepdims=True)
    variance = jnp.mean(centered * centered, axis=-1, keepdims=True)
    normed = centered * lax.rsqrt(variance + 1e-05) * pg_ref[...]
    pooled = jnp.concatenate(
        [
            jnp.mean(normed[f * PATCH : (f + 1) * PATCH], axis=0, keepdims=True)
            for f in range(frames)
        ],
        axis=0,
    )
    centered = pooled - jnp.mean(pooled, axis=-1, keepdims=True)
    variance = jnp.mean(centered * centered, axis=-1, keepdims=True)
    vec = centered * lax.rsqrt(variance + 1e-05) * post_ref[...]
    columns = jnp.transpose(
        jnp.concatenate([vec, jnp.zeros((8 - frames, vec.shape[1]), jnp.float32)], axis=0)
    )
    proj_copy.wait()
    for f in range(frames):
        row = jnp.sum(columns[:, f : f + 1] * proj_s[...], axis=0, keepdims=True)
        for n in range(sent_ref.shape[0]):
            sent_ref[n, f : f + 1, :] = row


def window_weight(weight):
    taps = weight.reshape(3, 3, 3, LAT_C, CH)
    grown = [
        jnp.pad(taps, ((0, 0), (a, 1 - a), (b, 1 - b), (0, 0), (0, 0))).reshape(-1, CH)
        for a in (0, 1)
        for b in (0, 1)
    ]
    return jnp.concatenate(grown, axis=1)


def decode(
    lead, far, near, own, w1, b1, gain, w2, b2, pw, patch_gain, post_gain, proj, devices
):
    rows = own.shape[0]
    frames = rows // PATCH
    wide = frames + 2
    return pl.pallas_call(
        functools.partial(decode_kernel, frames),
        out_shape=[
            jax.ShapeDtypeStruct((frames * 4 * PATCH, CH), jnp.bfloat16),
            jax.ShapeDtypeStruct((devices, frames, proj.shape[1]), jnp.float32),
        ],
        in_specs=[SM] + [VM] * 9 + [ANY, ANY, ANY],
        out_specs=[VM, VM],
        scratch_shapes=[
            pltpu.VMEM(w2.shape, jnp.bfloat16),
            pltpu.VMEM(pw.shape, jnp.bfloat16),
            pltpu.VMEM(proj.shape, jnp.float32),
            pltpu.VMEM((3 * rows, 16 * LAT_C), jnp.bfloat16),
            pltpu.VMEM((wide * 4 * PATCH, 9 * CH), jnp.bfloat16),
            pltpu.SemaphoreType.DMA((3,)),
        ],
        compiler_params=pltpu.CompilerParams(vmem_limit_bytes=48 << 20),
        name="decode",
    )(
        lead,
        far,
        near,
        own,
        w1,
        b1,
        gain,
        b2,
        patch_gain,
        post_gain,
        w2,
        pw,
        proj,
    )


def rate_kernel(frames, slot_ref, text_ref, got_ref, vec_ref, score_ref):
    text = text_ref[0]
    for n in range(1, text_ref.shape[0]):
        text = text + text_ref[n]
    text_rms = jnp.sqrt(jnp.mean(text * text) + 1e-06)
    for f in range(frames):
        slot = slot_ref[f]
        block = got_ref[slot // frames]
        row = block[:1]
        for n in range(1, frames):
            row = jnp.where(slot % frames == n, block[n : n + 1], row)
        vec_ref[f : f + 1] = row
        inner = jnp.sum(row * text)
        image_rms = jnp.sqrt(jnp.mean(row * row) + 1e-06)
        score_ref[f] = 100.0 * inner / (TEXT_W * image_rms * text_rms)


def rate(slots, text, got):
    frames = slots.shape[0]
    return pl.pallas_call(
        functools.partial(rate_kernel, frames),
        out_shape=[
            jax.ShapeDtypeStruct((frames, got.shape[2]), jnp.float32),
            jax.ShapeDtypeStruct((frames,), jnp.float32),
        ],
        in_specs=[SM, VM, VM],
        out_specs=[VM, SM],
        name="rate",
    )(slots, text, got)


def local(
    queries,
    keys,
    values,
    latent_in,
    mod_table,
    step_size,
    timestep,
    head_weight,
    conv_in_weight,
    conv_in_bias,
    norm_gain,
    conv_weight,
    conv_bias,
    patch_weight,
    patch_gain,
    post_gain,
    proj_weight,
    text_table,
    prompt_ids,
    frame_order,
):
    rows, width = queries.shape
    devices = lax.axis_size("seq")
    chips = devices // 2
    cols = width // chips
    heads = cols // HD
    frames = rows // PATCH
    me = lax.axis_index("seq")
    chip, core = me // 2, me % 2

    tail = max(1, heads // 2)
    phases = (heads - tail, tail) if heads > tail else (tail,)
    firsts = [sum(phases[:n]) for n in range(len(phases))]

    order = sorted(range(1, chips), key=lambda t: abs(2 * t - chips))

    def packed(first, count, turns):
        blocks = pack(
            keys, values, queries, chip_at, turns, chips, first * HD, count * HD
        )
        return dict(zip(turns, blocks))

    chip_at = chip.astype(jnp.int32).reshape(1)
    early = order[:2]
    blocks = packed(firsts[0], phases[0], early)
    blocks |= packed(firsts[0], phases[0], [t for t in range(chips) if t not in early])
    got = [blocks[0]] * chips
    for turn in order:
        got[turn] = rotate(blocks[turn], "seq", turn)
    scale = lax.dynamic_slice_in_dim(mod_table[:, 1, :], chip * cols, cols, 1)
    scale = scale.reshape(-1, heads, 1, HD)
    weight = lax.dynamic_slice_in_dim(head_weight, chip * cols, cols, 0).reshape(heads, HD, LAT)
    weight = jnp.pad(weight, ((0, 0), (0, 0), (0, 128 - LAT)))
    origin = 2 * ((chip - jnp.arange(chips)) % chips) + core
    steps = jnp.take(timestep.reshape(devices, frames), origin, axis=0).reshape(-1)
    near_steps = jnp.stack(
        [
            lax.dynamic_slice_in_dim(timestep, at * frames, frames, 0)
            for at in (me, jnp.maximum(me - 2, 0))
        ]
    ).reshape(-1)
    base = jnp.dot(jnp.take(mod_table[:, 0, :], near_steps, axis=0), head_weight, precision=highest)
    step_dt = jnp.take(step_size, near_steps)
    text_row = text_mean(
        (me * text_table.shape[1]).astype(jnp.int32).reshape(1), prompt_ids, text_table.T
    )
    slots = lax.dynamic_slice_in_dim(frame_order, me * frames, frames, 0)
    prepared = dict(
        scales=[scale[:, f : f + n] for f, n in zip(firsts, phases)],
        weights=[weight[f : f + n] for f, n in zip(firsts, phases)],
        steps=steps,
        base=base,
        step_dt=step_dt,
        text=text_row,
        slots=slots,
        w1=window_weight(conv_in_weight),
        b1=conv_in_bias.reshape(1, -1),
        gain=norm_gain.reshape(1, -1),
        b2=conv_bias.reshape(1, -1),
        patch_gain=patch_gain.reshape(1, -1),
        post_gain=post_gain.reshape(1, -1),
        lead=(me == 0).astype(jnp.int32).reshape(1),
        chip=chip.astype(jnp.int32).reshape(1),
        flags=jnp.stack([chip == 0, core]).astype(jnp.int32),
        later=[packed(f, n, list(range(chips))) for f, n in zip(firsts[1:], phases[1:])],
    )
    words = jnp.broadcast_to(prepared["text"][None], (devices, 1, TEXT_W))
    words = lax.all_to_all(words, "seq", split_axis=0, concat_axis=0, tiled=True)
    far_latent = rotate(latent_in.T, "seq", 1)
    steps = prepared["steps"]
    phase_blocks = [got]
    for gate, blocks in zip(GATES, prepared["later"]):
        before = phase_blocks[0][order[min(gate, len(order) - 1)]]
        blocks, _ = lax.optimization_barrier((blocks, before))
        got = [blocks[0]] * chips
        for turn in order:
            got[turn] = rotate(blocks[turn], "seq", turn)
        phase_blocks.append(got)
    sums = []
    for n, got in enumerate(phase_blocks):
        if n:
            sums[-1], words, far_latent, *got = lax.optimization_barrier(
                (sums[-1], words, far_latent, *got)
            )
        other = [swap_core(block, "seq") for block in got]
        last = n + 1 == len(phase_blocks)
        shares = attend(
            got,
            other,
            prepared["chip"],
            steps,
            prepared["scales"][n],
            prepared["weights"][n],
            sums if last else [],
            last,
        )
        if not last:
            sums.append(shares)
    same_core = [list(range(k, devices, 2)) for k in (0, 1)]
    parts = lax.all_to_all(
        shares, "seq", split_axis=0, concat_axis=0, axis_index_groups=same_core, tiled=True
    )

    latent_next, window, far, passed = step_latent(
        prepared["flags"],
        parts,
        latent_in.T,
        far_latent,
        prepared["base"],
        prepared["step_dt"],
        width,
    )
    near = swap_core(passed, "seq")
    decoded, sent = decode(
        prepared["lead"],
        far,
        near,
        window,
        prepared["w1"],
        prepared["b1"],
        prepared["gain"],
        conv_weight.reshape(-1, CH),
        prepared["b2"],
        patch_weight,
        prepared["patch_gain"],
        prepared["post_gain"],
        proj_weight,
        devices,
    )
    decoded = decoded.reshape(frames, 2 * GRID_H, 2 * GRID_W, CH)
    spread = lax.all_to_all(sent, "seq", split_axis=0, concat_axis=0, tiled=True)
    image_vec, scores = rate(prepared["slots"], words, spread)
    return (latent_next, decoded, image_vec, scores)


def solution(mesh):
    in_specs = (
        P(("grp", "seq"), None),
        P(("grp", "seq"), None),
        P(("grp", "seq"), None),
        P(("grp", "seq"), None),
        P(),
        P(),
        P("grp"),
        P(),
        P(),
        P(),
        P(),
        P(),
        P(),
        P(),
        P(),
        P(),
        P(),
        P(None, "seq"),
        P("grp"),
        P("grp"),
    )
    out_specs = (
        P(("grp", "seq"), None),
        P(("grp", "seq"), None, None, None),
        P(("grp", "seq"), None),
        P(("grp", "seq")),
    )

    return jax.shard_map(local, mesh=mesh, in_specs=in_specs, out_specs=out_specs, check_vma=False)
```

```python
import functools

import jax
import jax.numpy as jnp
import numpy as np
from jax import lax
from jax.experimental import pallas as pl
from jax.experimental.pallas import tpu as pltpu
from jax.sharding import PartitionSpec as P

GRID_H = 8
GRID_W = 12
PATCH = GRID_H * GRID_W
HD = 128
LAT = 64
LAT_C = 16
CH = 384
TEXT_W = 768
KEY_CHUNK = 256
GATES = (1,)


highest = lax.Precision.HIGHEST
VM = pl.BlockSpec(memory_space=pltpu.VMEM)
SM = pl.BlockSpec(memory_space=pltpu.SMEM)
ANY = pl.BlockSpec(memory_space=pl.ANY)


def rotate(value, axis, steps):
    count = lax.axis_size(axis)
    return lax.ppermute(value, axis, [(i, (i + 2 * steps) % count) for i in range(count)])


def swap_core(value, axis):
    count = lax.axis_size(axis)
    return lax.ppermute(value, axis, [(i, i ^ 1) for i in range(count)])


def pack_kernel(turns, chips, cols, first, chip_ref, k_hbm, v_hbm, q_hbm, *refs):
    blocks = len(turns)
    out_refs, (buf, in_sem, out_sem) = refs[:blocks], refs[blocks:]
    width = buf.shape[3]
    gets = []
    for n in range(blocks):
        owner = lax.rem(chip_ref[0] + turns[n], chips)
        at = pl.multiple_of(owner * cols + first, HD)
        gets.append(
            [
                pltpu.make_async_copy(src.at[:, pl.ds(at, width)], buf.at[n, i], in_sem.at[n, i])
                for i, src in enumerate((k_hbm, v_hbm, q_hbm))
            ]
        )
        for get in gets[-1]:
            get.start()
    puts = [
        pltpu.make_async_copy(buf.at[n], out_refs[n], out_sem.at[n]) for n in range(blocks)
    ]
    for n in range(blocks):
        for get in gets[n]:
            get.wait()
        puts[n].start()
    for put in puts:
        put.wait()


def pack(keys, values, queries, chip, turns, chips, first, width):
    rows, blocks = keys.shape[0], len(turns)
    cols = keys.shape[1] // chips
    return pl.pallas_call(
        functools.partial(pack_kernel, tuple(turns), chips, cols, first),
        out_shape=[jax.ShapeDtypeStruct((3, rows, width), jnp.bfloat16)] * blocks,
        in_specs=[SM, ANY, ANY, ANY],
        out_specs=[ANY] * blocks,
        scratch_shapes=[
            pltpu.VMEM((blocks, 3, rows, width), jnp.bfloat16),
            pltpu.SemaphoreType.DMA((blocks, 3)),
            pltpu.SemaphoreType.DMA((blocks,)),
        ],
        name="pack",
    )(chip, keys, values, queries)


def attend_kernel(blocks, heads, frames, earlier, last, chip_ref, t_ref, sc_ref, w_ref, *refs):
    prev_refs, refs = refs[:earlier], refs[earlier:]
    near_refs, far_refs, refs = refs[:blocks], refs[blocks : 2 * blocks], refs[2 * blocks :]
    if last:
        out_ref, refs = refs[0], refs[1:]
    else:
        sum_ref, refs = refs[0], refs[1:]
    q_s, k_s, v_s, s_a, s_b, m_a, m_b, acc_s, tot_s, sem, q_sem = refs[:11]
    if last:
        sum_ref, prev_s, prev_sem = refs[11:]
    sources = near_refs + far_refs
    rows = near_refs[0].shape[1]
    keys = len(sources) * rows
    scale = np.float32(HD**-0.5 * np.log2(np.e))

    def fetch(h, which):
        dst = (k_s, v_s)[which]
        for j, src in enumerate(sources):
            pltpu.make_async_copy(
                src.at[which, :, pl.ds(h * HD, HD)],
                dst.at[h, pl.ds(j * rows, rows), :],
                sem.at[h, which],
            ).start()

    fetch(0, 0)
    for b in range(blocks):
        pltpu.make_async_copy(near_refs[b].at[2], q_s.at[b], q_sem).start()
    fetch(0, 1)
    for h in range(1, heads):
        fetch(h, 0)
        fetch(h, 1)
    gets = []
    for n, prev in enumerate(prev_refs):
        gets.append(pltpu.make_async_copy(prev, prev_s.at[n], prev_sem.at[n]))
        gets[-1].start()
    sum_ref[...] = jnp.zeros(sum_ref.shape, jnp.float32)

    def arrived(h, which):
        whole = (k_s, v_s)[which].at[h]
        pltpu.make_async_copy(whole, whole, sem.at[h, which]).wait()

    def logits(h, b, at, s_ref, peak):
        q = q_s[b, :, pl.ds(pl.multiple_of(h * HD, HD), HD)]
        s = lax.dot_general(
            q,
            k_s[h, at : at + KEY_CHUNK, :],
            (((1,), (1,)), ((), ())),
            preferred_element_type=jnp.float32,
        )
        s_ref[:, at : at + KEY_CHUNK] = s
        folded = functools.reduce(
            jnp.maximum, [s[:, i : i + 128] for i in range(0, KEY_CHUNK, 128)]
        )
        return folded if peak is None else jnp.maximum(peak, folded)

    def keep_peak(peak, m_ref):
        m_ref[...] = jnp.broadcast_to(jnp.max(peak, axis=-1, keepdims=True) * scale, m_ref.shape)

    def finish(h, b, acc, total):
        o = acc / jnp.sum(total, axis=-1, keepdims=True)
        o = o.astype(jnp.bfloat16).astype(jnp.float32)
        square = jnp.sum(o * o, axis=-1, keepdims=True)
        per = rows // frames
        scaled = jnp.concatenate(
            [
                o[f * per : (f + 1) * per] * (1.0 + sc_ref[t_ref[b * frames + f], h])
                for f in range(frames)
            ],
            axis=0,
        )
        part = jnp.dot(scaled, w_ref[h], precision=highest, preferred_element_type=jnp.float32)
        lane = lax.broadcasted_iota(jnp.int32, part.shape, 1)
        return part + jnp.where(lane >= LAT, square, 0.0)

    def one_unit(h, now, top_ref, next_h, next_b, later, later_top_ref):
        top = top_ref[...]
        peak, total = None, None
        acc = jnp.zeros((rows, HD), jnp.float32)
        for at in chunks:
            peak = logits(next_h, next_b, at, later, peak)
            weights = []
            for i in range(at, at + KEY_CHUNK, 128):
                e = jnp.exp2(now[:, i : i + 128] * scale - top)
                total = e if total is None else total + e
                weights.append(e.astype(jnp.bfloat16))
            acc = acc + jnp.dot(
                jnp.concatenate(weights, axis=1),
                v_s[h, at : at + KEY_CHUNK, :],
                preferred_element_type=jnp.float32,
            )
        keep_peak(peak, later_top_ref)
        return acc, total

    chunks = range(0, keys, KEY_CHUNK)
    pltpu.make_async_copy(q_s, q_s, q_sem).wait()
    arrived(0, 0)
    peak = None
    for at in chunks:
        peak = logits(0, 0, at, s_a, peak)
    keep_peak(peak, m_a)
    pairs = blocks // 2
    acc_s[...] = jnp.zeros(acc_s.shape, jnp.float32)
    tot_s[...] = jnp.ones(tot_s.shape, jnp.float32)

    def one_pair(n, carry):
        h, p = n // pairs, n % pairs
        after = jnp.minimum(n + 1, heads * pairs - 1)
        after_h, after_p = after // pairs, after % pairs
        before = jnp.maximum(n - 1, 0)
        before_h, before_p = before // pairs, before % pairs

        @pl.when(p == 0)
        def _():
            arrived(h, 1)

        @pl.when(after_h > h)
        def _():
            arrived(after_h, 0)

        late = finish(before_h, 2 * before_p + 1, acc_s[...], tot_s[...])
        sum_ref[2 * before_p + 1] = sum_ref[2 * before_p + 1] + late
        even = one_unit(h, s_a, m_a, h, 2 * p + 1, s_b, m_b)
        sum_ref[2 * p] = sum_ref[2 * p] + finish(h, 2 * p, *even)
        acc, total = one_unit(h, s_b, m_b, after_h, 2 * after_p, s_a, m_a)
        acc_s[...] = acc
        tot_s[...] = total
        return carry

    lax.fori_loop(0, heads * pairs, one_pair, 0)
    sum_ref[blocks - 1] = sum_ref[blocks - 1] + finish(
        heads - 1, blocks - 1, acc_s[...], tot_s[...]
    )
    if last:
        for get in gets:
            get.wait()
        row, lane = grid_iota(8, 128)
        pick = jnp.where(lane == LAT, 1.0, 0.0)
        for b in range(blocks):
            share = sum_ref[b]
            for n in range(earlier):
                share = share + prev_s[n, b]
            half = PATCH + 8 * frames
            owner = lax.rem(chip_ref[0] - b + blocks, blocks)
            spots = ((owner, 0), (lax.rem(owner + 1, blocks), half))
            beside = jnp.concatenate(
                [share[f * PATCH : (f + 1) * PATCH, :LAT] for f in range(frames)], axis=1
            ).astype(jnp.bfloat16)
            for to, at in spots:
                out_ref[to, at : at + PATCH] = beside
            for f in range(frames):
                square = lax.dot_general(
                    pick,
                    share[f * PATCH : (f + 1) * PATCH],
                    (((1,), (1,)), ((), ())),
                    precision=highest,
                    preferred_element_type=jnp.float32,
                )
                square = jnp.concatenate(
                    [square, jnp.zeros((8, 128 - PATCH), jnp.float32)], axis=1
                )
                high = square.astype(jnp.bfloat16).astype(jnp.float32)
                both = jnp.where(row == 0, high, jnp.where(row == 1, square - high, 0.0))
                for to, at in spots:
                    at = at + PATCH + 8 * f
                    out_ref[to, at : at + 8] = both.astype(jnp.bfloat16)


def attend(near, far, chip, steps, scale, weight, earlier, last):
    blocks = len(near)
    _, rows, cols = near[0].shape
    heads, keys = cols // HD, 2 * blocks * rows
    frames = rows // PATCH
    sums = (blocks, rows, 128)
    if last:
        share = (blocks, 2 * (PATCH + 8 * frames), frames * LAT)
        out_shape = jax.ShapeDtypeStruct(share, jnp.bfloat16)
    else:
        out_shape = jax.ShapeDtypeStruct(sums, jnp.float32)
    return pl.pallas_call(
        functools.partial(attend_kernel, blocks, heads, frames, len(earlier), last),
        out_shape=out_shape,
        in_specs=[SM, SM, VM, VM] + [ANY] * (len(earlier) + 2 * blocks),
        out_specs=VM,
        scratch_shapes=[
            pltpu.VMEM((blocks, rows, cols), jnp.bfloat16),
            pltpu.VMEM((heads, keys, HD), jnp.bfloat16),
            pltpu.VMEM((heads, keys, HD), jnp.bfloat16),
            pltpu.VMEM((rows, keys), jnp.float32),
            pltpu.VMEM((rows, keys), jnp.float32),
            pltpu.VMEM((rows, 128), jnp.float32),
            pltpu.VMEM((rows, 128), jnp.float32),
            pltpu.VMEM((rows, HD), jnp.float32),
            pltpu.VMEM((rows, 128), jnp.float32),
            pltpu.SemaphoreType.DMA((heads, 2)),
            pltpu.SemaphoreType.DMA,
        ]
        + [
            pltpu.VMEM(sums, jnp.float32),
            pltpu.VMEM((max(1, len(earlier)),) + sums, jnp.float32),
            pltpu.SemaphoreType.DMA((max(1, len(earlier)),)),
        ]
        * last,
        cost_estimate=pl.CostEstimate(
            flops=4 * blocks * rows * keys * cols,
            bytes_accessed=4 * keys * cols,
            transcendentals=blocks * rows * keys * heads,
        ),
        compiler_params=pltpu.CompilerParams(vmem_limit_bytes=40 << 20),
        name="attend",
    )(chip, steps, scale, weight, *earlier, *near, *far)


WINDOW = ((-1, 1), (0, 0), (0, 1), (1, 0))


OFFSETS = [(di, dj) for di in (-1, 0, 1) for dj in (-1, 0, 1)]


def grid_iota(rows, cols):
    shape = (rows, cols)
    return lax.broadcasted_iota(jnp.int32, shape, 0), lax.broadcasted_iota(jnp.int32, shape, 1)


def over(value, count):
    return jnp.floor((value.astype(jnp.float32) + 0.5) * np.float32(1.0 / count)).astype(jnp.int32)


def as_matrix(hit):
    return jnp.where(hit, 1.0, 0.0).astype(jnp.bfloat16)


def move_matrix(di, dj, cols=PATCH):
    row, col = grid_iota(PATCH, cols)
    j = row - GRID_W * over(row, GRID_W)
    inside = (j + dj >= 0) & (j + dj < GRID_W) & (col < PATCH)
    return as_matrix((col - row == GRID_W * di + dj) & inside)


def place_matrix(di, dj):
    row, col = grid_iota(LAT, 16 * LAT_C)
    u, w, c = col >> 6, (col >> 4) & 3, col & 15
    source = 2 * LAT_C * (1 - (u & 1)) + LAT_C * (1 - (w & 1)) + c

    def seen(at, step):
        return {-1: at == 0, 0: (at == 1) | (at == 2), 1: at == 3}[step]

    return as_matrix((row == source) & seen(u, di) & seen(w, dj))


def order_matrix():
    row, col = grid_iota(4 * PATCH, 4 * PATCH)
    y = over(row, 2 * GRID_W)
    z = row - 2 * GRID_W * y
    source = (2 * (y & 1) + (z & 1)) * PATCH + (y >> 1) * GRID_W + (z >> 1)
    return as_matrix(col == source)


def latent_kernel(width, frames, flag_ref, dt_ref, part_ref, *refs):
    own_ref, far_ref, base_ref, next_ref, win_ref, before_ref, pass_ref = refs
    total = part_ref[0].astype(jnp.float32)
    for n in range(1, part_ref.shape[0]):
        total = total + part_ref[n].astype(jnp.float32)
    row, _ = grid_iota(8, 128)
    pick = jnp.where(row < 2, 1.0, 0.0)
    cols = 16 * LAT_C
    moves = jnp.concatenate([move_matrix(di, dj, 128) for di, dj in OFFSETS], axis=1)
    places = jnp.concatenate([place_matrix(di, dj) for di, dj in OFFSETS], axis=1)
    none = jnp.zeros((128 - PATCH, cols), jnp.bfloat16)
    first_chip, core = flag_ref[0], flag_ref[1]
    for side, latent in enumerate((jnp.transpose(own_ref[...]), jnp.transpose(far_ref[...]))):
        skip = side * (PATCH + 8 * frames)
        for f in range(frames):
            at = slice(f * PATCH, (f + 1) * PATCH)
            squares = total[skip + PATCH + 8 * f : skip + PATCH + 8 * (f + 1)]
            square = lax.dot_general(
                squares,
                pick,
                (((0,), (0,)), ((), ())),
                precision=highest,
                preferred_element_type=jnp.float32,
            )[:PATCH, :LAT]
            inverse = lax.rsqrt(square * np.float32(1.0 / width) + 1e-06)
            scaled = total[skip : skip + PATCH, f * LAT : (f + 1) * LAT] * inverse
            g = side * frames + f
            value = latent[at] + dt_ref[g] * (scaled + base_ref[g : g + 1])
            spread = jnp.dot(
                value.astype(jnp.bfloat16), places, preferred_element_type=jnp.float32
            ).astype(jnp.bfloat16)
            stacked = jnp.concatenate(
                [x for o in range(len(OFFSETS)) for x in (spread[:, o * cols : (o + 1) * cols], none)],
                axis=0,
            )
            window = jnp.dot(moves, stacked, preferred_element_type=jnp.float32)
            if side:
                window = jnp.where(first_chip == 1, 0.0, window)
                before_ref[at] = window.astype(jnp.bfloat16)
                pass_ref[at] = jnp.where(core == 0, win_ref[at], before_ref[at])
            else:
                next_ref[at] = value
                win_ref[at] = window.astype(jnp.bfloat16)


def step_latent(flags, parts, own, far, base, step_dt, width):
    rows = own.shape[1]
    window = jax.ShapeDtypeStruct((rows, 16 * LAT_C), jnp.bfloat16)
    return pl.pallas_call(
        functools.partial(latent_kernel, width, rows // PATCH),
        out_shape=[jax.ShapeDtypeStruct((rows, LAT), jnp.float32), window, window, window],
        in_specs=[SM, SM] + [VM] * 4,
        out_specs=[VM] * 4,
        compiler_params=pltpu.CompilerParams(vmem_limit_bytes=16 << 20),
        name="latent",
    )(flags, step_dt, parts, own, far, base)


def text_kernel(at_ref, id_ref, table_hbm, out_ref, buf, sem):
    count = id_ref.shape[0]

    def block(n):
        start = pl.multiple_of((id_ref[n] // 128) * 128, 128)
        return pltpu.make_async_copy(table_hbm.at[:, pl.ds(start, 128)], buf.at[n], sem)

    def fetch(n, carry):
        block(n).start()
        return carry

    lax.fori_loop(0, count, fetch, 0)
    pltpu.make_async_copy(buf, buf, sem).wait()
    width = buf.shape[1]
    _, lane = grid_iota(width, 128)

    def add(n, acc):
        return acc + jnp.where(lane == id_ref[n] % 128, buf[n].astype(jnp.float32), 0.0)

    acc = lax.fori_loop(0, count, add, jnp.zeros((width, 128), jnp.float32))
    own = lax.dot_general(
        jnp.ones((8, 128), jnp.float32),
        acc,
        (((1,), (1,)), ((), ())),
        precision=highest,
        preferred_element_type=jnp.float32,
    )
    row, col = grid_iota(width, out_ref.shape[1])
    spot = jnp.where(col == row + at_ref[0], 1.0, 0.0)
    placed = jnp.dot(own, spot, precision=highest, preferred_element_type=jnp.float32)
    out_ref[...] = placed[:1] * np.float32(1.0 / count)


def text_mean(at, ids, table):
    width = table.shape[0]
    return pl.pallas_call(
        text_kernel,
        out_shape=jax.ShapeDtypeStruct((1, TEXT_W), jnp.float32),
        in_specs=[SM, SM, ANY],
        out_specs=VM,
        scratch_shapes=[
            pltpu.VMEM((ids.shape[0], width, 128), jnp.bfloat16),
            pltpu.SemaphoreType.DMA,
        ],
        name="text",
    )(at, ids, table)


def decode_kernel(
    frames,
    lead_ref,
    far_ref,
    near_ref,
    own_ref,
    w1_ref,
    b1_ref,
    gain_ref,
    b2_ref,
    pg_ref,
    post_ref,
    w2_hbm,
    pw_hbm,
    proj_hbm,
    out_ref,
    sent_ref,
    w2_s,
    pw_s,
    proj_s,
    win_s,
    x_s,
    sem,
):
    taps = 9 * CH
    w2_copy = pltpu.make_async_copy(w2_hbm, w2_s, sem.at[0])
    pw_copy = pltpu.make_async_copy(pw_hbm, pw_s, sem.at[1])
    w2_copy.start()
    pw_copy.start()
    proj_copy = pltpu.make_async_copy(proj_hbm, proj_s, sem.at[2])
    proj_copy.start()
    rows = frames * PATCH
    for n, r in enumerate((far_ref, near_ref, own_ref)):
        win_s[n * rows : (n + 1) * rows] = r[...]
    wide = frames + 2
    skip = 3 * frames - wide - 2
    cols = 16 * LAT_C
    firsts = []
    for q in range(4):
        acc = jnp.zeros((wide * PATCH, CH), jnp.float32)
        for t in range(3):
            acc = acc + jnp.dot(
                win_s[(skip + t) * PATCH : (skip + t + wide) * PATCH],
                w1_ref[t * cols : (t + 1) * cols, q * CH : (q + 1) * CH],
                preferred_element_type=jnp.float32,
            )
        first = (acc + b1_ref[...]).astype(jnp.bfloat16).astype(jnp.float32)
        firsts.append(first[2 * PATCH :])
        mean = jnp.mean(first * first, axis=-1, keepdims=True)
        v = first * lax.rsqrt(mean + 1e-06) * gain_ref[...]
        act = v / (1.0 + jnp.exp(-v))
        row = lax.broadcasted_iota(jnp.int32, (wide * PATCH, 1), 0)
        act = jnp.where((row >= 2 * PATCH) | (lead_ref[0] == 0), act, 0.0).astype(jnp.bfloat16)
        a, b = q // 2, q % 2
        da, db = (1, -1)[a], (1, -1)[b]
        moves = jnp.concatenate(
            [move_matrix(da, 0), move_matrix(0, db), move_matrix(da, db)], axis=0
        )
        for f in range(wide):
            plane = act[f * PATCH : (f + 1) * PATCH]
            moved = jnp.dot(
                moves, plane, preferred_element_type=jnp.float32
            ).astype(jnp.bfloat16)
            pieces = {
                (0, 0): plane,
                (1, 0): moved[:PATCH],
                (0, 1): moved[PATCH : 2 * PATCH],
                (1, 1): moved[2 * PATCH :],
            }
            for (ma, mb), piece in pieces.items():
                u = WINDOW.index(((1, -1)[a] if ma else 0, a))
                w = WINDOW.index(((1, -1)[b] if mb else 0, b))
                for oa in (0, 1):
                    for ob in (0, 1):
                        dy, dz = u - oa, w - ob
                        if 0 <= dy < 3 and 0 <= dz < 3:
                            at = (f * 4 + 2 * oa + ob) * PATCH
                            tap = (3 * dy + dz) * CH
                            x_s[at : at + PATCH, tap : tap + CH] = piece
    w2_copy.wait()
    block = 4 * PATCH
    out = jnp.zeros((frames * block, CH), jnp.float32)
    for t in range(3):
        out = out + jnp.dot(
            x_s[t * block : (t + frames) * block],
            w2_s[t * taps : (t + 1) * taps],
            preferred_element_type=jnp.float32,
        )
    first = jnp.concatenate(
        [firsts[q][f * PATCH : (f + 1) * PATCH] for f in range(frames) for q in range(4)], axis=0
    )
    dec = (out + b2_ref[...] + first).astype(jnp.bfloat16)
    order = order_matrix()
    for f in range(frames):
        out_ref[f * block : (f + 1) * block] = jnp.dot(
            order, dec[f * block : (f + 1) * block], preferred_element_type=jnp.float32
        ).astype(jnp.bfloat16)
    pw_copy.wait()
    emb = jnp.zeros((rows, pw_s.shape[1]), jnp.float32)
    for q in range(4):
        lhs = jnp.concatenate(
            [dec[(f * 4 + q) * PATCH : (f * 4 + q + 1) * PATCH] for f in range(frames)], axis=0
        )
        emb = emb + jnp.dot(
            lhs, pw_s[q * CH : (q + 1) * CH], preferred_element_type=jnp.float32
        )
    emb = emb.astype(jnp.bfloat16).astype(jnp.float32)
    centered = emb - jnp.mean(emb, axis=-1, keepdims=True)
    variance = jnp.mean(centered * centered, axis=-1, keepdims=True)
    normed = centered * lax.rsqrt(variance + 1e-05) * pg_ref[...]
    pooled = jnp.concatenate(
        [
            jnp.mean(normed[f * PATCH : (f + 1) * PATCH], axis=0, keepdims=True)
            for f in range(frames)
        ],
        axis=0,
    )
    centered = pooled - jnp.mean(pooled, axis=-1, keepdims=True)
    variance = jnp.mean(centered * centered, axis=-1, keepdims=True)
    vec = centered * lax.rsqrt(variance + 1e-05) * post_ref[...]
    columns = jnp.transpose(
        jnp.concatenate([vec, jnp.zeros((8 - frames, vec.shape[1]), jnp.float32)], axis=0)
    )
    proj_copy.wait()
    for f in range(frames):
        row = jnp.sum(columns[:, f : f + 1] * proj_s[...], axis=0, keepdims=True)
        for n in range(sent_ref.shape[0]):
            sent_ref[n, f : f + 1, :] = row


def window_weight(weight):
    taps = weight.reshape(3, 3, 3, LAT_C, CH)
    grown = [
        jnp.pad(taps, ((0, 0), (a, 1 - a), (b, 1 - b), (0, 0), (0, 0))).reshape(-1, CH)
        for a in (0, 1)
        for b in (0, 1)
    ]
    return jnp.concatenate(grown, axis=1)


def decode(
    lead, far, near, own, w1, b1, gain, w2, b2, pw, patch_gain, post_gain, proj, devices
):
    rows = own.shape[0]
    frames = rows // PATCH
    wide = frames + 2
    return pl.pallas_call(
        functools.partial(decode_kernel, frames),
        out_shape=[
            jax.ShapeDtypeStruct((frames * 4 * PATCH, CH), jnp.bfloat16),
            jax.ShapeDtypeStruct((devices, frames, proj.shape[1]), jnp.float32),
        ],
        in_specs=[SM] + [VM] * 9 + [ANY, ANY, ANY],
        out_specs=[VM, VM],
        scratch_shapes=[
            pltpu.VMEM(w2.shape, jnp.bfloat16),
            pltpu.VMEM(pw.shape, jnp.bfloat16),
            pltpu.VMEM(proj.shape, jnp.float32),
            pltpu.VMEM((3 * rows, 16 * LAT_C), jnp.bfloat16),
            pltpu.VMEM((wide * 4 * PATCH, 9 * CH), jnp.bfloat16),
            pltpu.SemaphoreType.DMA((3,)),
        ],
        compiler_params=pltpu.CompilerParams(vmem_limit_bytes=48 << 20),
        name="decode",
    )(
        lead,
        far,
        near,
        own,
        w1,
        b1,
        gain,
        b2,
        patch_gain,
        post_gain,
        w2,
        pw,
        proj,
    )


def rate_kernel(frames, slot_ref, text_ref, got_ref, vec_ref, score_ref):
    text = text_ref[0]
    for n in range(1, text_ref.shape[0]):
        text = text + text_ref[n]
    text_rms = jnp.sqrt(jnp.mean(text * text) + 1e-06)
    for f in range(frames):
        slot = slot_ref[f]
        block = got_ref[slot // frames]
        row = block[:1]
        for n in range(1, frames):
            row = jnp.where(slot % frames == n, block[n : n + 1], row)
        vec_ref[f : f + 1] = row
        inner = jnp.sum(row * text)
        image_rms = jnp.sqrt(jnp.mean(row * row) + 1e-06)
        score_ref[f] = 100.0 * inner / (TEXT_W * image_rms * text_rms)


def rate(slots, text, got):
    frames = slots.shape[0]
    return pl.pallas_call(
        functools.partial(rate_kernel, frames),
        out_shape=[
            jax.ShapeDtypeStruct((frames, got.shape[2]), jnp.float32),
            jax.ShapeDtypeStruct((frames,), jnp.float32),
        ],
        in_specs=[SM, VM, VM],
        out_specs=[VM, SM],
        name="rate",
    )(slots, text, got)


def local(
    queries,
    keys,
    values,
    latent_in,
    mod_table,
    step_size,
    timestep,
    head_weight,
    conv_in_weight,
    conv_in_bias,
    norm_gain,
    conv_weight,
    conv_bias,
    patch_weight,
    patch_gain,
    post_gain,
    proj_weight,
    text_table,
    prompt_ids,
    frame_order,
):
    rows, width = queries.shape
    devices = lax.axis_size("seq")
    chips = devices // 2
    cols = width // chips
    heads = cols // HD
    frames = rows // PATCH
    me = lax.axis_index("seq")
    chip, core = me // 2, me % 2

    tail = max(1, heads // 2)
    phases = (heads - tail, tail) if heads > tail else (tail,)
    firsts = [sum(phases[:n]) for n in range(len(phases))]

    order = sorted(range(1, chips), key=lambda t: abs(2 * t - chips))

    def packed(first, count, turns):
        blocks = pack(
            keys, values, queries, chip_at, turns, chips, first * HD, count * HD
        )
        return dict(zip(turns, blocks))

    chip_at = chip.astype(jnp.int32).reshape(1)
    early = order[:2]
    blocks = packed(firsts[0], phases[0], early)
    blocks |= packed(firsts[0], phases[0], [t for t in range(chips) if t not in early])
    got = [blocks[0]] * chips
    for turn in order:
        got[turn] = rotate(blocks[turn], "seq", turn)
    scale = lax.dynamic_slice_in_dim(mod_table[:, 1, :], chip * cols, cols, 1)
    scale = scale.reshape(-1, heads, 1, HD)
    weight = lax.dynamic_slice_in_dim(head_weight, chip * cols, cols, 0).reshape(heads, HD, LAT)
    weight = jnp.pad(weight, ((0, 0), (0, 0), (0, 128 - LAT)))
    origin = 2 * ((chip - jnp.arange(chips)) % chips) + core
    steps = jnp.take(timestep.reshape(devices, frames), origin, axis=0).reshape(-1)
    near_steps = jnp.stack(
        [
            lax.dynamic_slice_in_dim(timestep, at * frames, frames, 0)
            for at in (me, jnp.maximum(me - 2, 0))
        ]
    ).reshape(-1)
    base = jnp.dot(jnp.take(mod_table[:, 0, :], near_steps, axis=0), head_weight, precision=highest)
    step_dt = jnp.take(step_size, near_steps)
    text_row = text_mean(
        (me * text_table.shape[1]).astype(jnp.int32).reshape(1), prompt_ids, text_table.T
    )
    slots = lax.dynamic_slice_in_dim(frame_order, me * frames, frames, 0)
    prepared = dict(
        scales=[scale[:, f : f + n] for f, n in zip(firsts, phases)],
        weights=[weight[f : f + n] for f, n in zip(firsts, phases)],
        steps=steps,
        base=base,
        step_dt=step_dt,
        text=text_row,
        slots=slots,
        w1=window_weight(conv_in_weight),
        b1=conv_in_bias.reshape(1, -1),
        gain=norm_gain.reshape(1, -1),
        b2=conv_bias.reshape(1, -1),
        patch_gain=patch_gain.reshape(1, -1),
        post_gain=post_gain.reshape(1, -1),
        lead=(me == 0).astype(jnp.int32).reshape(1),
        chip=chip.astype(jnp.int32).reshape(1),
        flags=jnp.stack([chip == 0, core]).astype(jnp.int32),
        later=[packed(f, n, list(range(chips))) for f, n in zip(firsts[1:], phases[1:])],
    )
    words = jnp.broadcast_to(prepared["text"][None], (devices, 1, TEXT_W))
    words = lax.all_to_all(words, "seq", split_axis=0, concat_axis=0, tiled=True)
    far_latent = rotate(latent_in.T, "seq", 1)
    steps = prepared["steps"]
    phase_blocks = [got]
    for gate, blocks in zip(GATES, prepared["later"]):
        before = phase_blocks[0][order[min(gate, len(order) - 1)]]
        blocks, _ = lax.optimization_barrier((blocks, before))
        got = [blocks[0]] * chips
        for turn in order:
            got[turn] = rotate(blocks[turn], "seq", turn)
        phase_blocks.append(got)
    sums = []
    for n, got in enumerate(phase_blocks):
        if n:
            words, far_latent, _ = lax.optimization_barrier((words, far_latent, sums[-1]))
            got = [lax.optimization_barrier((block, sums[-1]))[0] for block in got]
        other = [swap_core(block, "seq") for block in got]
        last = n + 1 == len(phase_blocks)
        shares = attend(
            got,
            other,
            prepared["chip"],
            steps,
            prepared["scales"][n],
            prepared["weights"][n],
            sums if last else [],
            last,
        )
        if not last:
            sums.append(shares)
    same_core = [list(range(k, devices, 2)) for k in (0, 1)]
    parts = lax.all_to_all(
        shares, "seq", split_axis=0, concat_axis=0, axis_index_groups=same_core, tiled=True
    )

    latent_next, window, far, passed = step_latent(
        prepared["flags"],
        parts,
        latent_in.T,
        far_latent,
        prepared["base"],
        prepared["step_dt"],
        width,
    )
    near = swap_core(passed, "seq")
    decoded, sent = decode(
        prepared["lead"],
        far,
        near,
        window,
        prepared["w1"],
        prepared["b1"],
        prepared["gain"],
        conv_weight.reshape(-1, CH),
        prepared["b2"],
        patch_weight,
        prepared["patch_gain"],
        prepared["post_gain"],
        proj_weight,
        devices,
    )
    decoded = decoded.reshape(frames, 2 * GRID_H, 2 * GRID_W, CH)
    spread = lax.all_to_all(sent, "seq", split_axis=0, concat_axis=0, tiled=True)
    image_vec, scores = rate(prepared["slots"], words, spread)
    return (latent_next, decoded, image_vec, scores)


def solution(mesh):
    in_specs = (
        P(("grp", "seq"), None),
        P(("grp", "seq"), None),
        P(("grp", "seq"), None),
        P(("grp", "seq"), None),
        P(),
        P(),
        P("grp"),
        P(),
        P(),
        P(),
        P(),
        P(),
        P(),
        P(),
        P(),
        P(),
        P(),
        P(None, "seq"),
        P("grp"),
        P("grp"),
    )
    out_specs = (
        P(("grp", "seq"), None),
        P(("grp", "seq"), None, None, None),
        P(("grp", "seq"), None),
        P(("grp", "seq")),
    )

    return jax.shard_map(local, mesh=mesh, in_specs=in_specs, out_specs=out_specs, check_vma=False)
```
